128 devices in a mesh: comp: 4 (over x), dom: 32 (over z, y, core).
Axes of the slice: x: 4, y: 4, z: 4, core: 2. Of those that a mesh axis runs over, the one named last changes fastest.
Arguments:
- state: float32 [4, 128, 65536], P('comp', None, 'dom'), may hold values from -6 to 6
- neighbors: int32 [4, 4, 65536], P('comp', None, 'dom'), may hold values from 0 to 2559, as said below
- edge_coef: float32 [4, 4, 65536], P('comp', None, 'dom'), may hold values from 0.02 to 0.22
- sea_mask: int32 [65536], P('dom'), may hold values 0 or 1
- pair_source: int32 [32, 16], replicated, may hold values from 0 to 95, as said below
- pair_rows: int32 [32, 16, 512], P('dom'), may hold values from 0 to 2047, as said below
- pair_cols: int32 [32, 16, 512], replicated, may hold values from 0 to 2047, as said below
- remap_weight: float32 [32, 16, 512, 512], P('dom'), may hold values from -0.25 to 0.25
Outputs:
- advanced_state: float32 [4, 128, 65536], P('comp', None, 'dom')
The draws below stay inside these ranges and needn't reach their ends.
Inputs may be any that keep to these rules, and one draw needn't show every extreme that they name: `neighbors`: each entry indexes the 2048 columns of its domain widened by 256 columns of each adjacent domain of the cycle, the left rim first. `pair_source`: row d names 16 different atmosphere devices: in each atmosphere band the domains d - 2 to d + 2 around the cycle, and one more atmosphere device outside these. `pair_rows`: cells of the ocean domain, different within one block. `pair_cols`: columns of the atmosphere device of the block, different within one block.
All inputs are finite; a program needn't handle non-finite values. No bound on the sum of `sea_mask` on one device may be relied on, other than what follows from the above.
Results may differ from the reference program's by a relative error of at most 0.000052.
Values sent between devices are 32-bit elements; how exact they have to be, the bound alone decides.
A program may use at most 128 MiB of HBM per device.

```python
import jax
import jax.numpy as jnp
from jax import lax

LEVELS = 128
FIELDS = 4
COLS = 2048
RIM = 256
EDGES = 4
STEPS = 4
NPAIRS = 16
BLOCK = 512
GROUPS = 4
DOMAINS = 32
COLUMNS = 65536
N_COMP = 4
N_DOM = 32


def draw_neighbors(key, part):
    key_list = jax.random.split(jax.random.fold_in(key, 5), 4)
    shape = (GROUPS, COLUMNS)
    local = jnp.broadcast_to(jnp.arange(COLUMNS, dtype=jnp.int32) % COLS, shape)
    shift_left = jax.random.randint(key_list[0], shape, 0, 2)
    shift_right = jax.random.randint(key_list[1], shape, 0, 2)
    shift_below = jax.random.randint(key_list[2], shape, -2, 3)
    shift_above = jax.random.randint(key_list[3], shape, -2, 3)
    top_index = COLS + 2 * RIM - 1
    left = local + RIM - 1 - shift_left
    right = local + RIM + 1 + shift_right
    below = jnp.clip(local + shift_below, 0, top_index)
    above = jnp.clip(local + 2 * RIM + shift_above, 0, top_index)
    below = jnp.where(local == 0, 0, below)
    above = jnp.where(local == COLS - 1, top_index, above)
    return jnp.stack([left, right, below, above], axis=1).astype(jnp.int32)


def draw_pair_source(key, part):
    key_list = jax.random.split(jax.random.fold_in(key, 11), DOMAINS)
    atmos_ids = jnp.arange((GROUPS - 1) * DOMAINS, dtype=jnp.int32)

    def one_row(row_key, row_dom):
        scores = jax.random.permutation(row_key, (GROUPS - 1) * DOMAINS).astype(jnp.int32)
        offset = (atmos_ids % DOMAINS - row_dom) % DOMAINS
        nearby = jnp.logical_or(offset <= 2, offset >= DOMAINS - 2)
        scores = scores + jnp.where(nearby, 4 * GROUPS * DOMAINS, 0)
        return lax.top_k(scores, NPAIRS)[1].astype(jnp.int32)
    return jax.vmap(one_row)(key_list, jnp.arange(DOMAINS, dtype=jnp.int32))


def window_indices(key):
    start_key, order_key = jax.random.split(key)
    window_start = jax.random.randint(start_key, (DOMAINS, NPAIRS), 0, COLS)
    window_start = window_start.at[:, 0].set(COLS - BLOCK).at[:, 1].set(0)
    key_list = jax.random.split(order_key, DOMAINS * NPAIRS)
    shuffles = jax.vmap(lambda one_key: jax.random.permutation(one_key, BLOCK))(key_list)
    shuffles = shuffles.reshape(DOMAINS, NPAIRS, BLOCK)
    return ((window_start[:, :, None] + shuffles) % COLS).astype(jnp.int32)


def draw_pair_rows(key, part):
    return window_indices(jax.random.fold_in(key, 23))


def draw_pair_cols(key, part):
    return window_indices(jax.random.fold_in(key, 37))


def set_ends(result, rng, least, largest):
    index_at = [jax.random.randint(jax.random.fold_in(rng, axis), (), 0, length) for axis, length in enumerate(result.shape)]
    main_axis = result.shape.index(max(result.shape))
    neighbour = index_at[:main_axis] + [(index_at[main_axis] + 1) % result.shape[main_axis]] + index_at[main_axis + 1:]
    return result.at[tuple(index_at)].set(least).at[tuple(neighbour)].set(largest)


def shard_levels(stream_key, shape, shards, smallest, top_value):
    def one(position, blocks):
        draws = jax.random.uniform(jax.random.fold_in(jax.random.fold_in(stream_key, 6), position), (blocks,), jnp.float32, smallest / len(shards), top_value / len(shards))
        return jnp.repeat(jnp.exp(draws), shape[position] // blocks).reshape((-1,) + (1,) * (len(shape) - position - 1))

    level = one(*shards[0])
    for cut in shards[1:]:
        level = level * one(*cut)
    return level


def noise(own_key, shape, deviation, most, pieces=(), kind=jnp.bfloat16):
    loudness = shard_levels(own_key, shape, pieces, -0.22, 0.18) if pieces else 1.0
    entries = jax.random.normal(own_key, shape, jnp.float32) * deviation * loudness
    return jnp.minimum(jnp.maximum(entries, -most), most).astype(kind)


def setup_inputs(seed: int = 0) -> dict:
    arg_keys = jax.random.split(jax.random.key(seed), 9)
    state = noise(arg_keys[0], (N_COMP, LEVELS, COLS * N_DOM), 1.0, 6.0, ((0, 4), (2, 32)), jnp.float32)
    neighbors = draw_neighbors(jax.random.fold_in(arg_keys[8], 71), 0)
    edge_coef = jnp.clip(0.02 + 0.2 * jax.random.uniform(arg_keys[2], (N_COMP, EDGES, COLS * N_DOM), jnp.float32) ** shard_levels(arg_keys[2], (N_COMP, EDGES, COLS * N_DOM), ((0, 4), (2, 32)), -0.2, 0.2), 0.02, 0.22)
    sea_mask = set_ends((jax.random.randint(arg_keys[3], (COLS * N_DOM,), 0, 4) < 3).astype(jnp.int32), jax.random.fold_in(arg_keys[3], 1), 0, 1)
    pair_source = draw_pair_source(jax.random.fold_in(arg_keys[8], 71), 0)
    pair_rows = draw_pair_rows(jax.random.fold_in(arg_keys[8], 71), 0)
    pair_cols = draw_pair_cols(jax.random.fold_in(arg_keys[8], 71), 0)
    remap_weight = noise(arg_keys[7], (N_DOM, NPAIRS, BLOCK, BLOCK), BLOCK ** -0.5, 0.25, ((0, 32),), jnp.float32)
    return dict(state=state, neighbors=neighbors, edge_coef=edge_coef, sea_mask=sea_mask, pair_source=pair_source, pair_rows=pair_rows, pair_cols=pair_cols, remap_weight=remap_weight)


FORCE_GAIN = 0.5


def reference(state, neighbors, edge_coef, sea_mask, pair_source, pair_rows, pair_cols, remap_weight):
    highest = lax.Precision.HIGHEST
    surfaces = state[:, :FIELDS, :]
    atmos_flat = jnp.transpose(surfaces[:GROUPS - 1], (1, 0, 2)).reshape(FIELDS, (GROUPS - 1) * COLUMNS)
    source_comp = pair_source // DOMAINS
    source_dom = pair_source % DOMAINS
    atmos_index = (source_comp * COLUMNS + source_dom * COLS)[:, :, None] + pair_cols
    ocean_index = (jnp.arange(DOMAINS, dtype=jnp.int32) * COLS)[:, None, None] + pair_rows
    air_values = atmos_flat[:, atmos_index]
    downward = jnp.einsum("dpbj,fdpj->fdpb", remap_weight, air_values, precision=highest)
    sea_force = jnp.zeros((FIELDS, COLUMNS), jnp.float32).at[:, ocean_index].add(downward)
    sea_values = surfaces[GROUPS - 1][:, ocean_index]
    upward = jnp.einsum("dpbj,fdpb->fdpj", remap_weight, sea_values, precision=highest)
    air_force = jnp.zeros((FIELDS, (GROUPS - 1) * COLUMNS), jnp.float32).at[:, atmos_index].add(upward)
    air_force = jnp.transpose(air_force.reshape(FIELDS, GROUPS - 1, COLUMNS), (1, 0, 2))
    forcing = jnp.concatenate([air_force, sea_force[None]], axis=0)
    block_start = (jnp.arange(COLUMNS, dtype=jnp.int32) // COLS) * COLS - RIM
    global_index = (block_start[None, None, :] + neighbors) % COLUMNS
    evolving = jnp.concatenate([jnp.ones((GROUPS - 1, COLUMNS), jnp.int32), sea_mask[None]], axis=0) == 1
    current = state
    for step_number in range(STEPS):
        updated = current
        for edge_number in range(EDGES):
            index_k = jnp.broadcast_to(global_index[:, edge_number][:, None, :], current.shape)
            beside = jnp.take_along_axis(current, index_k, axis=2)
            updated = updated + edge_coef[:, edge_number][:, None, :] * (beside - current)
        updated = updated.at[:, :FIELDS].add(FORCE_GAIN * (forcing - current[:, :FIELDS]))
        current = jnp.where(evolving[:, None, :], updated, current)
    return current
```

```python
import functools

import jax
import jax.numpy as jnp
from jax import lax
from jax.experimental import pallas as pl
from jax.experimental.pallas import tpu as pltpu
from jax.sharding import PartitionSpec as P

FIELDS = 4
RIM = 256
EDGES = 4
STEPS = 4
FORCE_GAIN = 0.5

LANES = 128
SUB = 8
NEAR = 2
NEAR_COUNT = 2 * NEAR + 1
EXTRAS = 4
MESH = pl.DeviceIdType.MESH
F32 = jnp.float32
BF16 = jnp.bfloat16


def with_halo(array, sides, width):
    for axis, dim in sides:
        devices, length = (lax.axis_size(axis), array.shape[dim])
        up = [(i, (i + 1) % devices) for i in range(devices)]
        down = [(j, i) for i, j in up]
        last = lax.slice_in_dim(array, length - width, length, axis=dim)
        leading = lax.slice_in_dim(array, 0, width, axis=dim)
        before = lax.ppermute(last, axis, up)
        after = lax.ppermute(leading, axis, down)
        array = jnp.concatenate([before, array, after], axis=dim)
    return array


def general(state, neighbors, edge_coef, sea_mask, pair_source, pair_rows, pair_cols, remap_weight):
    highest = lax.Precision.HIGHEST
    comp_count = lax.axis_size("comp")
    dom_count = lax.axis_size("dom")
    comp_id = lax.axis_index("comp")
    dom_id = lax.axis_index("dom")
    current = state[0]
    fields = FIELDS
    column_count = current.shape[1]
    pair_count = pair_source.shape[1]
    block = pair_rows.shape[2]
    device_total = comp_count * dom_count
    is_ocean = comp_id == comp_count - 1
    myself = comp_id * dom_count + dom_id
    surface = current[:fields]
    pair_index = jnp.arange(pair_count, dtype=jnp.int32)
    matched = pair_source == myself
    partner = jnp.any(matched, axis=1)
    which_pair = jnp.sum(jnp.where(matched, pair_index[None, :], 0), axis=1)
    my_columns = jnp.sum(jnp.where(matched[:, :, None], pair_cols, 0), axis=1)
    handler_comp = jnp.full_like(which_pair, comp_count - 1)
    activity = jnp.where(is_ocean, 1.0, 0.0).astype(jnp.float32)
    rows_here = pair_rows[0]
    weights_here = remap_weight[0]
    own_sources = lax.dynamic_index_in_dim(pair_source, dom_id, 0, keepdims=False)
    sea_values = surface[:, rows_here]
    upward = jnp.einsum("qbj,fqb->fqj", weights_here, sea_values, precision=highest) * activity
    to_air = jnp.zeros((fields, device_total, block), jnp.float32).at[:, own_sources].add(upward)
    slot_index = handler_comp * dom_count + jnp.arange(dom_count, dtype=jnp.int32)
    air_values = surface[:, my_columns] * partner[None, :, None]
    to_sea = jnp.zeros((fields, device_total, block), jnp.float32).at[:, slot_index].add(air_values)
    got_sea, got_air = (
        lax.all_to_all(to_sea, ("comp", "dom"), split_axis=1, concat_axis=1, tiled=True),
        lax.all_to_all(to_air, ("comp", "dom"), split_axis=1, concat_axis=1, tiled=True),
    )
    incoming = got_sea[:, own_sources]
    downward = jnp.einsum("qbj,fqj->fqb", weights_here, incoming, precision=highest) * activity
    sea_force = jnp.zeros((fields, column_count), jnp.float32).at[:, rows_here].add(downward)
    arrived = got_air[:, slot_index] * partner[None, :, None]
    air_force = jnp.zeros((fields, column_count), jnp.float32).at[:, my_columns].add(arrived)
    forcing = jnp.where(is_ocean, sea_force, air_force)
    adjacency = neighbors[0]
    rates = edge_coef[0]
    evolving = jnp.logical_or(jnp.logical_not(is_ocean), sea_mask == 1)
    for step_number in range(STEPS):
        padded = with_halo(current, (("dom", 1),), RIM)
        updated = current
        for edge_number in range(EDGES):
            updated = updated + rates[edge_number] * (padded[:, adjacency[edge_number]] - current)
        updated = updated.at[:fields].add(FORCE_GAIN * (forcing - current[:fields]))
        current = jnp.where(evolving[None, :], updated, current)
    return current


def lane_gather(values, lanes):
    return jnp.take_along_axis(values, lanes, axis=1, mode="promise_in_bounds")


def interval_kernel(nd, nc, tiles, levels, block, pairs,
                    tab, win, nbr, coef, mask, rows, state_hbm, cols_hbm, w_hbm,
                    out_hbm,
                    pb0, pb1, pb2, pb3, pg0, pg1, pg2, pg3, outb, outg,
                    cols, wbuf, compact, slots, gsl, zslots, usl, sea, fpart, fgot, force,
                    load_sem, w_sem, cols_sem, out_sem,
                    hsend, hrecv, asend, arecv, usend, urecv, ssend, srecv, fsend, frecv):
    comp = lax.axis_index("comp")
    dom = lax.axis_index("dom")
    ocean = nc - 1
    bulk = levels - SUB
    halo = RIM // LANES
    pb = [pb0, pb1, pb2, pb3]
    pg = [pg0, pg1, pg2, pg3]
    left = lax.rem(dom + nd - 1, nd)
    right = lax.rem(dom + 1, nd)
    is_air = comp < ocean
    near_rel = [0, 1, 2, nd - 2, nd - 1]
    T_WHICH, T_SEL, T_EXT, T_VALID = 0, nd, 2 * nd, 2 * nd + EXTRAS
    T_NEARP = 2 * nd + 2 * EXTRAS
    T_EP, T_EVALID, T_ESRC = T_NEARP + NEAR_COUNT, T_NEARP + NEAR_COUNT + 1, T_NEARP + NEAR_COUNT + 2

    def load_g(j):
        return pltpu.make_async_copy(state_hbm.at[pl.ds(0, SUB), pl.ds(j * LANES, LANES)], pg0.at[j + halo], load_sem.at[0])

    def load_b(j):
        return pltpu.make_async_copy(state_hbm.at[pl.ds(SUB, bulk), pl.ds(j * LANES, LANES)], pb0.at[j + halo], load_sem.at[1])

    for j in range(tiles):
        load_g(j).start()
    cols_copy = pltpu.make_async_copy(cols_hbm, cols, cols_sem)
    cols_copy.start()
    for j in range(tiles):
        load_b(j).start()

    @pl.when(is_air)
    def _():
        for p in range(pairs):
            pltpu.make_async_copy(w_hbm.at[p], wbuf.at[p], w_sem).start()

    barrier = pltpu.get_barrier_semaphore()

    @pl.when(is_air)
    def _():
        def greet(r, _):
            pl.semaphore_signal(barrier, inc=1, device_id=(comp, lax.rem(dom + r, nd)), device_id_type=MESH)
            return 0
        lax.fori_loop(1, nd, greet, 0)
        pl.semaphore_signal(barrier, inc=1, device_id=(ocean, dom), device_id_type=MESH)

    @pl.when(jnp.logical_not(is_air))
    def _():
        pl.semaphore_signal(barrier, inc=1, device_id=(comp, left), device_id_type=MESH)
        pl.semaphore_signal(barrier, inc=1, device_id=(comp, right), device_id_type=MESH)
        for c in range(ocean):
            pl.semaphore_signal(barrier, inc=1, device_id=(c, dom), device_id_type=MESH)

    row8 = lax.broadcasted_iota(jnp.int32, (SUB, LANES), 0)

    def doubled(ref, offset):
        out = []
        for h in range(tiles):
            v = ref[h + offset]
            out.append(jnp.where(row8 < FIELDS, v, pltpu.roll(v, FIELDS, axis=0)))
        return out

    def gather_slot(table, index):
        res = []
        for q in range(0, block // LANES, 2):
            i0 = index[:, q * LANES:(q + 1) * LANES]
            i1 = index[:, (q + 1) * LANES:(q + 2) * LANES]
            i8 = jnp.where(row8 < FIELDS, jnp.broadcast_to(i0, (SUB, LANES)), jnp.broadcast_to(i1, (SUB, LANES)))
            lo = i8 & (LANES - 1)
            hi = i8 >> 7
            acc = lane_gather(table[0], lo)
            for h in range(1, tiles):
                acc = jnp.where(hi == h, lane_gather(table[h], lo), acc)
            res.append(acc)
        return res

    def split_rows(res):
        cols_ = []
        for acc in res:
            high = acc.astype(BF16).astype(F32)
            low = acc - high
            cols_.append(jnp.where(row8 < FIELDS, high, pltpu.roll(low, FIELDS, axis=0)))
            cols_.append(jnp.where(row8 < FIELDS, pltpu.roll(high, FIELDS, axis=0), low))
        return jnp.concatenate(cols_, axis=1)

    def scatter(eight, index):
        hi = jnp.broadcast_to(index >> 7, (SUB, block))
        lhs = jnp.concatenate([jnp.where(hi == h, eight, 0.0) for h in range(tiles)], axis=0).astype(BF16)
        lo = jnp.broadcast_to(index & (LANES - 1), (LANES, block))
        hot = jnp.where(lo == lax.broadcasted_iota(jnp.int32, (LANES, block), 0), 1.0, 0.0).astype(BF16)
        return lax.dot_general(lhs, hot, (((1,), (1,)), ((), ())), preferred_element_type=F32)

    def cols_of(t):
        return cols[t, pl.ds(tab[T_WHICH + t], 1), :]

    pltpu.make_async_copy(pg0.at[pl.ds(halo, tiles)], pg0.at[pl.ds(halo, tiles)], load_sem.at[0]).wait()
    cols_copy.wait()

    @pl.when(is_air)
    def _():
        table = doubled(pg0, halo)
        for n, r in enumerate(near_rel):
            t = lax.rem(dom + r, nd)
            res = gather_slot(table, cols_of(t))
            for i, acc in enumerate(res):
                if r == 0:
                    gsl[dom, i] = acc
                else:
                    slots[r, i] = acc

        def extra(e, _):
            res = gather_slot(table, cols_of(tab[T_EXT + e]))
            for i, acc in enumerate(res):
                compact[e, i] = acc
            return 0
        lax.fori_loop(0, EXTRAS, extra, 0)

        def fill(r, _):
            t = lax.rem(dom + r, nd)
            slots[r] = compact[tab[T_SEL + t]]
            return 0
        lax.fori_loop(NEAR + 1, nd - NEAR, fill, 0)

    @pl.when(is_air)
    def _():
        pl.semaphore_wait(barrier, nd)

    @pl.when(jnp.logical_not(is_air))
    def _():
        pl.semaphore_wait(barrier, 2 + ocean)

    def a_copy(r):
        return pltpu.make_async_remote_copy(
            src_ref=slots.at[r], dst_ref=gsl.at[dom], send_sem=asend, recv_sem=arecv,
            device_id=(comp, lax.rem(dom + r, nd)), device_id_type=MESH)

    def halo_copies(ref, s, kind):
        to_left = pltpu.make_async_remote_copy(
            src_ref=ref.at[pl.ds(halo, halo)], dst_ref=ref.at[pl.ds(tiles + halo, halo)],
            send_sem=hsend.at[kind, s, 0], recv_sem=hrecv.at[kind, s, 0], device_id=(comp, left), device_id_type=MESH)
        to_right = pltpu.make_async_remote_copy(
            src_ref=ref.at[pl.ds(tiles, halo)], dst_ref=ref.at[pl.ds(0, halo)],
            send_sem=hsend.at[kind, s, 1], recv_sem=hrecv.at[kind, s, 1], device_id=(comp, right), device_id_type=MESH)
        return to_left, to_right

    def sea_copy(c):
        return pltpu.make_async_remote_copy(
            src_ref=pg0.at[pl.ds(halo, tiles)], dst_ref=sea, send_sem=ssend, recv_sem=srecv,
            device_id=(c, dom), device_id_type=MESH)

    @pl.when(jnp.logical_not(is_air))
    def _():
        for c in range(ocean):
            sea_copy(c).start()

    @pl.when(is_air)
    def _():
        def send(r, _):
            a_copy(r).start()
            return 0
        lax.fori_loop(1, nd, send, 0)

    for c in halo_copies(pg[0], 0, 0):
        c.start()
    pltpu.make_async_copy(pb0.at[pl.ds(halo, tiles)], pb0.at[pl.ds(halo, tiles)], load_sem.at[1]).wait()
    for c in halo_copies(pb[0], 0, 1):
        c.start()

    lane1 = lax.broadcasted_iota(jnp.int32, (1, LANES), 1)

    def tile_step(src, j, rows_, forced):
        cols_j = pl.ds(pl.multiple_of(j * LANES, LANES), LANES)
        cur = src[j + halo]
        upd = cur
        low = jnp.broadcast_to(lane1 < LANES // 2, (rows_, LANES))
        for k in range(EDGES):
            lo = jnp.broadcast_to(nbr[pl.ds(k, 1), cols_j] & (LANES - 1), (rows_, LANES))
            got = []
            for h in range(2):
                w = win[(k * tiles + j) * 2 + h]
                b = jnp.minimum(w >> 7, tiles + 2 * halo - 2)
                edge = jnp.broadcast_to(lane1 >= w - b * LANES, (rows_, LANES))
                got.append(lane_gather(jnp.where(edge, src[b], src[b + 1]), lo))
            upd = upd + coef[pl.ds(k, 1), cols_j] * (jnp.where(low, got[0], got[1]) - cur)
        if forced:
            gain = jnp.where(row8 < FIELDS, FORCE_GAIN, 0.0)
            upd = upd + gain * (force[j] - cur)
        keep = jnp.logical_or(is_air, mask[:, cols_j] == 1)
        return jnp.where(jnp.broadcast_to(keep, (rows_, LANES)), upd, cur)

    def bulk_step(s):
        src = pb[s]
        dst, off = (pb[s + 1], halo) if s + 1 < STEPS else (outb, 0)
        per = 2

        def body(i, _):
            new = [tile_step(src, i * per + u, bulk, False) for u in range(per)]
            for u in range(per):
                dst[i * per + u + off] = new[u]
            return 0
        for c in halo_copies(src, s, 1):
            c.wait()
        lax.fori_loop(0, tiles // per, body, 0)
        if s + 1 < STEPS:
            for c in halo_copies(pb[s + 1], s + 1, 1):
                c.start()

    def group_step(s):
        src = pg[s]
        dst, off = (pg[s + 1], halo) if s + 1 < STEPS else (outg, 0)
        for c in halo_copies(src, s, 0):
            c.wait()
        new = [tile_step(src, j, SUB, True) for j in range(tiles)]
        for j in range(tiles):
            dst[j + off] = new[j]
        if s + 1 < STEPS:
            for c in halo_copies(pg[s + 1], s + 1, 0):
                c.start()

    bulk_step(0)

    @pl.when(is_air)
    def _():
        pltpu.make_async_copy(gsl.at[pl.ds(0, nd - 1)], gsl.at[pl.ds(0, nd - 1)], arecv).wait()
        pltpu.make_async_copy(sea, sea, srecv).wait()
        pltpu.make_async_copy(w_hbm, wbuf, w_sem).wait()
        sea_table = doubled(sea, 0)
        total = jnp.zeros((tiles * SUB, LANES), F32)

        def dense(p, src):
            w = wbuf[p]
            wh = w.astype(BF16)
            wl = (w - wh.astype(F32)).astype(BF16)
            index = rows[pl.ds(p, 1), :]
            x = split_rows([gsl[src, i] for i in range(block // (2 * LANES))]).astype(BF16)
            v = split_rows(gather_slot(sea_table, index)).astype(BF16)
            dims = (((1,), (1,)), ((), ()))
            y = (lax.dot_general(x, wh, dims, preferred_element_type=F32)
                 + lax.dot_general(x, wl, dims, preferred_element_type=F32))
            z = jnp.dot(v, wh, preferred_element_type=F32) + jnp.dot(v, wl, preferred_element_type=F32)
            y = y[:FIELDS] + y[FIELDS:]
            z = z[:FIELDS] + z[FIELDS:]
            yh = y.astype(BF16).astype(F32)
            return jnp.concatenate([yh, y - yh], axis=0), z, index

        def put(ref, at, z):
            for q in range(block // LANES):
                ref[at, q // 2, pl.ds((q % 2) * FIELDS, FIELDS), :] = z[:, q * LANES:(q + 1) * LANES]

        def u_copy(slot, r):
            return pltpu.make_async_remote_copy(
                src_ref=zslots.at[slot], dst_ref=usl.at[dom], send_sem=usend, recv_sem=urecv,
                device_id=(comp, lax.rem(dom + r, nd)), device_id_type=MESH)

        eight, z, index = dense(tab[T_EP], tab[T_ESRC])
        put(zslots, NEAR_COUNT, z)

        def send(r, _):
            u_copy(NEAR_COUNT, r).start()
            return 0
        lax.fori_loop(NEAR + 1, nd - NEAR, send, 0)
        total = total + scatter(jnp.where(tab[T_EVALID] == 1, eight, 0.0), index)
        for n, r in enumerate(near_rel):
            eight, z, index = dense(tab[T_NEARP + n], lax.rem(dom + r, nd))
            if r == 0:
                put(usl, dom, z)
            else:
                put(zslots, n, z)
                u_copy(n, r).start()
            total = total + scatter(eight, index)
        for h in range(tiles):
            part = total[h * SUB:(h + 1) * SUB]
            fpart[h] = part + pltpu.roll(part, FIELDS, axis=0)
        pltpu.make_async_remote_copy(
            src_ref=fpart, dst_ref=fgot.at[comp], send_sem=fsend, recv_sem=frecv,
            device_id=(ocean, dom), device_id_type=MESH).start()

    bulk_step(1)

    @pl.when(is_air)
    def _():
        pltpu.make_async_copy(usl.at[pl.ds(0, nd - 1)], usl.at[pl.ds(0, nd - 1)], urecv).wait()
        total = jnp.zeros((tiles * SUB, LANES), F32)
        for r in near_rel:
            t = lax.rem(dom + r, nd)
            total = total + scatter(split_rows([usl[t, i] for i in range(block // (2 * LANES))]), cols_of(t))
        for e in range(EXTRAS):
            t = tab[T_EXT + e]
            eight = split_rows([usl[t, i] for i in range(block // (2 * LANES))])
            total = total + scatter(jnp.where(tab[T_VALID + e] == 1, eight, 0.0), cols_of(t))
        for h in range(tiles):
            part = total[h * SUB:(h + 1) * SUB]
            force[h] = part + pltpu.roll(part, FIELDS, axis=0)

    @pl.when(jnp.logical_not(is_air))
    def _():
        pltpu.make_async_copy(fgot, fgot, frecv).wait()
        for h in range(tiles):
            force[h] = fgot[0, h] + fgot[1, h] + fgot[2, h]

    group_step(0)
    bulk_step(2)
    group_step(1)
    bulk_step(3)

    def store_b(j):
        return pltpu.make_async_copy(outb.at[j], out_hbm.at[pl.ds(SUB, bulk), pl.ds(j * LANES, LANES)], out_sem.at[1])

    def store_g(j):
        return pltpu.make_async_copy(outg.at[j], out_hbm.at[pl.ds(0, SUB), pl.ds(j * LANES, LANES)], out_sem.at[0])

    for j in range(tiles):
        store_b(j).start()
    group_step(2)
    group_step(3)
    for j in range(tiles):
        store_g(j).start()

    @pl.when(is_air)
    def _():
        pltpu.make_async_copy(slots.at[pl.ds(0, nd - 1)], slots.at[pl.ds(0, nd - 1)], asend).wait()
        pltpu.make_async_copy(slots.at[pl.ds(0, nd - 1)], slots.at[pl.ds(0, nd - 1)], usend).wait()
        pltpu.make_async_copy(fpart, fpart, fsend).wait()

    @pl.when(jnp.logical_not(is_air))
    def _():
        pltpu.make_async_copy(fgot, fgot, ssend).wait()

    pltpu.make_async_copy(outb, outb, out_sem.at[1]).wait()
    pltpu.make_async_copy(outg, outg, out_sem.at[0]).wait()


def windowed(state, neighbors, edge_coef, sea_mask, pair_rows, pair_cols, remap_weight, table, windows):
    nd, nc = lax.axis_size("dom"), lax.axis_size("comp")
    _, levels, columns = state.shape
    tiles = columns // LANES
    padded = tiles + 2 * RIM // LANES
    pairs, block = pair_rows.shape[1:]
    pieces = block // (2 * LANES)
    bulk = levels - SUB
    smem = pl.BlockSpec(memory_space=pltpu.SMEM)
    vmem = pl.BlockSpec(memory_space=pltpu.VMEM)
    hbm = pl.BlockSpec(memory_space=pl.ANY)
    dma = pltpu.SemaphoreType.DMA
    scratch = (
        [pltpu.VMEM((padded, bulk, LANES), F32)] * STEPS
        + [pltpu.VMEM((padded, SUB, LANES), F32)] * STEPS
        + [pltpu.VMEM((tiles, bulk, LANES), F32), pltpu.VMEM((tiles, SUB, LANES), F32)]
        + [
            pltpu.VMEM(pair_cols.shape, jnp.int32),
            pltpu.VMEM((pairs, block, block), F32),
            pltpu.VMEM((EXTRAS, pieces, SUB, LANES), F32),
            pltpu.VMEM((nd, pieces, SUB, LANES), F32),
            pltpu.VMEM((nd, pieces, SUB, LANES), F32),
            pltpu.VMEM((NEAR_COUNT + 1, pieces, SUB, LANES), F32),
            pltpu.VMEM((nd, pieces, SUB, LANES), F32),
            pltpu.VMEM((tiles, SUB, LANES), F32),
            pltpu.VMEM((tiles, SUB, LANES), F32),
            pltpu.VMEM((nc - 1, tiles, SUB, LANES), F32),
            pltpu.VMEM((tiles, SUB, LANES), F32),
        ]
        + [dma((2,)), dma, dma, dma((2,))]
        + [dma((2, STEPS, 2)), dma((2, STEPS, 2))]
        + [dma] * 8
    )
    return pl.pallas_call(
        functools.partial(interval_kernel, nd, nc, tiles, levels, block, pairs),
        out_shape=jax.ShapeDtypeStruct((levels, columns), F32),
        in_specs=[smem, smem, vmem, vmem, vmem, vmem, hbm, hbm, hbm],
        out_specs=hbm,
        scratch_shapes=scratch,
        name="interval",
        cost_estimate=pl.CostEstimate(flops=10**9, bytes_accessed=10**8, transcendentals=0),
        compiler_params=pltpu.CompilerParams(
            collective_id=0, has_side_effects=True, vmem_limit_bytes=48 * 2**20),
    )(table, windows, neighbors[0], edge_coef[0], sea_mask[None], pair_rows[0], state[0], pair_cols, remap_weight[0])


def local(state, neighbors, edge_coef, sea_mask, pair_source, pair_rows, pair_cols, remap_weight):
    nd, nc = lax.axis_size("dom"), lax.axis_size("comp")
    comp, dom = lax.axis_index("comp"), lax.axis_index("dom")
    columns = state.shape[2]
    tiles = columns // LANES
    pairs = pair_source.shape[1]
    i32 = jnp.int32

    halves = neighbors[0].reshape(EDGES * tiles * 2, LANES // 2)
    windows = jnp.minimum(jnp.min(halves, axis=1), columns + 2 * RIM - LANES)
    wide = jnp.max(jnp.max(halves, axis=1) - windows) >= LANES

    t = jnp.arange(nd, dtype=i32)
    index = jnp.arange(pairs, dtype=i32)
    matched = pair_source == comp * nd + dom
    which = jnp.sum(jnp.where(matched, index[None], 0), axis=1).astype(i32)
    offset = jnp.mod(t - dom, nd)
    far = jnp.any(matched, axis=1) & (offset > NEAR) & (offset < nd - NEAR)
    rank = jnp.cumsum(far.astype(i32)) - 1
    sel = jnp.clip(jnp.where(far, rank, 0), 0, EXTRAS - 1).astype(i32)
    hit = far[None] & (rank[None] == jnp.arange(EXTRAS, dtype=i32)[:, None])
    ext = jnp.sum(jnp.where(hit, t[None], 0), axis=1).astype(i32)
    valid = jnp.any(hit, axis=1).astype(i32)
    crowded = jnp.sum(far.astype(i32)) > EXTRAS

    own = lax.dynamic_index_in_dim(pair_source, dom, 0, keepdims=False)
    own_offset = jnp.mod(own % nd - dom, nd)
    own_band = own // nd == comp
    rel = jnp.array([0, 1, 2, nd - 2, nd - 1], i32)
    near_p = jnp.sum(jnp.where((own_offset[None] == rel[:, None]) & own_band[None], index[None], 0), axis=1).astype(i32)
    own_far = (own_offset > NEAR) & (own_offset < nd - NEAR) & own_band
    e_p = jnp.sum(jnp.where(own_far, index, 0)).astype(i32)
    e_valid = jnp.any(own_far).astype(i32)
    e_src = jnp.sum(jnp.where(own_far, own % nd, 0)).astype(i32)
    table = jnp.concatenate([which, sel, ext, valid, near_p, jnp.stack([e_p, e_valid, e_src])])

    bad = lax.psum(jnp.where(wide | crowded, 1.0, 0.0).astype(F32), ("comp", "dom")) > 0
    fast = windowed(state, neighbors, edge_coef, sea_mask, pair_rows, pair_cols, remap_weight, table, windows)
    args = (state, neighbors, edge_coef, sea_mask, pair_source, pair_rows, pair_cols, remap_weight)
    return lax.cond(bad, lambda f, *a: general(*a), lambda f, *a: f, fast, *args)[None]


def solution(mesh):
    placed = (
        P("comp", None, "dom"),
        P("comp", None, "dom"),
        P("comp", None, "dom"),
        P("dom"),
        P(),
        P("dom", None, None),
        P(),
        P("dom", None, None, None),
    )
    return jax.shard_map(
        local, mesh=mesh, in_specs=placed, out_specs=P("comp", None, "dom"), check_vma=False
    )
```

```python
import functools

import jax
import jax.numpy as jnp
from jax import lax
from jax.experimental import pallas as pl
from jax.experimental.layout import Layout, with_layout_constraint
from jax.experimental.pallas import tpu as pltpu
from jax.sharding import PartitionSpec as P

FIELDS = 4
RIM = 256
EDGES = 4
STEPS = 4
FORCE_GAIN = 0.5

LANES = 128
SUB = 8
NEAR = 2
NEAR_COUNT = 2 * NEAR + 1
EXTRAS = 4
MESH = pl.DeviceIdType.MESH
F32 = jnp.float32
BF16 = jnp.bfloat16


def with_halo(array, sides, width):
    for axis, dim in sides:
        devices, length = (lax.axis_size(axis), array.shape[dim])
        up = [(i, (i + 1) % devices) for i in range(devices)]
        down = [(j, i) for i, j in up]
        last = lax.slice_in_dim(array, length - width, length, axis=dim)
        leading = lax.slice_in_dim(array, 0, width, axis=dim)
        before = lax.ppermute(last, axis, up)
        after = lax.ppermute(leading, axis, down)
        array = jnp.concatenate([before, array, after], axis=dim)
    return array


def general(state, neighbors, edge_coef, sea_mask, pair_source, pair_rows, pair_cols, remap_weight):
    highest = lax.Precision.HIGHEST
    comp_count = lax.axis_size("comp")
    dom_count = lax.axis_size("dom")
    comp_id = lax.axis_index("comp")
    dom_id = lax.axis_index("dom")
    current = with_layout_constraint(state, Layout((0, 1, 2)))[0]
    fields = FIELDS
    column_count = current.shape[1]
    pair_count = pair_source.shape[1]
    block = pair_rows.shape[2]
    device_total = comp_count * dom_count
    is_ocean = comp_id == comp_count - 1
    myself = comp_id * dom_count + dom_id
    surface = current[:fields]
    pair_index = jnp.arange(pair_count, dtype=jnp.int32)
    matched = pair_source == myself
    partner = jnp.any(matched, axis=1)
    which_pair = jnp.sum(jnp.where(matched, pair_index[None, :], 0), axis=1)
    my_columns = jnp.sum(jnp.where(matched[:, :, None], pair_cols, 0), axis=1)
    handler_comp = jnp.full_like(which_pair, comp_count - 1)
    activity = jnp.where(is_ocean, 1.0, 0.0).astype(jnp.float32)
    rows_here = pair_rows[0]
    weights_here = remap_weight[0]
    own_sources = lax.dynamic_index_in_dim(pair_source, dom_id, 0, keepdims=False)
    sea_values = surface[:, rows_here]
    upward = jnp.einsum("qbj,fqb->fqj", weights_here, sea_values, precision=highest) * activity
    to_air = jnp.zeros((fields, device_total, block), jnp.float32).at[:, own_sources].add(upward)
    slot_index = handler_comp * dom_count + jnp.arange(dom_count, dtype=jnp.int32)
    air_values = surface[:, my_columns] * partner[None, :, None]
    to_sea = jnp.zeros((fields, device_total, block), jnp.float32).at[:, slot_index].add(air_values)
    got_sea, got_air = (
        lax.all_to_all(to_sea, ("comp", "dom"), split_axis=1, concat_axis=1, tiled=True),
        lax.all_to_all(to_air, ("comp", "dom"), split_axis=1, concat_axis=1, tiled=True),
    )
    incoming = got_sea[:, own_sources]
    downward = jnp.einsum("qbj,fqj->fqb", weights_here, incoming, precision=highest) * activity
    sea_force = jnp.zeros((fields, column_count), jnp.float32).at[:, rows_here].add(downward)
    arrived = got_air[:, slot_index] * partner[None, :, None]
    air_force = jnp.zeros((fields, column_count), jnp.float32).at[:, my_columns].add(arrived)
    forcing = jnp.where(is_ocean, sea_force, air_force)
    adjacency = neighbors[0]
    rates = edge_coef[0]
    evolving = jnp.logical_or(jnp.logical_not(is_ocean), sea_mask == 1)

    def advance(_, current):
        padded = with_halo(current, (("dom", 1),), RIM)
        updated = current
        for edge_number in range(EDGES):
            updated = updated + rates[edge_number] * (padded[:, adjacency[edge_number]] - current)
        updated = updated.at[:fields].add(FORCE_GAIN * (forcing - current[:fields]))
        return jnp.where(evolving[None, :], updated, current)

    return with_layout_constraint(lax.fori_loop(0, STEPS, advance, current), Layout((0, 1)))


def lane_gather(values, lanes):
    return jnp.take_along_axis(values, lanes, axis=1, mode="promise_in_bounds")


def interval_kernel(nd, nc, tiles, levels, block, pairs,
                    nbr, coef, mask, rows, sources, state_hbm, cols_hbm, w_hbm,
                    out_hbm, flag_out,
                    pb0, pb1, pb2, pb3, pg0, pg1, pg2, pg3, outb, outg,
                    cols, wbuf, compact, slots, gsl, zslots, usl, sea, fpart, fgot, force,
                    tabv, tab, flags, flags_in, tab_sem, gsend, grecv,
                    load_sem, w_sem, cols_sem, out_sem,
                    hsend, hrecv, asend, arecv, usend, urecv, ssend, srecv, fsend, frecv):
    comp = lax.axis_index("comp")
    dom = lax.axis_index("dom")
    ocean = nc - 1
    bulk = levels - SUB
    halo = RIM // LANES
    pb = [pb0, pb1, pb2, pb3]
    pg = [pg0, pg1, pg2, pg3]
    left = lax.rem(dom + nd - 1, nd)
    right = lax.rem(dom + 1, nd)
    is_air = comp < ocean
    near_rel = [0, 1, 2, nd - 2, nd - 1]
    T_WHICH, T_SEL, T_EXT, T_VALID = 0, 1, 2, 2 + EXTRAS
    T_NEARP = 2 + 2 * EXTRAS
    T_EP = T_NEARP + NEAR_COUNT
    T_EVALID, T_ESRC = T_EP + 1, T_EP + 2

    def load_g(j):
        return pltpu.make_async_copy(state_hbm.at[pl.ds(0, SUB), pl.ds(j * LANES, LANES)], pg0.at[j + halo], load_sem.at[0])

    def load_b(j):
        return pltpu.make_async_copy(state_hbm.at[pl.ds(SUB, bulk), pl.ds(j * LANES, LANES)], pb0.at[j + halo], load_sem.at[1])

    for j in range(tiles):
        load_g(j).start()
    cols_copy = pltpu.make_async_copy(cols_hbm, cols, cols_sem)
    cols_copy.start()
    for j in range(tiles):
        load_b(j).start()

    @pl.when(is_air)
    def _():
        for p in range(pairs):
            pltpu.make_async_copy(w_hbm.at[p], wbuf.at[p], w_sem).start()

    barrier = pltpu.get_barrier_semaphore()

    def greet(r, _):
        pl.semaphore_signal(barrier, inc=1, device_id=(comp, lax.rem(dom + r, nd)), device_id_type=MESH)
        return 0
    lax.fori_loop(1, nd, greet, 0)
    for c in range(1, nc):
        pl.semaphore_signal(barrier, inc=1, device_id=(lax.rem(comp + c, nc), dom), device_id_type=MESH)

    def build_tables():
        src = sources[...]
        p_i = lax.broadcasted_iota(jnp.int32, (nd, pairs), 1)
        t_i = lax.broadcasted_iota(jnp.int32, (nd, pairs), 0)
        t_c = lax.broadcasted_iota(jnp.int32, (nd, 1), 0)
        dom_f = dom
        base = (comp * nd)

        def is_far(offset):
            offset = jnp.where(offset < 0, offset + nd, offset)
            return jnp.logical_and(offset > NEAR, offset < nd - NEAR)

        mine = src == base + dom_f
        which = jnp.sum(jnp.where(mine, p_i, 0), axis=1, keepdims=True)
        hit = jnp.max(jnp.where(mine, 1, 0), axis=1, keepdims=True)
        far = jnp.where(jnp.logical_and(hit > 0, is_far(t_c - dom_f)), 1, 0)
        lanes = [(T_WHICH, which)]
        sel = jnp.zeros((nd, 1), jnp.int32)
        last = jnp.full((1, 1), -1, jnp.int32)
        for e in range(EXTRAS):
            last = jnp.min(jnp.where(jnp.logical_and(far > 0, t_c > last), t_c, nd), axis=0, keepdims=True)
            sel = jnp.where(t_c == last, e, sel)
            lanes.append((T_EXT + e, last))
            lanes.append((T_VALID + e, jnp.where(last < nd, 1, 0)))
        lanes.append((T_SEL, sel))
        crowded = jnp.sum(far, axis=0, keepdims=True) > EXTRAS

        own = jnp.sum(jnp.where(t_i == dom_f, src, 0), axis=0, keepdims=True) - base
        p_r = p_i[:1]
        for n, r in enumerate(near_rel):
            place = lax.rem(dom + r, nd)
            lanes.append((T_NEARP + n, jnp.sum(jnp.where(own == place, p_r, 0), axis=1, keepdims=True)))
        in_band = jnp.logical_and(own >= 0, own < nd)
        far_own = jnp.where(jnp.logical_and(in_band, is_far(own - dom_f)), 1, 0)
        lanes.append((T_EP, jnp.sum(far_own * p_r, axis=1, keepdims=True)))
        lanes.append((T_EVALID, jnp.max(far_own, axis=1, keepdims=True)))
        lanes.append((T_ESRC, jnp.sum(far_own * own, axis=1, keepdims=True)))
        lane = lax.broadcasted_iota(jnp.int32, (nd, LANES), 1)
        packed = jnp.zeros((nd, LANES), jnp.int32)
        for at, value in lanes:
            value = jnp.minimum(value, ((nd if at in (T_ESRC, *range(T_EXT, T_EXT + EXTRAS)) else pairs) - 1))
            packed = jnp.where(lane == at, jnp.broadcast_to(value, (nd, LANES)), packed)
        tabv[pl.ds(0, nd), :] = packed

        reach = jnp.concatenate(
            [nbr[:, j * LANES:(j + 1) * LANES] for j in range(tiles)], axis=0)
        lane = lax.broadcasted_iota(jnp.int32, reach.shape, 1)
        wide = jnp.zeros((1, 1), jnp.int32)
        packed = jnp.zeros(reach.shape, jnp.int32)
        for h, side in enumerate((lane < LANES // 2, lane >= LANES // 2)):
            first = jnp.min(jnp.where(side, reach, 2**30), axis=1, keepdims=True)
            first = jnp.clip(first, 0, ((tiles + 2 * halo - 1) * LANES))
            final = jnp.max(jnp.where(side, reach, -1), axis=1, keepdims=True)
            wide = jnp.maximum(wide, jnp.max(final - first, axis=0, keepdims=True))
            packed = jnp.where(lane == h, jnp.broadcast_to(first, reach.shape), packed)
        tabv[pl.ds(nd, EDGES * tiles), :] = packed
        bad = jnp.logical_or(wide >= LANES, crowded)
        flags[0] = jnp.broadcast_to(jnp.where(bad, 1.0, 0.0), (SUB, LANES))

    build_tables()
    to_smem = pltpu.make_async_copy(tabv, tab, tab_sem)
    to_smem.start()

    hops = []
    reach_d = 1
    while reach_d < nd:
        hops.append((0, reach_d))
        reach_d *= 2
    reach_c = 1
    while reach_c < nc:
        hops.append((reach_c, 0))
        reach_c *= 2

    def flag_copy(i):
        dc, dd = hops[i]
        return pltpu.make_async_remote_copy(
            src_ref=flags.at[i], dst_ref=flags_in.at[i], send_sem=gsend.at[i], recv_sem=grecv.at[i],
            device_id=(lax.rem(comp + dc, nc), lax.rem(dom + dd, nd)), device_id_type=MESH)

    def flag_next(i):
        flag_copy(i).wait()
        flags[i + 1] = jnp.maximum(flags[i], flags_in[i])
        if i + 1 < len(hops):
            flag_copy(i + 1).start()

    row8 = lax.broadcasted_iota(jnp.int32, (SUB, LANES), 0)

    def doubled(ref, offset):
        out = []
        for h in range(tiles):
            v = ref[h + offset]
            out.append(jnp.where(row8 < FIELDS, v, pltpu.roll(v, FIELDS, axis=0)))
        return out

    def gather_slot(table, index):
        res = []
        for q in range(0, block // LANES, 2):
            i0 = index[:, q * LANES:(q + 1) * LANES]
            i1 = index[:, (q + 1) * LANES:(q + 2) * LANES]
            i8 = jnp.where(row8 < FIELDS, jnp.broadcast_to(i0, (SUB, LANES)), jnp.broadcast_to(i1, (SUB, LANES)))
            lo = i8 & (LANES - 1)
            hi = i8 >> 7
            acc = lane_gather(table[0], lo)
            for h in range(1, tiles):
                acc = jnp.where(hi == h, lane_gather(table[h], lo), acc)
            res.append(acc)
        return res

    def split_rows(res):
        cols_ = []
        for acc in res:
            high = acc.astype(BF16).astype(F32)
            low = acc - high
            cols_.append(jnp.where(row8 < FIELDS, high, pltpu.roll(low, FIELDS, axis=0)))
            cols_.append(jnp.where(row8 < FIELDS, pltpu.roll(high, FIELDS, axis=0), low))
        return jnp.concatenate(cols_, axis=1)

    def scatter(eight, index):
        hi = jnp.broadcast_to(index >> 7, (SUB, block))
        lhs = jnp.concatenate([jnp.where(hi == h, eight, 0.0) for h in range(tiles)], axis=0).astype(BF16)
        lo = jnp.broadcast_to(index & (LANES - 1), (LANES, block))
        hot = jnp.where(lo == lax.broadcasted_iota(jnp.int32, (LANES, block), 0), 1.0, 0.0).astype(BF16)
        return lax.dot_general(lhs, hot, (((1,), (1,)), ((), ())), preferred_element_type=F32)

    def cols_of(t):
        return cols[t, pl.ds(tab[t, T_WHICH], 1), :]

    pltpu.make_async_copy(pg0.at[pl.ds(halo, tiles)], pg0.at[pl.ds(halo, tiles)], load_sem.at[0]).wait()
    cols_copy.wait()
    to_smem.wait()

    @pl.when(is_air)
    def _():
        table = doubled(pg0, halo)
        for n, r in enumerate(near_rel):
            t = lax.rem(dom + r, nd)
            res = gather_slot(table, cols_of(t))
            for i, acc in enumerate(res):
                if r == 0:
                    gsl[dom, i] = acc
                else:
                    slots[r, i] = acc

        def extra(e, _):
            res = gather_slot(table, cols_of(tab[0, T_EXT + e]))
            for i, acc in enumerate(res):
                compact[e, i] = acc
            return 0
        lax.fori_loop(0, EXTRAS, extra, 0)

        def fill(r, _):
            t = lax.rem(dom + r, nd)
            slots[r] = compact[tab[t, T_SEL]]
            return 0
        lax.fori_loop(NEAR + 1, nd - NEAR, fill, 0)

    pl.semaphore_wait(barrier, nd + nc - 2)

    def a_copy(r):
        return pltpu.make_async_remote_copy(
            src_ref=slots.at[r], dst_ref=gsl.at[dom], send_sem=asend, recv_sem=arecv,
            device_id=(comp, lax.rem(dom + r, nd)), device_id_type=MESH)

    def halo_copies(ref, s, kind):
        to_left = pltpu.make_async_remote_copy(
            src_ref=ref.at[pl.ds(halo, halo)], dst_ref=ref.at[pl.ds(tiles + halo, halo)],
            send_sem=hsend.at[kind, s, 0], recv_sem=hrecv.at[kind, s, 0], device_id=(comp, left), device_id_type=MESH)
        to_right = pltpu.make_async_remote_copy(
            src_ref=ref.at[pl.ds(tiles, halo)], dst_ref=ref.at[pl.ds(0, halo)],
            send_sem=hsend.at[kind, s, 1], recv_sem=hrecv.at[kind, s, 1], device_id=(comp, right), device_id_type=MESH)
        return to_left, to_right

    def sea_copy(c):
        return pltpu.make_async_remote_copy(
            src_ref=pg0.at[pl.ds(halo, tiles)], dst_ref=sea, send_sem=ssend, recv_sem=srecv,
            device_id=(c, dom), device_id_type=MESH)

    @pl.when(jnp.logical_not(is_air))
    def _():
        for c in range(ocean):
            sea_copy(c).start()

    @pl.when(is_air)
    def _():
        def send(r, _):
            a_copy(r).start()
            return 0
        lax.fori_loop(1, nd, send, 0)

    for c in halo_copies(pg[0], 0, 0):
        c.start()
    pltpu.make_async_copy(pb0.at[pl.ds(halo, tiles)], pb0.at[pl.ds(halo, tiles)], load_sem.at[1]).wait()
    for c in halo_copies(pb[0], 0, 1):
        c.start()
    flag_copy(0).start()

    lane1 = lax.broadcasted_iota(jnp.int32, (1, LANES), 1)

    def tile_step(src, j, rows_, forced):
        cols_j = pl.ds(pl.multiple_of(j * LANES, LANES), LANES)
        cur = src[j + halo]
        upd = cur
        low = jnp.broadcast_to(lane1 < LANES // 2, (rows_, LANES))
        for k in range(EDGES):
            lo = jnp.broadcast_to(nbr[pl.ds(k, 1), cols_j] & (LANES - 1), (rows_, LANES))
            got = []
            for h in range(2):
                w = tab[nd + j * EDGES + k, h]
                b = jnp.minimum(w >> 7, tiles + 2 * halo - 2)
                edge = jnp.broadcast_to(lane1 >= w - b * LANES, (rows_, LANES))
                got.append(lane_gather(jnp.where(edge, src[b], src[b + 1]), lo))
            upd = upd + coef[pl.ds(k, 1), cols_j] * (jnp.where(low, got[0], got[1]) - cur)
        if forced:
            gain = jnp.where(row8 < FIELDS, FORCE_GAIN, 0.0)
            upd = upd + gain * (force[j] - cur)
        keep = jnp.logical_or(is_air, mask[:, cols_j] == 1)
        return jnp.where(jnp.broadcast_to(keep, (rows_, LANES)), upd, cur)

    def bulk_step(s):
        src = pb[s]
        dst, off = (pb[s + 1], halo) if s + 1 < STEPS else (outb, 0)
        per = 4

        def body(i, _):
            new = [tile_step(src, i * per + u, bulk, False) for u in range(per)]
            for u in range(per):
                dst[i * per + u + off] = new[u]
            return 0
        for c in halo_copies(src, s, 1):
            c.wait()
        lax.fori_loop(0, tiles // per, body, 0)
        if s + 1 < STEPS:
            for c in halo_copies(pb[s + 1], s + 1, 1):
                c.start()

    def group_step(s):
        src = pg[s]
        dst, off = (pg[s + 1], halo) if s + 1 < STEPS else (outg, 0)
        for c in halo_copies(src, s, 0):
            c.wait()
        new = [tile_step(src, j, SUB, True) for j in range(tiles)]
        for j in range(tiles):
            dst[j + off] = new[j]
        if s + 1 < STEPS:
            for c in halo_copies(pg[s + 1], s + 1, 0):
                c.start()

    bulk_step(0)
    flag_next(0)

    @pl.when(is_air)
    def _():
        pltpu.make_async_copy(gsl.at[pl.ds(0, nd - 1)], gsl.at[pl.ds(0, nd - 1)], arecv).wait()
        pltpu.make_async_copy(sea, sea, srecv).wait()
        pltpu.make_async_copy(w_hbm, wbuf, w_sem).wait()
        sea_table = doubled(sea, 0)
        total = jnp.zeros((tiles * SUB, LANES), F32)

        def dense(p, src):
            w = wbuf[p]
            wh = w.astype(BF16)
            wl = (w - wh.astype(F32)).astype(BF16)
            index = rows[pl.ds(p, 1), :]
            x = split_rows([gsl[src, i] for i in range(block // (2 * LANES))]).astype(BF16)
            v = split_rows(gather_slot(sea_table, index)).astype(BF16)
            dims = (((1,), (1,)), ((), ()))
            y = (lax.dot_general(x, wh, dims, preferred_element_type=F32)
                 + lax.dot_general(x, wl, dims, preferred_element_type=F32))
            z = jnp.dot(v, wh, preferred_element_type=F32) + jnp.dot(v, wl, preferred_element_type=F32)
            y = y[:FIELDS] + y[FIELDS:]
            z = z[:FIELDS] + z[FIELDS:]
            yh = y.astype(BF16).astype(F32)
            return jnp.concatenate([yh, y - yh], axis=0), z, index

        def put(ref, at, z):
            for q in range(block // LANES):
                ref[at, q // 2, pl.ds((q % 2) * FIELDS, FIELDS), :] = z[:, q * LANES:(q + 1) * LANES]

        def u_copy(slot, r):
            return pltpu.make_async_remote_copy(
                src_ref=zslots.at[slot], dst_ref=usl.at[dom], send_sem=usend, recv_sem=urecv,
                device_id=(comp, lax.rem(dom + r, nd)), device_id_type=MESH)

        eight, z, index = dense(tab[0, T_EP], tab[0, T_ESRC])
        put(zslots, NEAR_COUNT, z)

        def send(r, _):
            u_copy(NEAR_COUNT, r).start()
            return 0
        lax.fori_loop(NEAR + 1, nd - NEAR, send, 0)
        total = total + scatter(jnp.where(tab[0, T_EVALID] == 1, eight, 0.0), index)
        for n, r in enumerate(near_rel):
            eight, z, index = dense(tab[0, T_NEARP + n], lax.rem(dom + r, nd))
            if r == 0:
                put(usl, dom, z)
            else:
                put(zslots, n, z)
                u_copy(n, r).start()
            total = total + scatter(eight, index)
        for h in range(tiles):
            part = total[h * SUB:(h + 1) * SUB]
            fpart[h] = part + pltpu.roll(part, FIELDS, axis=0)
        pltpu.make_async_remote_copy(
            src_ref=fpart, dst_ref=fgot.at[comp], send_sem=fsend, recv_sem=frecv,
            device_id=(ocean, dom), device_id_type=MESH).start()

    flag_next(1)
    bulk_step(1)
    flag_next(2)

    @pl.when(is_air)
    def _():
        pltpu.make_async_copy(usl.at[pl.ds(0, nd - 1)], usl.at[pl.ds(0, nd - 1)], urecv).wait()
        total = jnp.zeros((tiles * SUB, LANES), F32)
        for r in near_rel:
            t = lax.rem(dom + r, nd)
            total = total + scatter(split_rows([usl[t, i] for i in range(block // (2 * LANES))]), cols_of(t))
        for e in range(EXTRAS):
            t = tab[0, T_EXT + e]
            eight = split_rows([usl[t, i] for i in range(block // (2 * LANES))])
            total = total + scatter(jnp.where(tab[0, T_VALID + e] == 1, eight, 0.0), cols_of(t))
        for h in range(tiles):
            part = total[h * SUB:(h + 1) * SUB]
            force[h] = part + pltpu.roll(part, FIELDS, axis=0)

    @pl.when(jnp.logical_not(is_air))
    def _():
        pltpu.make_async_copy(fgot, fgot, frecv).wait()
        for h in range(tiles):
            force[h] = fgot[0, h] + fgot[1, h] + fgot[2, h]

    group_step(0)
    flag_next(3)
    bulk_step(2)
    group_step(1)
    flag_next(4)
    bulk_step(3)

    def store_b(j):
        return pltpu.make_async_copy(outb.at[j], out_hbm.at[pl.ds(SUB, bulk), pl.ds(j * LANES, LANES)], out_sem.at[1])

    def store_g(j):
        return pltpu.make_async_copy(outg.at[j], out_hbm.at[pl.ds(0, SUB), pl.ds(j * LANES, LANES)], out_sem.at[0])

    for j in range(tiles):
        store_b(j).start()
    for i in range(5, len(hops) - 1):
        flag_next(i)
    group_step(2)
    flag_next(len(hops) - 1)
    flag_out[...] = flags[len(hops)]
    group_step(3)
    for j in range(tiles):
        store_g(j).start()

    @pl.when(is_air)
    def _():
        pltpu.make_async_copy(slots.at[pl.ds(0, nd - 1)], slots.at[pl.ds(0, nd - 1)], asend).wait()
        pltpu.make_async_copy(slots.at[pl.ds(0, nd - 1)], slots.at[pl.ds(0, nd - 1)], usend).wait()
        pltpu.make_async_copy(fpart, fpart, fsend).wait()

    @pl.when(jnp.logical_not(is_air))
    def _():
        pltpu.make_async_copy(fgot, fgot, ssend).wait()

    pltpu.make_async_copy(outb, outb, out_sem.at[1]).wait()
    pltpu.make_async_copy(outg, outg, out_sem.at[0]).wait()


def windowed(state, neighbors, edge_coef, sea_mask, pair_rows, pair_cols, remap_weight, pair_source):
    nd, nc = lax.axis_size("dom"), lax.axis_size("comp")
    _, levels, columns = state.shape
    tiles = columns // LANES
    padded = tiles + 2 * RIM // LANES
    pairs, block = pair_rows.shape[1:]
    pieces = block // (2 * LANES)
    bulk = levels - SUB
    hops = (nd - 1).bit_length() + (nc - 1).bit_length()
    vmem = pl.BlockSpec(memory_space=pltpu.VMEM)
    hbm = pl.BlockSpec(memory_space=pl.ANY)
    dma = pltpu.SemaphoreType.DMA
    scratch = (
        [pltpu.VMEM((padded, bulk, LANES), F32)] * STEPS
        + [pltpu.VMEM((padded, SUB, LANES), F32)] * STEPS
        + [pltpu.VMEM((tiles, bulk, LANES), F32), pltpu.VMEM((tiles, SUB, LANES), F32)]
        + [
            pltpu.VMEM(pair_cols.shape, jnp.int32),
            pltpu.VMEM((pairs, block, block), F32),
            pltpu.VMEM((EXTRAS, pieces, SUB, LANES), F32),
            pltpu.VMEM((nd, pieces, SUB, LANES), F32),
            pltpu.VMEM((nd, pieces, SUB, LANES), F32),
            pltpu.VMEM((NEAR_COUNT + 1, pieces, SUB, LANES), F32),
            pltpu.VMEM((nd, pieces, SUB, LANES), F32),
            pltpu.VMEM((tiles, SUB, LANES), F32),
            pltpu.VMEM((tiles, SUB, LANES), F32),
            pltpu.VMEM((nc - 1, tiles, SUB, LANES), F32),
            pltpu.VMEM((tiles, SUB, LANES), F32),
        ]
        + [pltpu.VMEM((nd + EDGES * tiles, LANES), jnp.int32), pltpu.SMEM((nd + EDGES * tiles, LANES), jnp.int32)]
        + [pltpu.VMEM((hops + 1, SUB, LANES), F32), pltpu.VMEM((hops, SUB, LANES), F32), dma, dma((hops,)), dma((hops,))]
        + [dma((2,)), dma, dma, dma((2,))]
        + [dma((2, STEPS, 2)), dma((2, STEPS, 2))]
        + [dma] * 8
    )
    return pl.pallas_call(
        functools.partial(interval_kernel, nd, nc, tiles, levels, block, pairs),
        out_shape=[jax.ShapeDtypeStruct((levels, columns), F32), jax.ShapeDtypeStruct((SUB, LANES), F32)],
        in_specs=[vmem] * 5 + [hbm] * 3,
        out_specs=[hbm, vmem],
        scratch_shapes=scratch,
        name="interval",
        cost_estimate=pl.CostEstimate(flops=10**9, bytes_accessed=10**8, transcendentals=0),
        compiler_params=pltpu.CompilerParams(
            collective_id=0, has_side_effects=True, vmem_limit_bytes=60 * 2**20),
    )(neighbors[0], edge_coef[0], sea_mask[None], pair_rows[0], pair_source, state[0], pair_cols, remap_weight[0])


def local(state, neighbors, edge_coef, sea_mask, pair_source, pair_rows, pair_cols, remap_weight):
    fast, flags = windowed(state, neighbors, edge_coef, sea_mask, pair_rows, pair_cols, remap_weight, pair_source)
    args = (state, neighbors, edge_coef, sea_mask, pair_source, pair_rows, pair_cols, remap_weight)
    done = lax.while_loop(lambda c: c[0], lambda c: (False, general(*args)), (flags[0, 0] > 0, fast))
    return done[1][None]


def solution(mesh):
    placed = (
        P("comp", None, "dom"),
        P("comp", None, "dom"),
        P("comp", None, "dom"),
        P("dom"),
        P(),
        P("dom", None, None),
        P(),
        P("dom", None, None, None),
    )
    return jax.shard_map(
        local, mesh=mesh, in_specs=placed, out_specs=P("comp", None, "dom"), check_vma=False
    )
```

```python
import functools

import jax
import jax.numpy as jnp
from jax import lax
from jax.experimental import pallas as pl
from jax.experimental.layout import Layout, with_layout_constraint
from jax.experimental.pallas import tpu as pltpu
from jax.sharding import PartitionSpec as P

FIELDS = 4
RIM = 256
EDGES = 4
STEPS = 4
FORCE_GAIN = 0.5

LANES = 128
SUB = 8
NEAR = 2
NEAR_COUNT = 2 * NEAR + 1
EXTRAS = 4
MESH = pl.DeviceIdType.MESH
F32 = jnp.float32
BF16 = jnp.bfloat16


def with_halo(array, sides, width):
    for axis, dim in sides:
        devices, length = (lax.axis_size(axis), array.shape[dim])
        up = [(i, (i + 1) % devices) for i in range(devices)]
        down = [(j, i) for i, j in up]
        last = lax.slice_in_dim(array, length - width, length, axis=dim)
        leading = lax.slice_in_dim(array, 0, width, axis=dim)
        before = lax.ppermute(last, axis, up)
        after = lax.ppermute(leading, axis, down)
        array = jnp.concatenate([before, array, after], axis=dim)
    return array


def general(state, neighbors, edge_coef, sea_mask, pair_source, pair_rows, pair_cols, remap_weight):
    highest = lax.Precision.HIGHEST
    comp_count = lax.axis_size("comp")
    dom_count = lax.axis_size("dom")
    comp_id = lax.axis_index("comp")
    dom_id = lax.axis_index("dom")
    current = with_layout_constraint(state, Layout((0, 1, 2)))[0]
    fields = FIELDS
    column_count = current.shape[1]
    pair_count = pair_source.shape[1]
    block = pair_rows.shape[2]
    device_total = comp_count * dom_count
    is_ocean = comp_id == comp_count - 1
    myself = comp_id * dom_count + dom_id
    surface = current[:fields]
    pair_index = jnp.arange(pair_count, dtype=jnp.int32)
    matched = pair_source == myself
    partner = jnp.any(matched, axis=1)
    which_pair = jnp.sum(jnp.where(matched, pair_index[None, :], 0), axis=1)
    my_columns = jnp.sum(jnp.where(matched[:, :, None], pair_cols, 0), axis=1)
    handler_comp = jnp.full_like(which_pair, comp_count - 1)
    activity = jnp.where(is_ocean, 1.0, 0.0).astype(jnp.float32)
    rows_here = pair_rows[0]
    weights_here = remap_weight[0]
    own_sources = lax.dynamic_index_in_dim(pair_source, dom_id, 0, keepdims=False)
    sea_values = surface[:, rows_here]
    upward = jnp.einsum("qbj,fqb->fqj", weights_here, sea_values, precision=highest) * activity
    to_air = jnp.zeros((fields, device_total, block), jnp.float32).at[:, own_sources].add(upward)
    slot_index = handler_comp * dom_count + jnp.arange(dom_count, dtype=jnp.int32)
    air_values = surface[:, my_columns] * partner[None, :, None]
    to_sea = jnp.zeros((fields, device_total, block), jnp.float32).at[:, slot_index].add(air_values)
    got_sea, got_air = (
        lax.all_to_all(to_sea, ("comp", "dom"), split_axis=1, concat_axis=1, tiled=True),
        lax.all_to_all(to_air, ("comp", "dom"), split_axis=1, concat_axis=1, tiled=True),
    )
    incoming = got_sea[:, own_sources]
    downward = jnp.einsum("qbj,fqj->fqb", weights_here, incoming, precision=highest) * activity
    sea_force = jnp.zeros((fields, column_count), jnp.float32).at[:, rows_here].add(downward)
    arrived = got_air[:, slot_index] * partner[None, :, None]
    air_force = jnp.zeros((fields, column_count), jnp.float32).at[:, my_columns].add(arrived)
    forcing = jnp.where(is_ocean, sea_force, air_force)
    adjacency = neighbors[0]
    rates = edge_coef[0]
    evolving = jnp.logical_or(jnp.logical_not(is_ocean), sea_mask == 1)

    def advance(_, current):
        padded = with_halo(current, (("dom", 1),), RIM)
        updated = current
        for edge_number in range(EDGES):
            updated = updated + rates[edge_number] * (padded[:, adjacency[edge_number]] - current)
        updated = updated.at[:fields].add(FORCE_GAIN * (forcing - current[:fields]))
        return jnp.where(evolving[None, :], updated, current)

    return with_layout_constraint(lax.fori_loop(0, STEPS, advance, current), Layout((0, 1)))


def lane_gather(values, lanes):
    return jnp.take_along_axis(values, lanes, axis=1, mode="promise_in_bounds")


def interval_kernel(nd, nc, tiles, levels, block, pairs,
                    nbr, coef, mask, rows, sources, state_hbm, cols_hbm, w_hbm,
                    out_hbm, flag_out,
                    pb0, pb1, pb2, pb3, pg0, pg1, pg2, pg3, outb, outg,
                    cols, wbuf, compact, slots, gsl, zslots, usl, sea, fpart, fgot, force,
                    tabv, tab, flag, pflag, flags_in, tab_sem, gsend, grecv,
                    load_sem, w_sem, cols_sem, out_sem,
                    hsend, hrecv, asend, arecv, usend, urecv, ssend, srecv, fsend, frecv):
    comp = lax.axis_index("comp")
    dom = lax.axis_index("dom")
    ocean = nc - 1
    bulk = levels - SUB
    pieces = block // (2 * LANES)
    halo = RIM // LANES
    pb = [pb0, pb1, pb2, pb3]
    pg = [pg0, pg1, pg2, pg3]
    left = lax.rem(dom + nd - 1, nd)
    right = lax.rem(dom + 1, nd)
    is_air = comp < ocean
    near_rel = [0, 1, 2, nd - 2, nd - 1]
    T_WHICH, T_SEL, T_EXT, T_VALID = 0, 1, 2, 2 + EXTRAS
    T_NEARP = 2 + 2 * EXTRAS
    T_EP = T_NEARP + NEAR_COUNT
    T_EVALID, T_ESRC = T_EP + 1, T_EP + 2

    def load_g(j):
        return pltpu.make_async_copy(state_hbm.at[pl.ds(0, SUB), pl.ds(j * LANES, LANES)], pg0.at[j + halo], load_sem.at[0])

    def load_b(j):
        return pltpu.make_async_copy(state_hbm.at[pl.ds(SUB, bulk), pl.ds(j * LANES, LANES)], pb0.at[j + halo], load_sem.at[1])

    for j in range(tiles):
        load_g(j).start()
    cols_copy = pltpu.make_async_copy(cols_hbm, cols, cols_sem)
    cols_copy.start()
    for j in range(tiles):
        load_b(j).start()

    @pl.when(is_air)
    def _():
        for p in range(pairs):
            pltpu.make_async_copy(w_hbm.at[p], wbuf.at[p], w_sem).start()

    barrier = pltpu.get_barrier_semaphore()

    def greet(device):
        pl.semaphore_signal(barrier, inc=1, device_id=device, device_id_type=MESH)

    for c in range(1, nc):
        greet((lax.rem(comp + c, nc), dom))

    @pl.when(is_air)
    def _():
        def greet_plane(r, _):
            greet((comp, lax.rem(dom + r, nd)))
            return 0
        lax.fori_loop(1, nd, greet_plane, 0)

    @pl.when(jnp.logical_not(is_air))
    def _():
        greet((comp, left))
        greet((comp, right))

    def build_tables():
        src = sources[...]
        p_i = lax.broadcasted_iota(jnp.int32, (nd, pairs), 1)
        t_i = lax.broadcasted_iota(jnp.int32, (nd, pairs), 0)
        t_c = lax.broadcasted_iota(jnp.int32, (nd, 1), 0)
        dom_f = dom
        base = (comp * nd)

        def is_far(offset):
            offset = jnp.where(offset < 0, offset + nd, offset)
            return jnp.logical_and(offset > NEAR, offset < nd - NEAR)

        mine = src == base + dom_f
        which = jnp.sum(jnp.where(mine, p_i, 0), axis=1, keepdims=True)
        hit = jnp.max(jnp.where(mine, 1, 0), axis=1, keepdims=True)
        far = jnp.where(jnp.logical_and(hit > 0, is_far(t_c - dom_f)), 1, 0)
        lanes = [(T_WHICH, which)]
        sel = jnp.zeros((nd, 1), jnp.int32)
        last = jnp.full((1, 1), -1, jnp.int32)
        for e in range(EXTRAS):
            last = jnp.min(jnp.where(jnp.logical_and(far > 0, t_c > last), t_c, nd), axis=0, keepdims=True)
            sel = jnp.where(t_c == last, e, sel)
            lanes.append((T_EXT + e, last))
            lanes.append((T_VALID + e, jnp.where(last < nd, 1, 0)))
        lanes.append((T_SEL, sel))
        crowded = jnp.sum(far, axis=0, keepdims=True) > EXTRAS

        own = jnp.sum(jnp.where(t_i == dom_f, src, 0), axis=0, keepdims=True) - base
        p_r = p_i[:1]
        for n, r in enumerate(near_rel):
            place = lax.rem(dom + r, nd)
            lanes.append((T_NEARP + n, jnp.sum(jnp.where(own == place, p_r, 0), axis=1, keepdims=True)))
        in_band = jnp.logical_and(own >= 0, own < nd)
        far_own = jnp.where(jnp.logical_and(in_band, is_far(own - dom_f)), 1, 0)
        lanes.append((T_EP, jnp.sum(far_own * p_r, axis=1, keepdims=True)))
        lanes.append((T_EVALID, jnp.max(far_own, axis=1, keepdims=True)))
        lanes.append((T_ESRC, jnp.sum(far_own * own, axis=1, keepdims=True)))
        lane = lax.broadcasted_iota(jnp.int32, (nd, LANES), 1)
        packed = jnp.zeros((nd, LANES), jnp.int32)
        for at, value in lanes:
            value = jnp.minimum(value, ((nd if at in (T_ESRC, *range(T_EXT, T_EXT + EXTRAS)) else pairs) - 1))
            packed = jnp.where(lane == at, jnp.broadcast_to(value, (nd, LANES)), packed)
        tabv[pl.ds(0, nd), :] = packed

        reach = jnp.concatenate(
            [nbr[:, j * LANES:(j + 1) * LANES] for j in range(tiles)], axis=0)
        lane = lax.broadcasted_iota(jnp.int32, reach.shape, 1)
        wide = jnp.zeros((1, 1), jnp.int32)
        packed = jnp.zeros(reach.shape, jnp.int32)
        for h, side in enumerate((lane < LANES // 2, lane >= LANES // 2)):
            first = jnp.min(jnp.where(side, reach, 2**30), axis=1, keepdims=True)
            first = jnp.clip(first, 0, ((tiles + 2 * halo - 1) * LANES))
            final = jnp.max(jnp.where(side, reach, -1), axis=1, keepdims=True)
            wide = jnp.maximum(wide, jnp.max(final - first, axis=0, keepdims=True))
            packed = jnp.where(lane == h, jnp.broadcast_to(first, reach.shape), packed)
        tabv[pl.ds(nd, EDGES * tiles), :] = packed
        bad = jnp.logical_or(wide >= LANES, crowded)
        mark = jnp.broadcast_to(jnp.where(bad, 1.0, 0.0), (SUB, LANES))
        flag[...] = mark

    build_tables()
    to_smem = pltpu.make_async_copy(tabv, tab, tab_sem)
    to_smem.start()

    row8 = lax.broadcasted_iota(jnp.int32, (SUB, LANES), 0)

    def doubled(ref, offset):
        out = []
        for h in range(tiles):
            v = ref[h + offset]
            out.append(jnp.where(row8 < FIELDS, v, pltpu.roll(v, FIELDS, axis=0)))
        return out

    def gather_slot(table, index):
        res = []
        for q in range(0, block // LANES, 2):
            i0 = index[:, q * LANES:(q + 1) * LANES]
            i1 = index[:, (q + 1) * LANES:(q + 2) * LANES]
            i8 = jnp.where(row8 < FIELDS, jnp.broadcast_to(i0, (SUB, LANES)), jnp.broadcast_to(i1, (SUB, LANES)))
            lo = i8 & (LANES - 1)
            hi = i8 >> 7
            acc = lane_gather(table[0], lo)
            for h in range(1, tiles):
                acc = jnp.where(hi == h, lane_gather(table[h], lo), acc)
            res.append(acc)
        return res

    def split_rows(res):
        cols_ = []
        for acc in res:
            high = acc.astype(BF16).astype(F32)
            low = acc - high
            cols_.append(jnp.where(row8 < FIELDS, high, pltpu.roll(low, FIELDS, axis=0)))
            cols_.append(jnp.where(row8 < FIELDS, pltpu.roll(high, FIELDS, axis=0), low))
        return jnp.concatenate(cols_, axis=1)

    def scatter(eight, index):
        hi = jnp.broadcast_to(index >> 7, (SUB, block))
        lhs = jnp.concatenate([jnp.where(hi == h, eight, 0.0) for h in range(tiles)], axis=0).astype(BF16)
        lo = jnp.broadcast_to(index & (LANES - 1), (LANES, block))
        hot = jnp.where(lo == lax.broadcasted_iota(jnp.int32, (LANES, block), 0), 1.0, 0.0).astype(BF16)
        return lax.dot_general(lhs, hot, (((1,), (1,)), ((), ())), preferred_element_type=F32)

    def cols_of(t):
        return cols[t, pl.ds(tab[t, T_WHICH], 1), :]

    pltpu.make_async_copy(pg0.at[pl.ds(halo, tiles)], pg0.at[pl.ds(halo, tiles)], load_sem.at[0]).wait()
    cols_copy.wait()
    to_smem.wait()

    @pl.when(is_air)
    def _():
        table = doubled(pg0, halo)
        for n, r in enumerate(near_rel):
            t = lax.rem(dom + r, nd)
            res = gather_slot(table, cols_of(t))
            for i, acc in enumerate(res):
                if r == 0:
                    gsl[dom, i] = acc
                else:
                    slots[r, i] = acc

        def extra(e, _):
            res = gather_slot(table, cols_of(tab[0, T_EXT + e]))
            for i, acc in enumerate(res):
                compact[e, i] = acc
            return 0
        lax.fori_loop(0, EXTRAS, extra, 0)

        def fill(r, _):
            t = lax.rem(dom + r, nd)
            slots[r] = compact[tab[t, T_SEL]]
            return 0
        lax.fori_loop(NEAR + 1, nd - NEAR, fill, 0)

    @pl.when(is_air)
    def _():
        pl.semaphore_wait(barrier, nd + nc - 2)

    @pl.when(jnp.logical_not(is_air))
    def _():
        pl.semaphore_wait(barrier, nc + 1)

    def a_copy(r):
        return pltpu.make_async_remote_copy(
            src_ref=slots.at[r], dst_ref=gsl.at[dom], send_sem=asend, recv_sem=arecv,
            device_id=(comp, lax.rem(dom + r, nd)), device_id_type=MESH)

    def halo_copies(ref, s, kind):
        to_left = pltpu.make_async_remote_copy(
            src_ref=ref.at[pl.ds(halo, halo)], dst_ref=ref.at[pl.ds(tiles + halo, halo)],
            send_sem=hsend.at[kind, s, 0], recv_sem=hrecv.at[kind, s, 0], device_id=(comp, left), device_id_type=MESH)
        to_right = pltpu.make_async_remote_copy(
            src_ref=ref.at[pl.ds(tiles, halo)], dst_ref=ref.at[pl.ds(0, halo)],
            send_sem=hsend.at[kind, s, 1], recv_sem=hrecv.at[kind, s, 1], device_id=(comp, right), device_id_type=MESH)
        return to_left, to_right

    def sea_copy(c):
        return pltpu.make_async_remote_copy(
            src_ref=pg0.at[pl.ds(halo, tiles)], dst_ref=sea, send_sem=ssend, recv_sem=srecv,
            device_id=(c, dom), device_id_type=MESH)

    def sea_flag_copy(c):
        return pltpu.make_async_remote_copy(
            src_ref=flag, dst_ref=flags_in.at[ocean], send_sem=gsend.at[0], recv_sem=grecv.at[0],
            device_id=(c, dom), device_id_type=MESH)

    def plane_flag_copy(c):
        return pltpu.make_async_remote_copy(
            src_ref=pflag, dst_ref=flags_in.at[comp], send_sem=gsend.at[1], recv_sem=grecv.at[1],
            device_id=(lax.rem(comp + c, nc), dom), device_id_type=MESH)

    def arrived(ref, sem):
        pltpu.make_async_copy(ref, ref, sem).wait()

    @pl.when(jnp.logical_not(is_air))
    def _():
        for c in range(ocean):
            sea_copy(c).start()
        for c in range(ocean):
            sea_flag_copy(c).start()

    @pl.when(is_air)
    def _():
        for r in near_rel[1:]:
            a_copy(r).start()

        def send(r, _):
            a_copy(r).start()
            return 0
        lax.fori_loop(NEAR + 1, nd - NEAR, send, 0)

    for c in halo_copies(pg[0], 0, 0):
        c.start()
    arrived(pb0.at[pl.ds(halo, tiles)], load_sem.at[1])
    for c in halo_copies(pb[0], 0, 1):
        c.start()

    lane1 = lax.broadcasted_iota(jnp.int32, (1, LANES), 1)

    def tile_step(src, j, rows_, forced):
        cols_j = pl.ds(pl.multiple_of(j * LANES, LANES), LANES)
        cur = src[j + halo]
        upd = cur
        low = jnp.broadcast_to(lane1 < LANES // 2, (rows_, LANES))
        for k in range(EDGES):
            lo = jnp.broadcast_to(nbr[pl.ds(k, 1), cols_j] & (LANES - 1), (rows_, LANES))
            got = []
            for h in range(2):
                w = tab[nd + j * EDGES + k, h]
                b = jnp.minimum(w >> 7, tiles + 2 * halo - 2)
                edge = jnp.broadcast_to(lane1 >= w - b * LANES, (rows_, LANES))
                got.append(lane_gather(jnp.where(edge, src[b], src[b + 1]), lo))
            upd = upd + coef[pl.ds(k, 1), cols_j] * (jnp.where(low, got[0], got[1]) - cur)
        if forced:
            gain = jnp.where(row8 < FIELDS, FORCE_GAIN, 0.0)
            upd = upd + gain * (force[j] - cur)
        keep = jnp.logical_or(is_air, mask[:, cols_j] == 1)
        return jnp.where(jnp.broadcast_to(keep, (rows_, LANES)), upd, cur)

    def bulk_step(s):
        src = pb[s]
        dst, off = (pb[s + 1], halo) if s + 1 < STEPS else (outb, 0)
        per = 4

        def body(i, _):
            new = [tile_step(src, i * per + u, bulk, False) for u in range(per)]
            for u in range(per):
                dst[i * per + u + off] = new[u]
            return 0
        for c in halo_copies(src, s, 1):
            c.wait()
        lax.fori_loop(0, tiles // per, body, 0)
        if s + 1 < STEPS:
            for c in halo_copies(pb[s + 1], s + 1, 1):
                c.start()

    def group_step(s):
        src = pg[s]
        dst, off = (pg[s + 1], halo) if s + 1 < STEPS else (outg, 0)
        for c in halo_copies(src, s, 0):
            c.wait()
        new = [tile_step(src, j, SUB, True) for j in range(tiles)]
        for j in range(tiles):
            dst[j + off] = new[j]
        if s + 1 < STEPS:
            for c in halo_copies(pg[s + 1], s + 1, 0):
                c.start()

    @pl.when(is_air)
    def _():
        pltpu.make_async_copy(gsl.at[pl.ds(0, nd - 1)], gsl.at[pl.ds(0, nd - 1)], arecv).wait()
        pltpu.make_async_copy(sea, sea, srecv).wait()
        pltpu.make_async_copy(w_hbm, wbuf, w_sem).wait()
        arrived(flag, grecv.at[0])
        flag[...] = jnp.maximum(flag[...], flags_in[ocean])
        for n in range(1, NEAR_COUNT + 1):
            zslots[n, pieces] = flag[...]
        usl[dom, pieces] = flag[...]
        sea_table = doubled(sea, 0)
        total = jnp.zeros((tiles * SUB, LANES), F32)

        def dense(p, src):
            w = wbuf[p]
            wh = w.astype(BF16)
            wl = (w - wh.astype(F32)).astype(BF16)
            index = rows[pl.ds(p, 1), :]
            x = split_rows([gsl[src, i] for i in range(pieces)]).astype(BF16)
            v = split_rows(gather_slot(sea_table, index)).astype(BF16)
            dims = (((1,), (1,)), ((), ()))
            y = (lax.dot_general(x, wh, dims, preferred_element_type=F32)
                 + lax.dot_general(x, wl, dims, preferred_element_type=F32))
            z = jnp.dot(v, wh, preferred_element_type=F32) + jnp.dot(v, wl, preferred_element_type=F32)
            y = y[:FIELDS] + y[FIELDS:]
            z = z[:FIELDS] + z[FIELDS:]
            yh = y.astype(BF16).astype(F32)
            return jnp.concatenate([yh, y - yh], axis=0), z, index

        def put(ref, at, z):
            for q in range(block // LANES):
                ref[at, q // 2, pl.ds((q % 2) * FIELDS, FIELDS), :] = z[:, q * LANES:(q + 1) * LANES]

        def u_copy(slot, r):
            return pltpu.make_async_remote_copy(
                src_ref=zslots.at[slot], dst_ref=usl.at[dom], send_sem=usend, recv_sem=urecv,
                device_id=(comp, lax.rem(dom + r, nd)), device_id_type=MESH)

        eight, z, index = dense(tab[0, T_EP], tab[0, T_ESRC])
        put(zslots, NEAR_COUNT, z)

        def send(r, _):
            u_copy(NEAR_COUNT, r).start()
            return 0
        lax.fori_loop(NEAR + 1, nd - NEAR, send, 0)
        total = total + scatter(jnp.where(tab[0, T_EVALID] == 1, eight, 0.0), index)
        for n, r in enumerate(near_rel):
            eight, z, index = dense(tab[0, T_NEARP + n], lax.rem(dom + r, nd))
            if r == 0:
                put(usl, dom, z)
            else:
                put(zslots, n, z)
                u_copy(n, r).start()
            total = total + scatter(eight, index)
        for h in range(tiles):
            part = total[h * SUB:(h + 1) * SUB]
            fpart[h] = part + pltpu.roll(part, FIELDS, axis=0)
        pltpu.make_async_remote_copy(
            src_ref=fpart, dst_ref=fgot.at[comp], send_sem=fsend, recv_sem=frecv,
            device_id=(ocean, dom), device_id_type=MESH).start()

    bulk_step(0)

    @pl.when(is_air)
    def _():
        pltpu.make_async_copy(usl.at[pl.ds(0, nd - 1)], usl.at[pl.ds(0, nd - 1)], urecv).wait()
        plane = usl[0, pieces]
        for t in range(1, nd):
            plane = jnp.maximum(plane, usl[t, pieces])
        pflag[...] = plane
        total = jnp.zeros((tiles * SUB, LANES), F32)
        for r in near_rel:
            t = lax.rem(dom + r, nd)
            total = total + scatter(split_rows([usl[t, i] for i in range(pieces)]), cols_of(t))
        for e in range(EXTRAS):
            t = tab[0, T_EXT + e]
            eight = split_rows([usl[t, i] for i in range(pieces)])
            total = total + scatter(jnp.where(tab[0, T_VALID + e] == 1, eight, 0.0), cols_of(t))
        for h in range(tiles):
            part = total[h * SUB:(h + 1) * SUB]
            force[h] = part + pltpu.roll(part, FIELDS, axis=0)

    @pl.when(jnp.logical_not(is_air))
    def _():
        pltpu.make_async_copy(fgot, fgot, frecv).wait()
        for h in range(tiles):
            force[h] = fgot[0, h] + fgot[1, h] + fgot[2, h]

    group_step(0)

    @pl.when(is_air)
    def _():
        for c in range(1, nc):
            plane_flag_copy(c).start()

    bulk_step(1)
    group_step(1)
    bulk_step(2)
    group_step(2)
    bulk_step(3)

    def store_b(j):
        return pltpu.make_async_copy(outb.at[j], out_hbm.at[pl.ds(SUB, bulk), pl.ds(j * LANES, LANES)], out_sem.at[1])

    def store_g(j):
        return pltpu.make_async_copy(outg.at[j], out_hbm.at[pl.ds(0, SUB), pl.ds(j * LANES, LANES)], out_sem.at[0])

    for j in range(tiles):
        store_b(j).start()
    group_step(3)
    for j in range(tiles):
        store_g(j).start()

    @pl.when(is_air)
    def _():
        arrived(flags_in.at[pl.ds(0, ocean - 1)], grecv.at[1])
        total = pflag[...]
        for c in range(ocean):
            total = jnp.maximum(total, jnp.where(comp == c, 0.0, flags_in[c]))
        flag_out[...] = total

    @pl.when(jnp.logical_not(is_air))
    def _():
        arrived(flags_in.at[pl.ds(0, ocean)], grecv.at[1])
        total = flags_in[0]
        for c in range(1, ocean):
            total = jnp.maximum(total, flags_in[c])
        flag_out[...] = total

    @pl.when(is_air)
    def _():
        pltpu.make_async_copy(slots.at[pl.ds(0, nd - 1)], slots.at[pl.ds(0, nd - 1)], asend).wait()
        arrived(usl.at[pl.ds(0, nd - 1)], usend)
        arrived(fpart, fsend)
        arrived(flags_in.at[pl.ds(0, ocean)], gsend.at[1])

    @pl.when(jnp.logical_not(is_air))
    def _():
        arrived(fgot, ssend)
        arrived(flags_in.at[pl.ds(0, ocean)], gsend.at[0])

    pltpu.make_async_copy(outb, outb, out_sem.at[1]).wait()
    pltpu.make_async_copy(outg, outg, out_sem.at[0]).wait()


def windowed(state, neighbors, edge_coef, sea_mask, pair_rows, pair_cols, remap_weight, pair_source):
    nd, nc = lax.axis_size("dom"), lax.axis_size("comp")
    _, levels, columns = state.shape
    tiles = columns // LANES
    padded = tiles + 2 * RIM // LANES
    pairs, block = pair_rows.shape[1:]
    pieces = block // (2 * LANES)
    bulk = levels - SUB
    vmem = pl.BlockSpec(memory_space=pltpu.VMEM)
    hbm = pl.BlockSpec(memory_space=pl.ANY)
    dma = pltpu.SemaphoreType.DMA
    scratch = (
        [pltpu.VMEM((padded, bulk, LANES), F32)] * STEPS
        + [pltpu.VMEM((padded, SUB, LANES), F32)] * STEPS
        + [pltpu.VMEM((tiles, bulk, LANES), F32), pltpu.VMEM((tiles, SUB, LANES), F32)]
        + [
            pltpu.VMEM(pair_cols.shape, jnp.int32),
            pltpu.VMEM((pairs, block, block), F32),
            pltpu.VMEM((EXTRAS, pieces, SUB, LANES), F32),
            pltpu.VMEM((nd, pieces, SUB, LANES), F32),
            pltpu.VMEM((nd, pieces, SUB, LANES), F32),
            pltpu.VMEM((NEAR_COUNT + 1, pieces + 1, SUB, LANES), F32),
            pltpu.VMEM((nd, pieces + 1, SUB, LANES), F32),
            pltpu.VMEM((tiles, SUB, LANES), F32),
            pltpu.VMEM((tiles, SUB, LANES), F32),
            pltpu.VMEM((nc - 1, tiles, SUB, LANES), F32),
            pltpu.VMEM((tiles, SUB, LANES), F32),
        ]
        + [pltpu.VMEM((nd + EDGES * tiles, LANES), jnp.int32), pltpu.SMEM((nd + EDGES * tiles, LANES), jnp.int32)]
        + [pltpu.VMEM((SUB, LANES), F32)] * 2 + [pltpu.VMEM((nc, SUB, LANES), F32), dma, dma((2,)), dma((2,))]
        + [dma((2,)), dma, dma, dma((2,))]
        + [dma((2, STEPS, 2)), dma((2, STEPS, 2))]
        + [dma] * 8
    )
    return pl.pallas_call(
        functools.partial(interval_kernel, nd, nc, tiles, levels, block, pairs),
        out_shape=[jax.ShapeDtypeStruct((levels, columns), F32), jax.ShapeDtypeStruct((SUB, LANES), F32)],
        in_specs=[vmem] * 5 + [hbm] * 3,
        out_specs=[hbm, vmem],
        scratch_shapes=scratch,
        name="interval",
        cost_estimate=pl.CostEstimate(flops=10**9, bytes_accessed=10**8, transcendentals=0),
        compiler_params=pltpu.CompilerParams(
            collective_id=0, has_side_effects=True, vmem_limit_bytes=60 * 2**20),
    )(neighbors[0], edge_coef[0], sea_mask[None], pair_rows[0], pair_source, state[0], pair_cols, remap_weight[0])


def local(state, neighbors, edge_coef, sea_mask, pair_source, pair_rows, pair_cols, remap_weight):
    fast, flags = windowed(state, neighbors, edge_coef, sea_mask, pair_rows, pair_cols, remap_weight, pair_source)
    args = (state, neighbors, edge_coef, sea_mask, pair_source, pair_rows, pair_cols, remap_weight)
    done = lax.while_loop(lambda c: c[0], lambda c: (False, general(*args)), (flags[0, 0] > 0, fast))
    return done[1][None]


def solution(mesh):
    placed = (
        P("comp", None, "dom"),
        P("comp", None, "dom"),
        P("comp", None, "dom"),
        P("dom"),
        P(),
        P("dom", None, None),
        P(),
        P("dom", None, None, None),
    )
    return jax.shard_map(
        local, mesh=mesh, in_specs=placed, out_specs=P("comp", None, "dom"), check_vma=False
    )
```

```python
import functools

import jax
import jax.numpy as jnp
from jax import lax
from jax.experimental import pallas as pl
from jax.experimental.layout import Layout, with_layout_constraint
from jax.experimental.pallas import tpu as pltpu
from jax.sharding import PartitionSpec as P

FIELDS = 4
RIM = 256
EDGES = 4
STEPS = 4
FORCE_GAIN = 0.5

LANES = 128
SUB = 8
NEAR = 2
NEAR_COUNT = 2 * NEAR + 1
EXTRAS = 4
MESH = pl.DeviceIdType.MESH
F32 = jnp.float32
BF16 = jnp.bfloat16


def with_halo(array, sides, width):
    for axis, dim in sides:
        devices, length = (lax.axis_size(axis), array.shape[dim])
        up = [(i, (i + 1) % devices) for i in range(devices)]
        down = [(j, i) for i, j in up]
        last = lax.slice_in_dim(array, length - width, length, axis=dim)
        leading = lax.slice_in_dim(array, 0, width, axis=dim)
        before = lax.ppermute(last, axis, up)
        after = lax.ppermute(leading, axis, down)
        array = jnp.concatenate([before, array, after], axis=dim)
    return array


def general(state, neighbors, edge_coef, sea_mask, pair_source, pair_rows, pair_cols, remap_weight):
    highest = lax.Precision.HIGHEST
    comp_count = lax.axis_size("comp")
    dom_count = lax.axis_size("dom")
    comp_id = lax.axis_index("comp")
    dom_id = lax.axis_index("dom")
    current = with_layout_constraint(state, Layout((0, 1, 2)))[0]
    fields = FIELDS
    column_count = current.shape[1]
    pair_count = pair_source.shape[1]
    block = pair_rows.shape[2]
    device_total = comp_count * dom_count
    is_ocean = comp_id == comp_count - 1
    myself = comp_id * dom_count + dom_id
    surface = current[:fields]
    pair_index = jnp.arange(pair_count, dtype=jnp.int32)
    matched = pair_source == myself
    partner = jnp.any(matched, axis=1)
    which_pair = jnp.sum(jnp.where(matched, pair_index[None, :], 0), axis=1)
    my_columns = jnp.sum(jnp.where(matched[:, :, None], pair_cols, 0), axis=1)
    handler_comp = jnp.full_like(which_pair, comp_count - 1)
    activity = jnp.where(is_ocean, 1.0, 0.0).astype(jnp.float32)
    rows_here = pair_rows[0]
    weights_here = remap_weight[0]
    own_sources = lax.dynamic_index_in_dim(pair_source, dom_id, 0, keepdims=False)
    sea_values = surface[:, rows_here]
    upward = jnp.einsum("qbj,fqb->fqj", weights_here, sea_values, precision=highest) * activity
    to_air = jnp.zeros((fields, device_total, block), jnp.float32).at[:, own_sources].add(upward)
    slot_index = handler_comp * dom_count + jnp.arange(dom_count, dtype=jnp.int32)
    air_values = surface[:, my_columns] * partner[None, :, None]
    to_sea = jnp.zeros((fields, device_total, block), jnp.float32).at[:, slot_index].add(air_values)
    got_sea, got_air = (
        lax.all_to_all(to_sea, ("comp", "dom"), split_axis=1, concat_axis=1, tiled=True),
        lax.all_to_all(to_air, ("comp", "dom"), split_axis=1, concat_axis=1, tiled=True),
    )
    incoming = got_sea[:, own_sources]
    downward = jnp.einsum("qbj,fqj->fqb", weights_here, incoming, precision=highest) * activity
    sea_force = jnp.zeros((fields, column_count), jnp.float32).at[:, rows_here].add(downward)
    arrived = got_air[:, slot_index] * partner[None, :, None]
    air_force = jnp.zeros((fields, column_count), jnp.float32).at[:, my_columns].add(arrived)
    forcing = jnp.where(is_ocean, sea_force, air_force)
    adjacency = neighbors[0]
    rates = edge_coef[0]
    evolving = jnp.logical_or(jnp.logical_not(is_ocean), sea_mask == 1)

    def advance(_, current):
        padded = with_halo(current, (("dom", 1),), RIM)
        updated = current
        for edge_number in range(EDGES):
            updated = updated + rates[edge_number] * (padded[:, adjacency[edge_number]] - current)
        updated = updated.at[:fields].add(FORCE_GAIN * (forcing - current[:fields]))
        return jnp.where(evolving[None, :], updated, current)

    return with_layout_constraint(lax.fori_loop(0, STEPS, advance, current), Layout((0, 1)))


def lane_gather(values, lanes):
    return jnp.take_along_axis(values, lanes, axis=1, mode="promise_in_bounds")


def interval_kernel(nd, nc, tiles, levels, block, pairs,
                    nbr, coef, mask, rows, sources, state_hbm, cols_hbm, w_hbm,
                    out, flag_out,
                    pb0, pb1, pb2, pb3, pg0, pg1, pg2, pg3,
                    cols, wbuf, compact, slots, gsl, zslots, usl, sea, fpart, fgot, force,
                    tabv, tab, flag, pflag, flags_in, tab_sem, gsend, grecv,
                    load_sem, w_sem, cols_sem,
                    hsend, hrecv, asend, arecv, usend, urecv, ssend, srecv, fsend, frecv):
    comp = lax.axis_index("comp")
    dom = lax.axis_index("dom")
    ocean = nc - 1
    bulk = levels - SUB
    pieces = block // (2 * LANES)
    halo = RIM // LANES
    pb = [pb0, pb1, pb2, pb3]
    pg = [pg0, pg1, pg2, pg3]
    left = lax.rem(dom + nd - 1, nd)
    right = lax.rem(dom + 1, nd)
    is_air = comp < ocean
    near_rel = [0, 1, 2, nd - 2, nd - 1]
    T_WHICH, T_SEL, T_EXT, T_VALID = 0, 1, 2, 2 + EXTRAS
    T_NEARP = 2 + 2 * EXTRAS
    T_EP = T_NEARP + NEAR_COUNT
    T_EVALID, T_ESRC = T_EP + 1, T_EP + 2

    def load_g(j):
        return pltpu.make_async_copy(state_hbm.at[pl.ds(0, SUB), pl.ds(j * LANES, LANES)], pg0.at[j + halo], load_sem.at[0])

    def load_b(j):
        return pltpu.make_async_copy(state_hbm.at[pl.ds(SUB, bulk), pl.ds(j * LANES, LANES)], pb0.at[j + halo], load_sem.at[1])

    for j in range(tiles):
        load_g(j).start()
    cols_copy = pltpu.make_async_copy(cols_hbm, cols, cols_sem)
    cols_copy.start()
    for j in range(tiles):
        load_b(j).start()

    @pl.when(is_air)
    def _():
        for p in range(pairs):
            pltpu.make_async_copy(w_hbm.at[p], wbuf.at[p], w_sem).start()

    barrier = pltpu.get_barrier_semaphore()

    def greet(device):
        pl.semaphore_signal(barrier, inc=1, device_id=device, device_id_type=MESH)

    for c in range(1, nc):
        greet((lax.rem(comp + c, nc), dom))

    @pl.when(is_air)
    def _():
        def greet_plane(r, _):
            greet((comp, lax.rem(dom + r, nd)))
            return 0
        lax.fori_loop(1, nd, greet_plane, 0)

    @pl.when(jnp.logical_not(is_air))
    def _():
        greet((comp, left))
        greet((comp, right))

    def build_tables():
        src = sources[...].T
        p_i = lax.broadcasted_iota(jnp.int32, (nd, pairs), 1)
        t_i = lax.broadcasted_iota(jnp.int32, (nd, pairs), 0)
        t_c = lax.broadcasted_iota(jnp.int32, (nd, 1), 0)
        dom_f = dom
        base = (comp * nd)

        def is_far(offset):
            offset = jnp.where(offset < 0, offset + nd, offset)
            return jnp.logical_and(offset > NEAR, offset < nd - NEAR)

        mine = src == base + dom_f
        which = jnp.sum(jnp.where(mine, p_i, 0), axis=1, keepdims=True)
        hit = jnp.max(jnp.where(mine, 1, 0), axis=1, keepdims=True)
        far = jnp.where(jnp.logical_and(hit > 0, is_far(t_c - dom_f)), 1, 0)
        lanes = [(T_WHICH, which)]
        sel = jnp.zeros((nd, 1), jnp.int32)
        last = jnp.full((1, 1), -1, jnp.int32)
        for e in range(EXTRAS):
            last = jnp.min(jnp.where(jnp.logical_and(far > 0, t_c > last), t_c, nd), axis=0, keepdims=True)
            sel = jnp.where(t_c == last, e, sel)
            lanes.append((T_EXT + e, last))
            lanes.append((T_VALID + e, jnp.where(last < nd, 1, 0)))
        lanes.append((T_SEL, sel))
        crowded = jnp.sum(far, axis=0, keepdims=True) > EXTRAS

        own = jnp.sum(jnp.where(t_i == dom_f, src, 0), axis=0, keepdims=True) - base
        p_r = p_i[:1]
        for n, r in enumerate(near_rel):
            place = lax.rem(dom + r, nd)
            lanes.append((T_NEARP + n, jnp.sum(jnp.where(own == place, p_r, 0), axis=1, keepdims=True)))
        in_band = jnp.logical_and(own >= 0, own < nd)
        far_own = jnp.where(jnp.logical_and(in_band, is_far(own - dom_f)), 1, 0)
        lanes.append((T_EP, jnp.sum(far_own * p_r, axis=1, keepdims=True)))
        lanes.append((T_EVALID, jnp.max(far_own, axis=1, keepdims=True)))
        lanes.append((T_ESRC, jnp.sum(far_own * own, axis=1, keepdims=True)))
        lane = lax.broadcasted_iota(jnp.int32, (nd, LANES), 1)
        packed = jnp.zeros((nd, LANES), jnp.int32)
        for at, value in lanes:
            value = jnp.minimum(value, ((nd if at in (T_ESRC, *range(T_EXT, T_EXT + EXTRAS)) else pairs) - 1))
            packed = jnp.where(lane == at, jnp.broadcast_to(value, (nd, LANES)), packed)
        tabv[pl.ds(0, nd), :] = packed

        reach = jnp.concatenate(
            [nbr[:, j * LANES:(j + 1) * LANES] for j in range(tiles)], axis=0)
        lane = lax.broadcasted_iota(jnp.int32, reach.shape, 1)
        wide = jnp.zeros((1, 1), jnp.int32)
        packed = jnp.zeros(reach.shape, jnp.int32)
        for h, side in enumerate((lane < LANES // 2, lane >= LANES // 2)):
            first = jnp.min(jnp.where(side, reach, 2**30), axis=1, keepdims=True)
            first = jnp.clip(first, 0, ((tiles + 2 * halo - 1) * LANES))
            final = jnp.max(jnp.where(side, reach, -1), axis=1, keepdims=True)
            wide = jnp.maximum(wide, jnp.max(final - first, axis=0, keepdims=True))
            packed = jnp.where(lane == h, jnp.broadcast_to(first, reach.shape), packed)
        tabv[pl.ds(nd, EDGES * tiles), :] = packed
        bad = jnp.logical_or(wide >= LANES, crowded)
        mark = jnp.broadcast_to(jnp.where(bad, 1.0, 0.0), (SUB, LANES))
        flag[...] = mark

    build_tables()
    to_smem = pltpu.make_async_copy(tabv, tab, tab_sem)
    to_smem.start()

    row8 = lax.broadcasted_iota(jnp.int32, (SUB, LANES), 0)

    def doubled(ref, offset):
        out = []
        for h in range(tiles):
            v = ref[h + offset]
            out.append(jnp.where(row8 < FIELDS, v, pltpu.roll(v, FIELDS, axis=0)))
        return out

    def gather_slot(table, index):
        res = []
        for q in range(0, block // LANES, 2):
            i0 = index[:, q * LANES:(q + 1) * LANES]
            i1 = index[:, (q + 1) * LANES:(q + 2) * LANES]
            i8 = jnp.where(row8 < FIELDS, jnp.broadcast_to(i0, (SUB, LANES)), jnp.broadcast_to(i1, (SUB, LANES)))
            lo = i8 & (LANES - 1)
            hi = i8 >> 7
            acc = lane_gather(table[0], lo)
            for h in range(1, tiles):
                acc = jnp.where(hi == h, lane_gather(table[h], lo), acc)
            res.append(acc)
        return res

    def split_rows(res):
        cols_ = []
        for acc in res:
            high = acc.astype(BF16).astype(F32)
            low = acc - high
            cols_.append(jnp.where(row8 < FIELDS, high, pltpu.roll(low, FIELDS, axis=0)))
            cols_.append(jnp.where(row8 < FIELDS, pltpu.roll(high, FIELDS, axis=0), low))
        return jnp.concatenate(cols_, axis=1)

    def scatter(eight, index):
        hi = jnp.broadcast_to(index >> 7, (SUB, block))
        lhs = jnp.concatenate([jnp.where(hi == h, eight, 0.0) for h in range(tiles)], axis=0).astype(BF16)
        lo = jnp.broadcast_to(index & (LANES - 1), (LANES, block))
        hot = jnp.where(lo == lax.broadcasted_iota(jnp.int32, (LANES, block), 0), 1.0, 0.0).astype(BF16)
        return lax.dot_general(lhs, hot, (((1,), (1,)), ((), ())), preferred_element_type=F32)

    def cols_of(t):
        return cols[t, pl.ds(tab[t, T_WHICH], 1), :]

    pltpu.make_async_copy(pg0.at[pl.ds(halo, tiles)], pg0.at[pl.ds(halo, tiles)], load_sem.at[0]).wait()
    cols_copy.wait()
    to_smem.wait()

    @pl.when(is_air)
    def _():
        table = doubled(pg0, halo)
        for n, r in enumerate(near_rel):
            t = lax.rem(dom + r, nd)
            res = gather_slot(table, cols_of(t))
            for i, acc in enumerate(res):
                if r == 0:
                    gsl[dom, i] = acc
                else:
                    slots[r, i] = acc

        def extra(e, _):
            res = gather_slot(table, cols_of(tab[0, T_EXT + e]))
            for i, acc in enumerate(res):
                compact[e, i] = acc
            return 0
        lax.fori_loop(0, EXTRAS, extra, 0)

        def fill(r, _):
            t = lax.rem(dom + r, nd)
            slots[r] = compact[tab[t, T_SEL]]
            return 0
        lax.fori_loop(NEAR + 1, nd - NEAR, fill, 0)

    @pl.when(is_air)
    def _():
        pl.semaphore_wait(barrier, nd + nc - 2)

    @pl.when(jnp.logical_not(is_air))
    def _():
        pl.semaphore_wait(barrier, nc + 1)

    def a_copy(r):
        return pltpu.make_async_remote_copy(
            src_ref=slots.at[r], dst_ref=gsl.at[dom], send_sem=asend, recv_sem=arecv,
            device_id=(comp, lax.rem(dom + r, nd)), device_id_type=MESH)

    def halo_copies(ref, s, kind):
        to_left = pltpu.make_async_remote_copy(
            src_ref=ref.at[pl.ds(halo, halo)], dst_ref=ref.at[pl.ds(tiles + halo, halo)],
            send_sem=hsend.at[kind, s, 0], recv_sem=hrecv.at[kind, s, 0], device_id=(comp, left), device_id_type=MESH)
        to_right = pltpu.make_async_remote_copy(
            src_ref=ref.at[pl.ds(tiles, halo)], dst_ref=ref.at[pl.ds(0, halo)],
            send_sem=hsend.at[kind, s, 1], recv_sem=hrecv.at[kind, s, 1], device_id=(comp, right), device_id_type=MESH)
        return to_left, to_right

    def sea_copy(c):
        return pltpu.make_async_remote_copy(
            src_ref=pg0.at[pl.ds(halo, tiles)], dst_ref=sea, send_sem=ssend, recv_sem=srecv,
            device_id=(c, dom), device_id_type=MESH)

    def sea_flag_copy(c):
        return pltpu.make_async_remote_copy(
            src_ref=flag, dst_ref=flags_in.at[ocean], send_sem=gsend.at[0], recv_sem=grecv.at[0],
            device_id=(c, dom), device_id_type=MESH)

    def plane_flag_copy(c):
        return pltpu.make_async_remote_copy(
            src_ref=pflag, dst_ref=flags_in.at[comp], send_sem=gsend.at[1], recv_sem=grecv.at[1],
            device_id=(lax.rem(comp + c, nc), dom), device_id_type=MESH)

    def arrived(ref, sem):
        pltpu.make_async_copy(ref, ref, sem).wait()

    @pl.when(jnp.logical_not(is_air))
    def _():
        for c in range(ocean):
            sea_copy(c).start()
        for c in range(ocean):
            sea_flag_copy(c).start()

    @pl.when(is_air)
    def _():
        for r in near_rel[1:]:
            a_copy(r).start()

        def send(r, _):
            a_copy(r).start()
            return 0
        lax.fori_loop(NEAR + 1, nd - NEAR, send, 0)

    for c in halo_copies(pg[0], 0, 0):
        c.start()
    arrived(pb0.at[pl.ds(halo, tiles)], load_sem.at[1])
    for c in halo_copies(pb[0], 0, 1):
        c.start()

    lane1 = lax.broadcasted_iota(jnp.int32, (1, LANES), 1)

    def tile_step(src, j, rows_, forced):
        cols_j = pl.ds(pl.multiple_of(j * LANES, LANES), LANES)
        cur = src[j + halo]
        upd = cur
        low = jnp.broadcast_to(lane1 < LANES // 2, (rows_, LANES))
        for k in range(EDGES):
            lo = jnp.broadcast_to(nbr[pl.ds(k, 1), cols_j] & (LANES - 1), (rows_, LANES))
            got = []
            for h in range(2):
                w = tab[nd + j * EDGES + k, h]
                b = jnp.minimum(w >> 7, tiles + 2 * halo - 2)
                edge = jnp.broadcast_to(lane1 >= w - b * LANES, (rows_, LANES))
                got.append(lane_gather(jnp.where(edge, src[b], src[b + 1]), lo))
            upd = upd + coef[pl.ds(k, 1), cols_j] * (jnp.where(low, got[0], got[1]) - cur)
        if forced:
            gain = jnp.where(row8 < FIELDS, FORCE_GAIN, 0.0)
            upd = upd + gain * (force[j] - cur)
        keep = jnp.logical_or(is_air, mask[:, cols_j] == 1)
        return jnp.where(jnp.broadcast_to(keep, (rows_, LANES)), upd, cur)

    def put_tile(bufs, s, j, levels_, value):
        if s + 1 < STEPS:
            bufs[s + 1][j + halo] = value
        else:
            out[levels_, pl.ds(pl.multiple_of(j * LANES, LANES), LANES)] = value

    def bulk_step(s):
        src = pb[s]
        per = 4

        def body(i, _):
            new = [tile_step(src, i * per + u, bulk, False) for u in range(per)]
            for u in range(per):
                put_tile(pb, s, i * per + u, pl.ds(SUB, bulk), new[u])
            return 0
        for c in halo_copies(src, s, 1):
            c.wait()
        lax.fori_loop(0, tiles // per, body, 0)
        if s + 1 < STEPS:
            for c in halo_copies(pb[s + 1], s + 1, 1):
                c.start()

    def group_step(s):
        src = pg[s]
        for c in halo_copies(src, s, 0):
            c.wait()
        new = [tile_step(src, j, SUB, True) for j in range(tiles)]
        for j in range(tiles):
            put_tile(pg, s, j, pl.ds(0, SUB), new[j])
        if s + 1 < STEPS:
            for c in halo_copies(pg[s + 1], s + 1, 0):
                c.start()

    bulk_step(0)

    @pl.when(is_air)
    def _():
        pltpu.make_async_copy(gsl.at[pl.ds(0, nd - 1)], gsl.at[pl.ds(0, nd - 1)], arecv).wait()
        pltpu.make_async_copy(sea, sea, srecv).wait()
        pltpu.make_async_copy(w_hbm, wbuf, w_sem).wait()
        arrived(flag, grecv.at[0])
        flag[...] = jnp.maximum(flag[...], flags_in[ocean])
        for n in range(1, NEAR_COUNT + 1):
            zslots[n, pieces] = flag[...]
        usl[dom, pieces] = flag[...]
        sea_table = doubled(sea, 0)
        total = jnp.zeros((tiles * SUB, LANES), F32)

        def dense(p, src):
            w = wbuf[p]
            wh = w.astype(BF16)
            wl = (w - wh.astype(F32)).astype(BF16)
            index = rows[pl.ds(p, 1), :]
            x = split_rows([gsl[src, i] for i in range(pieces)]).astype(BF16)
            v = split_rows(gather_slot(sea_table, index)).astype(BF16)
            dims = (((1,), (1,)), ((), ()))
            y = (lax.dot_general(x, wh, dims, preferred_element_type=F32)
                 + lax.dot_general(x, wl, dims, preferred_element_type=F32))
            z = jnp.dot(v, wh, preferred_element_type=F32) + jnp.dot(v, wl, preferred_element_type=F32)
            y = y[:FIELDS] + y[FIELDS:]
            z = z[:FIELDS] + z[FIELDS:]
            yh = y.astype(BF16).astype(F32)
            return jnp.concatenate([yh, y - yh], axis=0), z, index

        def put(ref, at, z):
            for q in range(block // LANES):
                ref[at, q // 2, pl.ds((q % 2) * FIELDS, FIELDS), :] = z[:, q * LANES:(q + 1) * LANES]

        def u_copy(slot, r):
            return pltpu.make_async_remote_copy(
                src_ref=zslots.at[slot], dst_ref=usl.at[dom], send_sem=usend, recv_sem=urecv,
                device_id=(comp, lax.rem(dom + r, nd)), device_id_type=MESH)

        eight, z, index = dense(tab[0, T_EP], tab[0, T_ESRC])
        put(zslots, NEAR_COUNT, z)

        def send(r, _):
            u_copy(NEAR_COUNT, r).start()
            return 0
        lax.fori_loop(NEAR + 1, nd - NEAR, send, 0)
        total = total + scatter(jnp.where(tab[0, T_EVALID] == 1, eight, 0.0), index)
        for n, r in enumerate(near_rel):
            eight, z, index = dense(tab[0, T_NEARP + n], lax.rem(dom + r, nd))
            if r == 0:
                put(usl, dom, z)
            else:
                put(zslots, n, z)
                u_copy(n, r).start()
            total = total + scatter(eight, index)
        for h in range(tiles):
            part = total[h * SUB:(h + 1) * SUB]
            fpart[h] = part + pltpu.roll(part, FIELDS, axis=0)
        pltpu.make_async_remote_copy(
            src_ref=fpart, dst_ref=fgot.at[comp], send_sem=fsend, recv_sem=frecv,
            device_id=(ocean, dom), device_id_type=MESH).start()

    bulk_step(1)

    @pl.when(is_air)
    def _():
        pltpu.make_async_copy(usl.at[pl.ds(0, nd - 1)], usl.at[pl.ds(0, nd - 1)], urecv).wait()
        plane = usl[0, pieces]
        for t in range(1, nd):
            plane = jnp.maximum(plane, usl[t, pieces])
        pflag[...] = plane
        total = jnp.zeros((tiles * SUB, LANES), F32)
        for r in near_rel:
            t = lax.rem(dom + r, nd)
            total = total + scatter(split_rows([usl[t, i] for i in range(pieces)]), cols_of(t))
        for e in range(EXTRAS):
            t = tab[0, T_EXT + e]
            eight = split_rows([usl[t, i] for i in range(pieces)])
            total = total + scatter(jnp.where(tab[0, T_VALID + e] == 1, eight, 0.0), cols_of(t))
        for h in range(tiles):
            part = total[h * SUB:(h + 1) * SUB]
            force[h] = part + pltpu.roll(part, FIELDS, axis=0)

    @pl.when(jnp.logical_not(is_air))
    def _():
        pltpu.make_async_copy(fgot, fgot, frecv).wait()
        for h in range(tiles):
            force[h] = fgot[0, h] + fgot[1, h] + fgot[2, h]

    group_step(0)

    @pl.when(is_air)
    def _():
        for c in range(1, nc):
            plane_flag_copy(c).start()

    bulk_step(2)
    group_step(1)
    bulk_step(3)
    group_step(2)
    group_step(3)

    @pl.when(is_air)
    def _():
        arrived(flags_in.at[pl.ds(0, ocean - 1)], grecv.at[1])
        total = pflag[...]
        for c in range(ocean):
            total = jnp.maximum(total, jnp.where(comp == c, 0.0, flags_in[c]))
        flag_out[...] = total

    @pl.when(jnp.logical_not(is_air))
    def _():
        arrived(flags_in.at[pl.ds(0, ocean)], grecv.at[1])
        total = flags_in[0]
        for c in range(1, ocean):
            total = jnp.maximum(total, flags_in[c])
        flag_out[...] = total

    @pl.when(is_air)
    def _():
        pltpu.make_async_copy(slots.at[pl.ds(0, nd - 1)], slots.at[pl.ds(0, nd - 1)], asend).wait()
        arrived(usl.at[pl.ds(0, nd - 1)], usend)
        arrived(fpart, fsend)
        arrived(flags_in.at[pl.ds(0, ocean)], gsend.at[1])

    @pl.when(jnp.logical_not(is_air))
    def _():
        arrived(fgot, ssend)
        arrived(flags_in.at[pl.ds(0, ocean)], gsend.at[0])


def windowed(state, neighbors, edge_coef, sea_mask, pair_rows, pair_cols, remap_weight, sources):
    nd, nc = lax.axis_size("dom"), lax.axis_size("comp")
    _, levels, columns = state.shape
    tiles = columns // LANES
    padded = tiles + 2 * RIM // LANES
    pairs, block = pair_rows.shape[1:]
    pieces = block // (2 * LANES)
    bulk = levels - SUB
    vmem = pl.BlockSpec(memory_space=pltpu.VMEM)
    hbm = pl.BlockSpec(memory_space=pltpu.HBM)
    dma = pltpu.SemaphoreType.DMA
    scratch = (
        [pltpu.VMEM((padded, bulk, LANES), F32)] * STEPS
        + [pltpu.VMEM((padded, SUB, LANES), F32)] * STEPS
        + [
            pltpu.VMEM(pair_cols.shape, jnp.int32),
            pltpu.VMEM((pairs, block, block), F32),
            pltpu.VMEM((EXTRAS, pieces, SUB, LANES), F32),
            pltpu.VMEM((nd, pieces, SUB, LANES), F32),
            pltpu.VMEM((nd, pieces, SUB, LANES), F32),
            pltpu.VMEM((NEAR_COUNT + 1, pieces + 1, SUB, LANES), F32),
            pltpu.VMEM((nd, pieces + 1, SUB, LANES), F32),
            pltpu.VMEM((tiles, SUB, LANES), F32),
            pltpu.VMEM((tiles, SUB, LANES), F32),
            pltpu.VMEM((nc - 1, tiles, SUB, LANES), F32),
            pltpu.VMEM((tiles, SUB, LANES), F32),
        ]
        + [pltpu.VMEM((nd + EDGES * tiles, LANES), jnp.int32), pltpu.SMEM((nd + EDGES * tiles, LANES), jnp.int32)]
        + [pltpu.VMEM((SUB, LANES), F32)] * 2 + [pltpu.VMEM((nc, SUB, LANES), F32), dma, dma((2,)), dma((2,))]
        + [dma((2,)), dma, dma]
        + [dma((2, STEPS, 2)), dma((2, STEPS, 2))]
        + [dma] * 8
    )
    return pl.pallas_call(
        functools.partial(interval_kernel, nd, nc, tiles, levels, block, pairs),
        out_shape=[jax.ShapeDtypeStruct((levels, columns), F32), jax.ShapeDtypeStruct((SUB, LANES), F32)],
        in_specs=[vmem] * 5 + [hbm] * 3,
        out_specs=[vmem, vmem],
        scratch_shapes=scratch,
        name="interval",
        cost_estimate=pl.CostEstimate(flops=10**9, bytes_accessed=10**8, transcendentals=0),
        compiler_params=pltpu.CompilerParams(
            collective_id=0, has_side_effects=True, vmem_limit_bytes=57 * 2**20),
    )(neighbors[0], edge_coef[0], sea_mask[None], pair_rows[0], sources, state[0], pair_cols, remap_weight[0])


def publish_kernel(parts, source, result, sems):
    rows = source.shape[0] // parts

    def part(i):
        at = pl.ds(i * rows, rows)
        return pltpu.make_async_copy(source.at[at], result.at[at], sems.at[i])
    for i in range(parts):
        part(i).start()
    for i in range(parts):
        part(i).wait()


def publish(array, parts=8):
    return pl.pallas_call(
        functools.partial(publish_kernel, parts),
        out_shape=jax.ShapeDtypeStruct(array.shape, array.dtype),
        in_specs=[pl.BlockSpec(memory_space=pl.ANY)],
        out_specs=pl.BlockSpec(memory_space=pl.ANY),
        scratch_shapes=[pltpu.SemaphoreType.DMA((parts,))],
        name="publish",
    )(array)


def local(state, neighbors, edge_coef, sea_mask, pair_source, pair_rows, pair_cols, remap_weight):
    sources = lax.optimization_barrier(pair_source.T)
    fast, flags = windowed(state, neighbors, edge_coef, sea_mask, pair_rows, pair_cols, remap_weight, sources)

    def anyway(_):
        return False, general(state, neighbors, edge_coef, sea_mask, sources.T, pair_rows, pair_cols, remap_weight)

    done = lax.while_loop(lambda c: c[0], anyway, (flags[0, 0] > 0, fast))
    return publish(done[1])[None]


def solution(mesh):
    placed = (
        P("comp", None, "dom"),
        P("comp", None, "dom"),
        P("comp", None, "dom"),
        P("dom"),
        P(),
        P("dom", None, None),
        P(),
        P("dom", None, None, None),
    )
    return jax.shard_map(
        local, mesh=mesh, in_specs=placed, out_specs=P("comp", None, "dom"), check_vma=False
    )
```

```python
import functools

import jax
import jax.numpy as jnp
from jax import lax
from jax.experimental import pallas as pl
from jax.experimental.layout import Layout, with_layout_constraint
from jax.experimental.pallas import tpu as pltpu
from jax.sharding import PartitionSpec as P

FIELDS = 4
RIM = 256
EDGES = 4
STEPS = 4
FORCE_GAIN = 0.5

LANES = 128
SUB = 8
NEAR = 2
NEAR_COUNT = 2 * NEAR + 1
EXTRAS = 4
MESH = pl.DeviceIdType.MESH
F32 = jnp.float32
BF16 = jnp.bfloat16


def with_halo(array, sides, width):
    for axis, dim in sides:
        devices, length = (lax.axis_size(axis), array.shape[dim])
        up = [(i, (i + 1) % devices) for i in range(devices)]
        down = [(j, i) for i, j in up]
        last = lax.slice_in_dim(array, length - width, length, axis=dim)
        leading = lax.slice_in_dim(array, 0, width, axis=dim)
        before = lax.ppermute(last, axis, up)
        after = lax.ppermute(leading, axis, down)
        array = jnp.concatenate([before, array, after], axis=dim)
    return array


def general(state, neighbors, edge_coef, sea_mask, pair_source, pair_rows, pair_cols, remap_weight):
    highest = lax.Precision.HIGHEST
    comp_count = lax.axis_size("comp")
    dom_count = lax.axis_size("dom")
    comp_id = lax.axis_index("comp")
    dom_id = lax.axis_index("dom")
    current = with_layout_constraint(state, Layout((0, 1, 2)))[0]
    fields = FIELDS
    column_count = current.shape[1]
    pair_count = pair_source.shape[1]
    block = pair_rows.shape[2]
    device_total = comp_count * dom_count
    is_ocean = comp_id == comp_count - 1
    myself = comp_id * dom_count + dom_id
    surface = current[:fields]
    pair_index = jnp.arange(pair_count, dtype=jnp.int32)
    matched = pair_source == myself
    partner = jnp.any(matched, axis=1)
    which_pair = jnp.sum(jnp.where(matched, pair_index[None, :], 0), axis=1)
    my_columns = jnp.sum(jnp.where(matched[:, :, None], pair_cols, 0), axis=1)
    handler_comp = jnp.full_like(which_pair, comp_count - 1)
    activity = jnp.where(is_ocean, 1.0, 0.0).astype(jnp.float32)
    rows_here = pair_rows[0]
    weights_here = remap_weight[0]
    own_sources = lax.dynamic_index_in_dim(pair_source, dom_id, 0, keepdims=False)
    sea_values = surface[:, rows_here]
    upward = jnp.einsum("qbj,fqb->fqj", weights_here, sea_values, precision=highest) * activity
    to_air = jnp.zeros((fields, device_total, block), jnp.float32).at[:, own_sources].add(upward)
    slot_index = handler_comp * dom_count + jnp.arange(dom_count, dtype=jnp.int32)
    air_values = surface[:, my_columns] * partner[None, :, None]
    to_sea = jnp.zeros((fields, device_total, block), jnp.float32).at[:, slot_index].add(air_values)
    got_sea, got_air = (
        lax.all_to_all(to_sea, ("comp", "dom"), split_axis=1, concat_axis=1, tiled=True),
        lax.all_to_all(to_air, ("comp", "dom"), split_axis=1, concat_axis=1, tiled=True),
    )
    incoming = got_sea[:, own_sources]
    downward = jnp.einsum("qbj,fqj->fqb", weights_here, incoming, precision=highest) * activity
    sea_force = jnp.zeros((fields, column_count), jnp.float32).at[:, rows_here].add(downward)
    arrived = got_air[:, slot_index] * partner[None, :, None]
    air_force = jnp.zeros((fields, column_count), jnp.float32).at[:, my_columns].add(arrived)
    forcing = jnp.where(is_ocean, sea_force, air_force)
    adjacency = neighbors[0]
    rates = edge_coef[0]
    evolving = jnp.logical_or(jnp.logical_not(is_ocean), sea_mask == 1)

    def advance(_, current):
        padded = with_halo(current, (("dom", 1),), RIM)
        updated = current
        for edge_number in range(EDGES):
            updated = updated + rates[edge_number] * (padded[:, adjacency[edge_number]] - current)
        updated = updated.at[:fields].add(FORCE_GAIN * (forcing - current[:fields]))
        return jnp.where(evolving[None, :], updated, current)

    return with_layout_constraint(lax.fori_loop(0, STEPS, advance, current), Layout((0, 1)))


def lane_gather(values, lanes):
    return jnp.take_along_axis(values, lanes, axis=1, mode="promise_in_bounds")


def interval_kernel(nd, nc, tiles, levels, block, pairs,
                    nbr, coef, mask, rows, sources, state_hbm, cols_hbm, w_hbm,
                    out, flag_out,
                    pb0, pb1, pb2, pb3, pg0, pg1, pg2, pg3, outb, outg,
                    cols, wbuf, compact, slots, gsl, zslots, usl, sea, fpart, fgot, force,
                    tabv, tab, flag, pflag, flags_in, tab_sem, gsend, grecv,
                    load_sem, w_sem, cols_sem, out_sem,
                    hsend, hrecv, asend, arecv, usend, urecv, ssend, srecv, fsend, frecv):
    comp = lax.axis_index("comp")
    dom = lax.axis_index("dom")
    ocean = nc - 1
    bulk = levels - SUB
    pieces = block // (2 * LANES)
    halo = RIM // LANES
    pb = [pb0, pb1, pb2, pb3]
    pg = [pg0, pg1, pg2, pg3]
    left = lax.rem(dom + nd - 1, nd)
    right = lax.rem(dom + 1, nd)
    is_air = comp < ocean
    near_rel = [0, 1, 2, nd - 2, nd - 1]
    T_WHICH, T_SEL, T_EXT, T_VALID = 0, 1, 2, 2 + EXTRAS
    T_NEARP = 2 + 2 * EXTRAS
    T_EP = T_NEARP + NEAR_COUNT
    T_EVALID, T_ESRC = T_EP + 1, T_EP + 2

    def load_g(j):
        return pltpu.make_async_copy(state_hbm.at[pl.ds(0, SUB), pl.ds(j * LANES, LANES)], pg0.at[j + halo], load_sem.at[0])

    def load_b(j):
        return pltpu.make_async_copy(state_hbm.at[pl.ds(SUB, bulk), pl.ds(j * LANES, LANES)], pb0.at[j + halo], load_sem.at[1])

    for j in range(tiles):
        load_g(j).start()
    cols_copy = pltpu.make_async_copy(cols_hbm, cols, cols_sem)
    cols_copy.start()
    for j in range(tiles):
        load_b(j).start()

    @pl.when(is_air)
    def _():
        for p in range(pairs):
            pltpu.make_async_copy(w_hbm.at[p], wbuf.at[p], w_sem).start()

    barrier = pltpu.get_barrier_semaphore()

    def greet(device):
        pl.semaphore_signal(barrier, inc=1, device_id=device, device_id_type=MESH)

    for c in range(1, nc):
        greet((lax.rem(comp + c, nc), dom))

    @pl.when(is_air)
    def _():
        def greet_plane(r, _):
            greet((comp, lax.rem(dom + r, nd)))
            return 0
        lax.fori_loop(1, nd, greet_plane, 0)

    @pl.when(jnp.logical_not(is_air))
    def _():
        greet((comp, left))
        greet((comp, right))

    def build_tables():
        src = sources[...].T
        p_i = lax.broadcasted_iota(jnp.int32, (nd, pairs), 1)
        t_i = lax.broadcasted_iota(jnp.int32, (nd, pairs), 0)
        t_c = lax.broadcasted_iota(jnp.int32, (nd, 1), 0)
        dom_f = dom
        base = (comp * nd)

        def is_far(offset):
            offset = jnp.where(offset < 0, offset + nd, offset)
            return jnp.logical_and(offset > NEAR, offset < nd - NEAR)

        mine = src == base + dom_f
        which = jnp.sum(jnp.where(mine, p_i, 0), axis=1, keepdims=True)
        hit = jnp.max(jnp.where(mine, 1, 0), axis=1, keepdims=True)
        far = jnp.where(jnp.logical_and(hit > 0, is_far(t_c - dom_f)), 1, 0)
        lanes = [(T_WHICH, which)]
        sel = jnp.zeros((nd, 1), jnp.int32)
        last = jnp.full((1, 1), -1, jnp.int32)
        for e in range(EXTRAS):
            last = jnp.min(jnp.where(jnp.logical_and(far > 0, t_c > last), t_c, nd), axis=0, keepdims=True)
            sel = jnp.where(t_c == last, e, sel)
            lanes.append((T_EXT + e, last))
            lanes.append((T_VALID + e, jnp.where(last < nd, 1, 0)))
        lanes.append((T_SEL, sel))
        crowded = jnp.sum(far, axis=0, keepdims=True) > EXTRAS

        own = jnp.sum(jnp.where(t_i == dom_f, src, 0), axis=0, keepdims=True) - base
        p_r = p_i[:1]
        for n, r in enumerate(near_rel):
            place = lax.rem(dom + r, nd)
            lanes.append((T_NEARP + n, jnp.sum(jnp.where(own == place, p_r, 0), axis=1, keepdims=True)))
        in_band = jnp.logical_and(own >= 0, own < nd)
        far_own = jnp.where(jnp.logical_and(in_band, is_far(own - dom_f)), 1, 0)
        lanes.append((T_EP, jnp.sum(far_own * p_r, axis=1, keepdims=True)))
        lanes.append((T_EVALID, jnp.max(far_own, axis=1, keepdims=True)))
        lanes.append((T_ESRC, jnp.sum(far_own * own, axis=1, keepdims=True)))
        lane = lax.broadcasted_iota(jnp.int32, (nd, LANES), 1)
        packed = jnp.zeros((nd, LANES), jnp.int32)
        for at, value in lanes:
            value = jnp.minimum(value, ((nd if at in (T_ESRC, *range(T_EXT, T_EXT + EXTRAS)) else pairs) - 1))
            packed = jnp.where(lane == at, jnp.broadcast_to(value, (nd, LANES)), packed)
        tabv[pl.ds(0, nd), :] = packed

        reach = jnp.concatenate(
            [nbr[:, j * LANES:(j + 1) * LANES] for j in range(tiles)], axis=0)
        lane = lax.broadcasted_iota(jnp.int32, reach.shape, 1)
        wide = jnp.zeros((1, 1), jnp.int32)
        packed = jnp.zeros(reach.shape, jnp.int32)
        for h, side in enumerate((lane < LANES // 2, lane >= LANES // 2)):
            first = jnp.min(jnp.where(side, reach, 2**30), axis=1, keepdims=True)
            first = jnp.clip(first, 0, ((tiles + 2 * halo - 1) * LANES))
            final = jnp.max(jnp.where(side, reach, -1), axis=1, keepdims=True)
            wide = jnp.maximum(wide, jnp.max(final - first, axis=0, keepdims=True))
            packed = jnp.where(lane == h, jnp.broadcast_to(first, reach.shape), packed)
        tabv[pl.ds(nd, EDGES * tiles), :] = packed
        bad = jnp.logical_or(wide >= LANES, crowded)
        mark = jnp.broadcast_to(jnp.where(bad, 1.0, 0.0), (SUB, LANES))
        flag[...] = mark

    build_tables()
    to_smem = pltpu.make_async_copy(tabv, tab, tab_sem)
    to_smem.start()

    row8 = lax.broadcasted_iota(jnp.int32, (SUB, LANES), 0)

    def doubled(ref, offset):
        out = []
        for h in range(tiles):
            v = ref[h + offset]
            out.append(jnp.where(row8 < FIELDS, v, pltpu.roll(v, FIELDS, axis=0)))
        return out

    def gather_slot(table, index):
        res = []
        for q in range(0, block // LANES, 2):
            i0 = index[:, q * LANES:(q + 1) * LANES]
            i1 = index[:, (q + 1) * LANES:(q + 2) * LANES]
            i8 = jnp.where(row8 < FIELDS, jnp.broadcast_to(i0, (SUB, LANES)), jnp.broadcast_to(i1, (SUB, LANES)))
            lo = i8 & (LANES - 1)
            hi = i8 >> 7
            acc = lane_gather(table[0], lo)
            for h in range(1, tiles):
                acc = jnp.where(hi == h, lane_gather(table[h], lo), acc)
            res.append(acc)
        return res

    def split_rows(res):
        cols_ = []
        for acc in res:
            high = acc.astype(BF16).astype(F32)
            low = acc - high
            cols_.append(jnp.where(row8 < FIELDS, high, pltpu.roll(low, FIELDS, axis=0)))
            cols_.append(jnp.where(row8 < FIELDS, pltpu.roll(high, FIELDS, axis=0), low))
        return jnp.concatenate(cols_, axis=1)

    def scatter(eight, index):
        hi = jnp.broadcast_to(index >> 7, (SUB, block))
        lhs = jnp.concatenate([jnp.where(hi == h, eight, 0.0) for h in range(tiles)], axis=0).astype(BF16)
        lo = jnp.broadcast_to(index & (LANES - 1), (LANES, block))
        hot = jnp.where(lo == lax.broadcasted_iota(jnp.int32, (LANES, block), 0), 1.0, 0.0).astype(BF16)
        return lax.dot_general(lhs, hot, (((1,), (1,)), ((), ())), preferred_element_type=F32)

    def cols_of(t):
        return cols[t, pl.ds(tab[t, T_WHICH], 1), :]

    pltpu.make_async_copy(pg0.at[pl.ds(halo, tiles)], pg0.at[pl.ds(halo, tiles)], load_sem.at[0]).wait()
    cols_copy.wait()
    to_smem.wait()

    @pl.when(is_air)
    def _():
        table = doubled(pg0, halo)
        for n, r in enumerate(near_rel):
            t = lax.rem(dom + r, nd)
            res = gather_slot(table, cols_of(t))
            for i, acc in enumerate(res):
                if r == 0:
                    gsl[dom, i] = acc
                else:
                    slots[r, i] = acc

        def extra(e, _):
            res = gather_slot(table, cols_of(tab[0, T_EXT + e]))
            for i, acc in enumerate(res):
                compact[e, i] = acc
            return 0
        lax.fori_loop(0, EXTRAS, extra, 0)

        def fill(r, _):
            t = lax.rem(dom + r, nd)
            slots[r] = compact[tab[t, T_SEL]]
            return 0
        lax.fori_loop(NEAR + 1, nd - NEAR, fill, 0)

    @pl.when(is_air)
    def _():
        pl.semaphore_wait(barrier, nd + nc - 2)

    @pl.when(jnp.logical_not(is_air))
    def _():
        pl.semaphore_wait(barrier, nc + 1)

    def a_copy(r):
        return pltpu.make_async_remote_copy(
            src_ref=slots.at[r], dst_ref=gsl.at[dom], send_sem=asend, recv_sem=arecv,
            device_id=(comp, lax.rem(dom + r, nd)), device_id_type=MESH)

    def halo_copies(ref, s, kind):
        to_left = pltpu.make_async_remote_copy(
            src_ref=ref.at[pl.ds(halo, halo)], dst_ref=ref.at[pl.ds(tiles + halo, halo)],
            send_sem=hsend.at[kind, s, 0], recv_sem=hrecv.at[kind, s, 0], device_id=(comp, left), device_id_type=MESH)
        to_right = pltpu.make_async_remote_copy(
            src_ref=ref.at[pl.ds(tiles, halo)], dst_ref=ref.at[pl.ds(0, halo)],
            send_sem=hsend.at[kind, s, 1], recv_sem=hrecv.at[kind, s, 1], device_id=(comp, right), device_id_type=MESH)
        return to_left, to_right

    def sea_copy(c):
        return pltpu.make_async_remote_copy(
            src_ref=pg0.at[pl.ds(halo, tiles)], dst_ref=sea, send_sem=ssend, recv_sem=srecv,
            device_id=(c, dom), device_id_type=MESH)

    def sea_flag_copy(c):
        return pltpu.make_async_remote_copy(
            src_ref=flag, dst_ref=flags_in.at[ocean], send_sem=gsend.at[0], recv_sem=grecv.at[0],
            device_id=(c, dom), device_id_type=MESH)

    def plane_flag_copy(c):
        return pltpu.make_async_remote_copy(
            src_ref=pflag, dst_ref=flags_in.at[comp], send_sem=gsend.at[1], recv_sem=grecv.at[1],
            device_id=(lax.rem(comp + c, nc), dom), device_id_type=MESH)

    def arrived(ref, sem):
        pltpu.make_async_copy(ref, ref, sem).wait()

    @pl.when(jnp.logical_not(is_air))
    def _():
        for c in range(ocean):
            sea_copy(c).start()
        for c in range(ocean):
            sea_flag_copy(c).start()

    for c in halo_copies(pg[0], 0, 0):
        c.start()

    @pl.when(is_air)
    def _():
        for r in near_rel[1:]:
            a_copy(r).start()

    arrived(pb0.at[pl.ds(halo, tiles)], load_sem.at[1])
    for c in halo_copies(pb[0], 0, 1):
        c.start()

    @pl.when(is_air)
    def _():
        def send(r, _):
            a_copy(r).start()
            return 0
        lax.fori_loop(NEAR + 1, nd - NEAR, send, 0)

    lane1 = lax.broadcasted_iota(jnp.int32, (1, LANES), 1)

    def tile_step(src, j, rows_, forced):
        cols_j = pl.ds(pl.multiple_of(j * LANES, LANES), LANES)
        cur = src[j + halo]
        upd = cur
        low = jnp.broadcast_to(lane1 < LANES // 2, (rows_, LANES))
        for k in range(EDGES):
            lo = jnp.broadcast_to(nbr[pl.ds(k, 1), cols_j] & (LANES - 1), (rows_, LANES))
            got = []
            for h in range(2):
                w = tab[nd + j * EDGES + k, h]
                b = jnp.minimum(w >> 7, tiles + 2 * halo - 2)
                edge = jnp.broadcast_to(lane1 >= w - b * LANES, (rows_, LANES))
                got.append(lane_gather(jnp.where(edge, src[b], src[b + 1]), lo))
            upd = upd + coef[pl.ds(k, 1), cols_j] * (jnp.where(low, got[0], got[1]) - cur)
        if forced:
            gain = jnp.where(row8 < FIELDS, FORCE_GAIN, 0.0)
            upd = upd + gain * (force[j] - cur)
        keep = jnp.logical_or(is_air, mask[:, cols_j] == 1)
        return jnp.where(jnp.broadcast_to(keep, (rows_, LANES)), upd, cur)

    def put_tile(bufs, last, s, j, value):
        if s + 1 < STEPS:
            bufs[s + 1][j + halo] = value
        else:
            last[j] = value

    def bulk_tiles(s, js):
        new = [tile_step(pb[s], j, bulk, False) for j in js]
        for j, value in zip(js, new):
            put_tile(pb, outb, s, j, value)

    per = 4

    def bulk_inner(s, first, last):
        def body(i, _):
            start = halo + i * per
            bulk_tiles(s, [start + u for u in range(per)])
            return 0
        lax.fori_loop(first, last, body, 0)

    def bulk_edges(s):
        for c in halo_copies(pb[s], s, 1):
            c.wait()
        bulk_tiles(s, list(range(halo)) + list(range(tiles - halo, tiles)))
        if s + 1 < STEPS:
            for c in halo_copies(pb[s + 1], s + 1, 1):
                c.start()

    inner = (tiles - 2 * halo) // per

    def bulk_step(s):
        bulk_edges(s)
        bulk_inner(s, 0, inner)

    def group_step(s):
        src = pg[s]
        for c in halo_copies(src, s, 0):
            c.wait()
        new = [tile_step(src, j, SUB, True) for j in range(tiles)]
        for j in range(tiles):
            put_tile(pg, outg, s, j, new[j])
        if s + 1 < STEPS:
            for c in halo_copies(pg[s + 1], s + 1, 0):
                c.start()

    bulk_step(0)

    @pl.when(is_air)
    def _():
        pltpu.make_async_copy(gsl.at[pl.ds(0, nd - 1)], gsl.at[pl.ds(0, nd - 1)], arecv).wait()
        pltpu.make_async_copy(sea, sea, srecv).wait()
        pltpu.make_async_copy(w_hbm, wbuf, w_sem).wait()
        arrived(flag, grecv.at[0])
        flag[...] = jnp.maximum(flag[...], flags_in[ocean])
        for n in range(1, NEAR_COUNT + 1):
            zslots[n, pieces] = flag[...]
        usl[dom, pieces] = flag[...]
        sea_table = doubled(sea, 0)
        total = jnp.zeros((tiles * SUB, LANES), F32)

        def dense(p, src):
            w = wbuf[p]
            wh = w.astype(BF16)
            wl = (w - wh.astype(F32)).astype(BF16)
            index = rows[pl.ds(p, 1), :]
            x = split_rows([gsl[src, i] for i in range(pieces)]).astype(BF16)
            v = split_rows(gather_slot(sea_table, index)).astype(BF16)
            dims = (((1,), (1,)), ((), ()))
            y = (lax.dot_general(x, wh, dims, preferred_element_type=F32)
                 + lax.dot_general(x, wl, dims, preferred_element_type=F32))
            z = jnp.dot(v, wh, preferred_element_type=F32) + jnp.dot(v, wl, preferred_element_type=F32)
            y = y[:FIELDS] + y[FIELDS:]
            z = z[:FIELDS] + z[FIELDS:]
            yh = y.astype(BF16).astype(F32)
            return jnp.concatenate([yh, y - yh], axis=0), z, index

        def put(ref, at, z):
            for q in range(block // LANES):
                ref[at, q // 2, pl.ds((q % 2) * FIELDS, FIELDS), :] = z[:, q * LANES:(q + 1) * LANES]

        def u_copy(slot, r):
            return pltpu.make_async_remote_copy(
                src_ref=zslots.at[slot], dst_ref=usl.at[dom], send_sem=usend, recv_sem=urecv,
                device_id=(comp, lax.rem(dom + r, nd)), device_id_type=MESH)

        eight, z, index = dense(tab[0, T_EP], tab[0, T_ESRC])
        put(zslots, NEAR_COUNT, z)

        def send(r, _):
            u_copy(NEAR_COUNT, r).start()
            return 0
        lax.fori_loop(NEAR + 1, nd - NEAR, send, 0)
        total = total + scatter(jnp.where(tab[0, T_EVALID] == 1, eight, 0.0), index)
        for n, r in enumerate(near_rel):
            eight, z, index = dense(tab[0, T_NEARP + n], lax.rem(dom + r, nd))
            if r == 0:
                put(usl, dom, z)
            else:
                put(zslots, n, z)
                u_copy(n, r).start()
            total = total + scatter(eight, index)
        for h in range(tiles):
            part = total[h * SUB:(h + 1) * SUB]
            fpart[h] = part + pltpu.roll(part, FIELDS, axis=0)
        pltpu.make_async_remote_copy(
            src_ref=fpart, dst_ref=fgot.at[comp], send_sem=fsend, recv_sem=frecv,
            device_id=(ocean, dom), device_id_type=MESH).start()

    bulk_step(1)

    @pl.when(is_air)
    def _():
        pltpu.make_async_copy(usl.at[pl.ds(0, nd - 1)], usl.at[pl.ds(0, nd - 1)], urecv).wait()
        plane = usl[0, pieces]
        for t in range(1, nd):
            plane = jnp.maximum(plane, usl[t, pieces])
        pflag[...] = plane
        total = jnp.zeros((tiles * SUB, LANES), F32)
        for r in near_rel:
            t = lax.rem(dom + r, nd)
            total = total + scatter(split_rows([usl[t, i] for i in range(pieces)]), cols_of(t))
        for e in range(EXTRAS):
            t = tab[0, T_EXT + e]
            eight = split_rows([usl[t, i] for i in range(pieces)])
            total = total + scatter(jnp.where(tab[0, T_VALID + e] == 1, eight, 0.0), cols_of(t))
        for h in range(tiles):
            part = total[h * SUB:(h + 1) * SUB]
            force[h] = part + pltpu.roll(part, FIELDS, axis=0)

    @pl.when(jnp.logical_not(is_air))
    def _():
        pltpu.make_async_copy(fgot, fgot, frecv).wait()
        for h in range(tiles):
            force[h] = fgot[0, h] + fgot[1, h] + fgot[2, h]

    group_step(0)

    @pl.when(is_air)
    def _():
        for c in range(1, nc):
            plane_flag_copy(c).start()

    bulk_step(2)
    group_step(1)
    bulk_edges(3)
    bulk_inner(3, 0, 1)
    group_step(2)
    bulk_inner(3, 1, inner)

    def store_b(j):
        return pltpu.make_async_copy(outb.at[j], out.at[pl.ds(SUB, bulk), pl.ds(j * LANES, LANES)], out_sem.at[1])

    def store_g(j):
        return pltpu.make_async_copy(outg.at[j], out.at[pl.ds(0, SUB), pl.ds(j * LANES, LANES)], out_sem.at[0])

    for j in range(tiles):
        store_b(j).start()
    group_step(3)
    for j in range(tiles):
        store_g(j).start()

    @pl.when(is_air)
    def _():
        arrived(flags_in.at[pl.ds(0, ocean - 1)], grecv.at[1])
        total = pflag[...]
        for c in range(ocean):
            total = jnp.maximum(total, jnp.where(comp == c, 0.0, flags_in[c]))
        flag_out[...] = total

    @pl.when(jnp.logical_not(is_air))
    def _():
        arrived(flags_in.at[pl.ds(0, ocean)], grecv.at[1])
        total = flags_in[0]
        for c in range(1, ocean):
            total = jnp.maximum(total, flags_in[c])
        flag_out[...] = total

    @pl.when(is_air)
    def _():
        pltpu.make_async_copy(slots.at[pl.ds(0, nd - 1)], slots.at[pl.ds(0, nd - 1)], asend).wait()
        arrived(usl.at[pl.ds(0, nd - 1)], usend)
        arrived(fpart, fsend)
        arrived(flags_in.at[pl.ds(0, ocean)], gsend.at[1])

    @pl.when(jnp.logical_not(is_air))
    def _():
        arrived(fgot, ssend)
        arrived(flags_in.at[pl.ds(0, ocean)], gsend.at[0])

    arrived(outb, out_sem.at[1])
    arrived(outg, out_sem.at[0])


def windowed(state, neighbors, edge_coef, sea_mask, pair_rows, pair_cols, remap_weight, sources):
    nd, nc = lax.axis_size("dom"), lax.axis_size("comp")
    _, levels, columns = state.shape
    tiles = columns // LANES
    padded = tiles + 2 * RIM // LANES
    pairs, block = pair_rows.shape[1:]
    pieces = block // (2 * LANES)
    bulk = levels - SUB
    vmem = pl.BlockSpec(memory_space=pltpu.VMEM)
    hbm = pl.BlockSpec(memory_space=pltpu.HBM)
    dma = pltpu.SemaphoreType.DMA
    scratch = (
        [pltpu.VMEM((padded, bulk, LANES), F32)] * STEPS
        + [pltpu.VMEM((padded, SUB, LANES), F32)] * STEPS
        + [pltpu.VMEM((tiles, bulk, LANES), F32), pltpu.VMEM((tiles, SUB, LANES), F32)]
        + [
            pltpu.VMEM(pair_cols.shape, jnp.int32),
            pltpu.VMEM((pairs, block, block), F32),
            pltpu.VMEM((EXTRAS, pieces, SUB, LANES), F32),
            pltpu.VMEM((nd, pieces, SUB, LANES), F32),
            pltpu.VMEM((nd, pieces, SUB, LANES), F32),
            pltpu.VMEM((NEAR_COUNT + 1, pieces + 1, SUB, LANES), F32),
            pltpu.VMEM((nd, pieces + 1, SUB, LANES), F32),
            pltpu.VMEM((tiles, SUB, LANES), F32),
            pltpu.VMEM((tiles, SUB, LANES), F32),
            pltpu.VMEM((nc - 1, tiles, SUB, LANES), F32),
            pltpu.VMEM((tiles, SUB, LANES), F32),
        ]
        + [pltpu.VMEM((nd + EDGES * tiles, LANES), jnp.int32), pltpu.SMEM((nd + EDGES * tiles, LANES), jnp.int32)]
        + [pltpu.VMEM((SUB, LANES), F32)] * 2 + [pltpu.VMEM((nc, SUB, LANES), F32), dma, dma((2,)), dma((2,))]
        + [dma((2,)), dma, dma, dma((2,))]
        + [dma((2, STEPS, 2)), dma((2, STEPS, 2))]
        + [dma] * 8
    )
    return pl.pallas_call(
        functools.partial(interval_kernel, nd, nc, tiles, levels, block, pairs),
        out_shape=[jax.ShapeDtypeStruct((levels, columns), F32), jax.ShapeDtypeStruct((SUB, LANES), F32)],
        in_specs=[vmem] * 5 + [hbm] * 3,
        out_specs=[hbm, vmem],
        scratch_shapes=scratch,
        name="interval",
        cost_estimate=pl.CostEstimate(flops=10**9, bytes_accessed=10**8, transcendentals=0),
        compiler_params=pltpu.CompilerParams(
            collective_id=0, has_side_effects=True, vmem_limit_bytes=57 * 2**20),
    )(neighbors[0], edge_coef[0], sea_mask[None], pair_rows[0], sources, state[0], pair_cols, remap_weight[0])


def publish_kernel(source, result):
    result[...] = source[...]


def publish(array, parts=4):
    spec = pl.BlockSpec((array.shape[0] // parts, array.shape[1]), lambda i: (i, 0))
    return pl.pallas_call(
        publish_kernel,
        out_shape=jax.ShapeDtypeStruct(array.shape, array.dtype),
        grid=(parts,),
        in_specs=[spec],
        out_specs=spec,
        name="publish",
    )(array)


def local(state, neighbors, edge_coef, sea_mask, pair_source, pair_rows, pair_cols, remap_weight):
    sources = lax.optimization_barrier(pair_source.T)
    fast, flags = windowed(state, neighbors, edge_coef, sea_mask, pair_rows, pair_cols, remap_weight, sources)

    def anyway(_):
        return False, general(state, neighbors, edge_coef, sea_mask,
                              with_layout_constraint(sources, Layout((0, 1))).T, pair_rows, pair_cols, remap_weight)

    done = lax.while_loop(lambda c: c[0], anyway, (flags[0, 0] > 0, fast))
    return publish(done[1])[None]


def solution(mesh):
    placed = (
        P("comp", None, "dom"),
        P("comp", None, "dom"),
        P("comp", None, "dom"),
        P("dom"),
        P(),
        P("dom", None, None),
        P(),
        P("dom", None, None, None),
    )
    return jax.shard_map(
        local, mesh=mesh, in_specs=placed, out_specs=P("comp", None, "dom"), check_vma=False
    )
```

```python
import functools

import jax
import jax.numpy as jnp
from jax import lax
from jax.experimental import pallas as pl
from jax.experimental.layout import Layout, with_layout_constraint
from jax.experimental.pallas import tpu as pltpu
from jax.sharding import PartitionSpec as P

FIELDS = 4
RIM = 256
EDGES = 4
STEPS = 4
FORCE_GAIN = 0.5

LANES = 128
SUB = 8
NEAR = 2
NEAR_COUNT = 2 * NEAR + 1
EXTRAS = 4
MESH = pl.DeviceIdType.MESH
F32 = jnp.float32
BF16 = jnp.bfloat16


def with_halo(array, sides, width):
    for axis, dim in sides:
        devices, length = (lax.axis_size(axis), array.shape[dim])
        up = [(i, (i + 1) % devices) for i in range(devices)]
        down = [(j, i) for i, j in up]
        last = lax.slice_in_dim(array, length - width, length, axis=dim)
        leading = lax.slice_in_dim(array, 0, width, axis=dim)
        before = lax.ppermute(last, axis, up)
        after = lax.ppermute(leading, axis, down)
        array = jnp.concatenate([before, array, after], axis=dim)
    return array


def general(state, neighbors, edge_coef, sea_mask, pair_source, pair_rows, pair_cols, remap_weight):
    highest = lax.Precision.HIGHEST
    comp_count = lax.axis_size("comp")
    dom_count = lax.axis_size("dom")
    comp_id = lax.axis_index("comp")
    dom_id = lax.axis_index("dom")
    current = with_layout_constraint(state, Layout((0, 1, 2)))[0]
    fields = FIELDS
    column_count = current.shape[1]
    pair_count = pair_source.shape[1]
    block = pair_rows.shape[2]
    device_total = comp_count * dom_count
    is_ocean = comp_id == comp_count - 1
    myself = comp_id * dom_count + dom_id
    surface = current[:fields]
    pair_index = jnp.arange(pair_count, dtype=jnp.int32)
    matched = pair_source == myself
    partner = jnp.any(matched, axis=1)
    which_pair = jnp.sum(jnp.where(matched, pair_index[None, :], 0), axis=1)
    my_columns = jnp.sum(jnp.where(matched[:, :, None], pair_cols, 0), axis=1)
    handler_comp = jnp.full_like(which_pair, comp_count - 1)
    activity = jnp.where(is_ocean, 1.0, 0.0).astype(jnp.float32)
    rows_here = pair_rows[0]
    weights_here = remap_weight[0]
    own_sources = lax.dynamic_index_in_dim(pair_source, dom_id, 0, keepdims=False)
    sea_values = surface[:, rows_here]
    upward = jnp.einsum("qbj,fqb->fqj", weights_here, sea_values, precision=highest) * activity
    to_air = jnp.zeros((fields, device_total, block), jnp.float32).at[:, own_sources].add(upward)
    slot_index = handler_comp * dom_count + jnp.arange(dom_count, dtype=jnp.int32)
    air_values = surface[:, my_columns] * partner[None, :, None]
    to_sea = jnp.zeros((fields, device_total, block), jnp.float32).at[:, slot_index].add(air_values)
    got_sea, got_air = (
        lax.all_to_all(to_sea, ("comp", "dom"), split_axis=1, concat_axis=1, tiled=True),
        lax.all_to_all(to_air, ("comp", "dom"), split_axis=1, concat_axis=1, tiled=True),
    )
    incoming = got_sea[:, own_sources]
    downward = jnp.einsum("qbj,fqj->fqb", weights_here, incoming, precision=highest) * activity
    sea_force = jnp.zeros((fields, column_count), jnp.float32).at[:, rows_here].add(downward)
    arrived = got_air[:, slot_index] * partner[None, :, None]
    air_force = jnp.zeros((fields, column_count), jnp.float32).at[:, my_columns].add(arrived)
    forcing = jnp.where(is_ocean, sea_force, air_force)
    adjacency = neighbors[0]
    rates = edge_coef[0]
    evolving = jnp.logical_or(jnp.logical_not(is_ocean), sea_mask == 1)

    def advance(_, current):
        padded = with_halo(current, (("dom", 1),), RIM)
        updated = current
        for edge_number in range(EDGES):
            updated = updated + rates[edge_number] * (padded[:, adjacency[edge_number]] - current)
        updated = updated.at[:fields].add(FORCE_GAIN * (forcing - current[:fields]))
        return jnp.where(evolving[None, :], updated, current)

    return with_layout_constraint(lax.fori_loop(0, STEPS, advance, current), Layout((0, 1)))


def lane_gather(values, lanes):
    return jnp.take_along_axis(values, lanes, axis=1, mode="promise_in_bounds")


def interval_kernel(nd, nc, tiles, levels, block, pairs,
                    nbr, coef, mask, rows, sources, state_hbm, cols_hbm, w_hbm,
                    out, flag_out,
                    pb0, pb1, pb2, pb3, pg0, pg1, pg2, pg3, outb, outg,
                    cols, wbuf, compact, slots, gsl, zslots, usl, nslots, gnear, unear, sea, fpart, fgot, force,
                    tabv, tab, flag, pflag, flags_in, tab_sem, gsend, grecv,
                    load_sem, w_sem, cols_sem, out_sem,
                    hsend, hrecv, asend, arecv, usend, urecv, ssend, srecv, fsend, frecv):
    comp = lax.axis_index("comp")
    dom = lax.axis_index("dom")
    ocean = nc - 1
    bulk = levels - SUB
    pieces = block // (2 * LANES)
    halo = RIM // LANES
    pb = [pb0, pb1, pb2, pb3]
    pg = [pg0, pg1, pg2, pg3]
    left = lax.rem(dom + nd - 1, nd)
    right = lax.rem(dom + 1, nd)
    is_air = comp < ocean
    near_rel = [0, 1, 2, nd - 2, nd - 1]
    far_count = nd - NEAR_COUNT
    T_WHICH, T_SEL, T_EXT, T_VALID = 0, 1, 2, 2 + EXTRAS
    T_NEARP = 2 + 2 * EXTRAS
    T_EP = T_NEARP + NEAR_COUNT
    T_EVALID, T_ESRC = T_EP + 1, T_EP + 2

    def load_g(j):
        return pltpu.make_async_copy(state_hbm.at[pl.ds(0, SUB), pl.ds(j * LANES, LANES)], pg0.at[j + halo], load_sem.at[0])

    def load_b(j):
        return pltpu.make_async_copy(state_hbm.at[pl.ds(SUB, bulk), pl.ds(j * LANES, LANES)], pb0.at[j + halo], load_sem.at[1])

    for j in range(tiles):
        load_g(j).start()
    cols_copy = pltpu.make_async_copy(cols_hbm, cols, cols_sem)
    cols_copy.start()
    for j in range(tiles):
        load_b(j).start()

    @pl.when(is_air)
    def _():
        for p in range(pairs):
            pltpu.make_async_copy(w_hbm.at[p], wbuf.at[p], w_sem).start()

    barrier = pltpu.get_barrier_semaphore()

    def greet(device):
        pl.semaphore_signal(barrier, inc=1, device_id=device, device_id_type=MESH)

    for c in range(1, nc):
        greet((lax.rem(comp + c, nc), dom))

    @pl.when(is_air)
    def _():
        def greet_plane(r, _):
            greet((comp, lax.rem(dom + r, nd)))
            return 0
        lax.fori_loop(1, nd, greet_plane, 0)

    @pl.when(jnp.logical_not(is_air))
    def _():
        greet((comp, left))
        greet((comp, right))

    def build_tables():
        src = sources[...].T
        p_i = lax.broadcasted_iota(jnp.int32, (nd, pairs), 1)
        t_i = lax.broadcasted_iota(jnp.int32, (nd, pairs), 0)
        t_c = lax.broadcasted_iota(jnp.int32, (nd, 1), 0)
        dom_f = dom
        base = (comp * nd)

        def is_far(offset):
            offset = jnp.where(offset < 0, offset + nd, offset)
            return jnp.logical_and(offset > NEAR, offset < nd - NEAR)

        mine = src == base + dom_f
        which = jnp.sum(jnp.where(mine, p_i, 0), axis=1, keepdims=True)
        hit = jnp.max(jnp.where(mine, 1, 0), axis=1, keepdims=True)
        far = jnp.where(jnp.logical_and(hit > 0, is_far(t_c - dom_f)), 1, 0)
        lanes = [(T_WHICH, which)]
        sel = jnp.zeros((nd, 1), jnp.int32)
        last = jnp.full((1, 1), -1, jnp.int32)
        for e in range(EXTRAS):
            last = jnp.min(jnp.where(jnp.logical_and(far > 0, t_c > last), t_c, nd), axis=0, keepdims=True)
            sel = jnp.where(t_c == last, e, sel)
            lanes.append((T_EXT + e, last))
            lanes.append((T_VALID + e, jnp.where(last < nd, 1, 0)))
        lanes.append((T_SEL, sel))
        crowded = jnp.sum(far, axis=0, keepdims=True) > EXTRAS

        own = jnp.sum(jnp.where(t_i == dom_f, src, 0), axis=0, keepdims=True) - base
        p_r = p_i[:1]
        for n, r in enumerate(near_rel):
            place = lax.rem(dom + r, nd)
            lanes.append((T_NEARP + n, jnp.sum(jnp.where(own == place, p_r, 0), axis=1, keepdims=True)))
        in_band = jnp.logical_and(own >= 0, own < nd)
        far_own = jnp.where(jnp.logical_and(in_band, is_far(own - dom_f)), 1, 0)
        lanes.append((T_EP, jnp.sum(far_own * p_r, axis=1, keepdims=True)))
        lanes.append((T_EVALID, jnp.max(far_own, axis=1, keepdims=True)))
        lanes.append((T_ESRC, jnp.sum(far_own * own, axis=1, keepdims=True)))
        lane = lax.broadcasted_iota(jnp.int32, (nd, LANES), 1)
        packed = jnp.zeros((nd, LANES), jnp.int32)
        for at, value in lanes:
            value = jnp.minimum(value, ((nd if at in (T_ESRC, *range(T_EXT, T_EXT + EXTRAS)) else pairs) - 1))
            packed = jnp.where(lane == at, jnp.broadcast_to(value, (nd, LANES)), packed)
        tabv[pl.ds(0, nd), :] = packed

        reach = jnp.concatenate(
            [nbr[:, j * LANES:(j + 1) * LANES] for j in range(tiles)], axis=0)
        lane = lax.broadcasted_iota(jnp.int32, reach.shape, 1)
        wide = jnp.zeros((1, 1), jnp.int32)
        packed = jnp.zeros(reach.shape, jnp.int32)
        for h, side in enumerate((lane < LANES // 2, lane >= LANES // 2)):
            first = jnp.min(jnp.where(side, reach, 2**30), axis=1, keepdims=True)
            first = jnp.clip(first, 0, ((tiles + 2 * halo - 1) * LANES))
            final = jnp.max(jnp.where(side, reach, -1), axis=1, keepdims=True)
            wide = jnp.maximum(wide, jnp.max(final - first, axis=0, keepdims=True))
            packed = jnp.where(lane == h, jnp.broadcast_to(first, reach.shape), packed)
        tabv[pl.ds(nd, EDGES * tiles), :] = packed
        bad = jnp.logical_or(wide >= LANES, crowded)
        mark = jnp.broadcast_to(jnp.where(bad, 1.0, 0.0), (SUB, LANES))
        flag[...] = mark

    build_tables()
    to_smem = pltpu.make_async_copy(tabv, tab, tab_sem)
    to_smem.start()

    row8 = lax.broadcasted_iota(jnp.int32, (SUB, LANES), 0)

    def doubled(ref, offset):
        out = []
        for h in range(tiles):
            v = ref[h + offset]
            out.append(jnp.where(row8 < FIELDS, v, pltpu.roll(v, FIELDS, axis=0)))
        return out

    def gather_slot(table, index):
        res = []
        for q in range(0, block // LANES, 2):
            i0 = index[:, q * LANES:(q + 1) * LANES]
            i1 = index[:, (q + 1) * LANES:(q + 2) * LANES]
            i8 = jnp.where(row8 < FIELDS, jnp.broadcast_to(i0, (SUB, LANES)), jnp.broadcast_to(i1, (SUB, LANES)))
            lo = i8 & (LANES - 1)
            hi = i8 >> 7
            acc = lane_gather(table[0], lo)
            for h in range(1, tiles):
                acc = jnp.where(hi == h, lane_gather(table[h], lo), acc)
            res.append(acc)
        return res

    def split_rows(res):
        cols_ = []
        for acc in res:
            high = acc.astype(BF16).astype(F32)
            low = acc - high
            cols_.append(jnp.where(row8 < FIELDS, high, pltpu.roll(low, FIELDS, axis=0)))
            cols_.append(jnp.where(row8 < FIELDS, pltpu.roll(high, FIELDS, axis=0), low))
        return jnp.concatenate(cols_, axis=1)

    def scatter(eight, index):
        hi = jnp.broadcast_to(index >> 7, (SUB, block))
        lhs = jnp.concatenate([jnp.where(hi == h, eight, 0.0) for h in range(tiles)], axis=0).astype(BF16)
        lo = jnp.broadcast_to(index & (LANES - 1), (LANES, block))
        hot = jnp.where(lo == lax.broadcasted_iota(jnp.int32, (LANES, block), 0), 1.0, 0.0).astype(BF16)
        return lax.dot_general(lhs, hot, (((1,), (1,)), ((), ())), preferred_element_type=F32)

    def cols_of(t):
        return cols[t, pl.ds(tab[t, T_WHICH], 1), :]

    pltpu.make_async_copy(pg0.at[pl.ds(halo, tiles)], pg0.at[pl.ds(halo, tiles)], load_sem.at[0]).wait()
    cols_copy.wait()
    to_smem.wait()

    @pl.when(is_air)
    def _():
        table = doubled(pg0, halo)

        def extra(e, _):
            res = gather_slot(table, cols_of(tab[0, T_EXT + e]))
            for i, acc in enumerate(res):
                compact[e, i] = acc
            return 0
        lax.fori_loop(0, EXTRAS, extra, 0)

        def fill(r, _):
            t = lax.rem(dom + r, nd)
            slots[r] = compact[tab[t, T_SEL]]
            return 0
        lax.fori_loop(NEAR + 1, nd - NEAR, fill, 0)

    @pl.when(is_air)
    def _():
        pl.semaphore_wait(barrier, nd + nc - 2)

    @pl.when(jnp.logical_not(is_air))
    def _():
        pl.semaphore_wait(barrier, nc + 1)

    def mirror(n):
        return near_rel.index((nd - near_rel[n]) % nd)

    def a_copy(r):
        return pltpu.make_async_remote_copy(
            src_ref=slots.at[r], dst_ref=gsl.at[dom], send_sem=asend.at[0], recv_sem=arecv.at[0],
            device_id=(comp, lax.rem(dom + r, nd)), device_id_type=MESH)

    def a_near(n):
        return pltpu.make_async_remote_copy(
            src_ref=nslots.at[n], dst_ref=gnear.at[mirror(n)], send_sem=asend.at[1], recv_sem=arecv.at[1],
            device_id=(comp, lax.rem(dom + near_rel[n], nd)), device_id_type=MESH)

    def halo_copies(ref, s, kind):
        to_left = pltpu.make_async_remote_copy(
            src_ref=ref.at[pl.ds(halo, halo)], dst_ref=ref.at[pl.ds(tiles + halo, halo)],
            send_sem=hsend.at[kind, s, 0], recv_sem=hrecv.at[kind, s, 0], device_id=(comp, left), device_id_type=MESH)
        to_right = pltpu.make_async_remote_copy(
            src_ref=ref.at[pl.ds(tiles, halo)], dst_ref=ref.at[pl.ds(0, halo)],
            send_sem=hsend.at[kind, s, 1], recv_sem=hrecv.at[kind, s, 1], device_id=(comp, right), device_id_type=MESH)
        return to_left, to_right

    def sea_copy(c):
        return pltpu.make_async_remote_copy(
            src_ref=pg0.at[pl.ds(halo, tiles)], dst_ref=sea, send_sem=ssend, recv_sem=srecv,
            device_id=(c, dom), device_id_type=MESH)

    def sea_flag_copy(c):
        return pltpu.make_async_remote_copy(
            src_ref=flag, dst_ref=flags_in.at[ocean], send_sem=gsend.at[0], recv_sem=grecv.at[0],
            device_id=(c, dom), device_id_type=MESH)

    def plane_flag_copy(c):
        return pltpu.make_async_remote_copy(
            src_ref=pflag, dst_ref=flags_in.at[comp], send_sem=gsend.at[1], recv_sem=grecv.at[1],
            device_id=(lax.rem(comp + c, nc), dom), device_id_type=MESH)

    def arrived(ref, sem):
        pltpu.make_async_copy(ref, ref, sem).wait()

    @pl.when(jnp.logical_not(is_air))
    def _():
        for c in range(ocean):
            sea_copy(c).start()
        for c in range(ocean):
            sea_flag_copy(c).start()

    arrived(pb0.at[pl.ds(halo, tiles)], load_sem.at[1])
    for c in halo_copies(pb[0], 0, 1):
        c.start()

    @pl.when(is_air)
    def _():
        def send(r, _):
            a_copy(r).start()
            return 0
        lax.fori_loop(NEAR + 1, nd - NEAR, send, 0)
        table = doubled(pg0, halo)
        for n, r in enumerate(near_rel):
            res = gather_slot(table, cols_of(lax.rem(dom + r, nd)))
            for i, acc in enumerate(res):
                if r == 0:
                    gnear[n, i] = acc
                else:
                    nslots[n, i] = acc
        for n in range(1, NEAR_COUNT):
            a_near(n).start()

    for c in halo_copies(pg[0], 0, 0):
        c.start()

    lane1 = lax.broadcasted_iota(jnp.int32, (1, LANES), 1)

    def tile_step(src, j, rows_, forced):
        cols_j = pl.ds(pl.multiple_of(j * LANES, LANES), LANES)
        cur = src[j + halo]
        upd = cur
        low = jnp.broadcast_to(lane1 < LANES // 2, (rows_, LANES))
        for k in range(EDGES):
            lo = jnp.broadcast_to(nbr[pl.ds(k, 1), cols_j] & (LANES - 1), (rows_, LANES))
            got = []
            for h in range(2):
                w = tab[nd + j * EDGES + k, h]
                b = jnp.minimum(w >> 7, tiles + 2 * halo - 2)
                edge = jnp.broadcast_to(lane1 >= w - b * LANES, (rows_, LANES))
                got.append(lane_gather(jnp.where(edge, src[b], src[b + 1]), lo))
            upd = upd + coef[pl.ds(k, 1), cols_j] * (jnp.where(low, got[0], got[1]) - cur)
        if forced:
            gain = jnp.where(row8 < FIELDS, FORCE_GAIN, 0.0)
            upd = upd + gain * (force[j] - cur)
        keep = jnp.logical_or(is_air, mask[:, cols_j] == 1)
        return jnp.where(jnp.broadcast_to(keep, (rows_, LANES)), upd, cur)

    def put_tile(bufs, last, s, j, value):
        if s + 1 < STEPS:
            bufs[s + 1][j + halo] = value
        else:
            last[j] = value

    def bulk_tiles(s, js):
        new = [tile_step(pb[s], j, bulk, False) for j in js]
        for j, value in zip(js, new):
            put_tile(pb, outb, s, j, value)

    per = 4

    def bulk_inner(s, first, last):
        def body(i, _):
            start = halo + i * per
            bulk_tiles(s, [start + u for u in range(per)])
            return 0
        lax.fori_loop(first, last, body, 0)

    def bulk_edges(s):
        for c in halo_copies(pb[s], s, 1):
            c.wait()
        bulk_tiles(s, list(range(halo)) + list(range(tiles - halo, tiles)))
        if s + 1 < STEPS:
            for c in halo_copies(pb[s + 1], s + 1, 1):
                c.start()

    inner = (tiles - 2 * halo) // per

    def bulk_step(s):
        bulk_edges(s)
        bulk_inner(s, 0, inner)

    def group_step(s):
        src = pg[s]
        for c in halo_copies(src, s, 0):
            c.wait()
        new = [tile_step(src, j, SUB, True) for j in range(tiles)]
        for j in range(tiles):
            put_tile(pg, outg, s, j, new[j])
        if s + 1 < STEPS:
            for c in halo_copies(pg[s + 1], s + 1, 0):
                c.start()

    bulk_step(0)

    @pl.when(is_air)
    def _():
        arrived(sea, srecv)
        arrived(flag, grecv.at[0])
        pltpu.make_async_copy(w_hbm, wbuf, w_sem).wait()
        flag[...] = jnp.maximum(flag[...], flags_in[ocean])
        for n in range(NEAR_COUNT + 1):
            zslots[n, pieces] = flag[...]
        sea_table = doubled(sea, 0)

        def dense(p, slot):
            w = wbuf[p]
            wh = w.astype(BF16)
            wl = (w - wh.astype(F32)).astype(BF16)
            index = rows[pl.ds(p, 1), :]
            x = split_rows(slot).astype(BF16)
            v = split_rows(gather_slot(sea_table, index)).astype(BF16)
            dims = (((1,), (1,)), ((), ()))
            y = (lax.dot_general(x, wh, dims, preferred_element_type=F32)
                 + lax.dot_general(x, wl, dims, preferred_element_type=F32))
            z = jnp.dot(v, wh, preferred_element_type=F32) + jnp.dot(v, wl, preferred_element_type=F32)
            y = y[:FIELDS] + y[FIELDS:]
            z = z[:FIELDS] + z[FIELDS:]
            yh = y.astype(BF16).astype(F32)
            return jnp.concatenate([yh, y - yh], axis=0), z, index

        def put(ref, at, z):
            for q in range(block // LANES):
                ref[at, q // 2, pl.ds((q % 2) * FIELDS, FIELDS), :] = z[:, q * LANES:(q + 1) * LANES]

        def u_copy(r):
            return pltpu.make_async_remote_copy(
                src_ref=zslots.at[NEAR_COUNT], dst_ref=usl.at[dom], send_sem=usend.at[0], recv_sem=urecv.at[0],
                device_id=(comp, lax.rem(dom + r, nd)), device_id_type=MESH)

        def u_near(n):
            return pltpu.make_async_remote_copy(
                src_ref=zslots.at[n], dst_ref=unear.at[mirror(n)], send_sem=usend.at[1], recv_sem=urecv.at[1],
                device_id=(comp, lax.rem(dom + near_rel[n], nd)), device_id_type=MESH)

        def near_block(n):
            eight, z, index = dense(tab[0, T_NEARP + n], [gnear[n, i] for i in range(pieces)])
            if n == 0:
                put(unear, n, z)
            else:
                put(zslots, n, z)
                u_near(n).start()
            return scatter(eight, index)

        arrived(gnear.at[pl.ds(0, NEAR_COUNT - 1)], arecv.at[1])
        total = near_block(1)
        total = total + near_block(NEAR_COUNT - 1)

        arrived(gsl.at[pl.ds(0, far_count)], arecv.at[0])
        src = tab[0, T_ESRC]
        eight, z, index = dense(tab[0, T_EP], [gsl[src, i] for i in range(pieces)])
        put(zslots, NEAR_COUNT, z)

        def send(r, _):
            u_copy(r).start()
            return 0
        lax.fori_loop(NEAR + 1, nd - NEAR, send, 0)
        total = total + scatter(jnp.where(tab[0, T_EVALID] == 1, eight, 0.0), index)
        for n in range(2, NEAR_COUNT - 1):
            total = total + near_block(n)
        total = total + near_block(0)
        for h in range(tiles):
            part = total[h * SUB:(h + 1) * SUB]
            fpart[h] = part + pltpu.roll(part, FIELDS, axis=0)
        pltpu.make_async_remote_copy(
            src_ref=fpart, dst_ref=fgot.at[comp], send_sem=fsend, recv_sem=frecv,
            device_id=(ocean, dom), device_id_type=MESH).start()

    bulk_step(1)

    @pl.when(is_air)
    def _():
        arrived(unear.at[pl.ds(0, NEAR_COUNT - 1)], urecv.at[1])
        total = jnp.zeros((tiles * SUB, LANES), F32)
        plane = flag[...]
        for n, r in enumerate(near_rel):
            if r:
                plane = jnp.maximum(plane, unear[n, pieces])
            total = total + scatter(split_rows([unear[n, i] for i in range(pieces)]), cols_of(lax.rem(dom + r, nd)))
        arrived(usl.at[pl.ds(0, far_count)], urecv.at[0])
        for r in range(NEAR + 1, nd - NEAR):
            plane = jnp.maximum(plane, usl[lax.rem(dom + r, nd), pieces])
        pflag[...] = plane
        for e in range(EXTRAS):
            t = tab[0, T_EXT + e]
            eight = split_rows([usl[t, i] for i in range(pieces)])
            total = total + scatter(jnp.where(tab[0, T_VALID + e] == 1, eight, 0.0), cols_of(t))
        for h in range(tiles):
            part = total[h * SUB:(h + 1) * SUB]
            force[h] = part + pltpu.roll(part, FIELDS, axis=0)

    @pl.when(jnp.logical_not(is_air))
    def _():
        pltpu.make_async_copy(fgot, fgot, frecv).wait()
        for h in range(tiles):
            force[h] = fgot[0, h] + fgot[1, h] + fgot[2, h]

    group_step(0)

    @pl.when(is_air)
    def _():
        for c in range(1, nc):
            plane_flag_copy(c).start()

    bulk_step(2)
    group_step(1)
    bulk_edges(3)
    bulk_inner(3, 0, 1)
    group_step(2)
    bulk_inner(3, 1, inner)

    def store_b(j):
        return pltpu.make_async_copy(outb.at[j], out.at[pl.ds(SUB, bulk), pl.ds(j * LANES, LANES)], out_sem.at[1])

    def store_g(j):
        return pltpu.make_async_copy(outg.at[j], out.at[pl.ds(0, SUB), pl.ds(j * LANES, LANES)], out_sem.at[0])

    for j in range(tiles):
        store_b(j).start()
    group_step(3)
    for j in range(tiles):
        store_g(j).start()

    @pl.when(is_air)
    def _():
        arrived(flags_in.at[pl.ds(0, ocean - 1)], grecv.at[1])
        total = pflag[...]
        for c in range(ocean):
            total = jnp.maximum(total, jnp.where(comp == c, 0.0, flags_in[c]))
        flag_out[...] = total

    @pl.when(jnp.logical_not(is_air))
    def _():
        arrived(flags_in.at[pl.ds(0, ocean)], grecv.at[1])
        total = flags_in[0]
        for c in range(1, ocean):
            total = jnp.maximum(total, flags_in[c])
        flag_out[...] = total

    @pl.when(is_air)
    def _():
        arrived(slots.at[pl.ds(0, far_count)], asend.at[0])
        arrived(nslots.at[pl.ds(0, NEAR_COUNT - 1)], asend.at[1])
        arrived(usl.at[pl.ds(0, far_count)], usend.at[0])
        arrived(unear.at[pl.ds(0, NEAR_COUNT - 1)], usend.at[1])
        arrived(fpart, fsend)
        arrived(flags_in.at[pl.ds(0, ocean)], gsend.at[1])

    @pl.when(jnp.logical_not(is_air))
    def _():
        arrived(fgot, ssend)
        arrived(flags_in.at[pl.ds(0, ocean)], gsend.at[0])

    arrived(outb, out_sem.at[1])
    arrived(outg, out_sem.at[0])


def windowed(state, neighbors, edge_coef, sea_mask, pair_rows, pair_cols, remap_weight, sources):
    nd, nc = lax.axis_size("dom"), lax.axis_size("comp")
    _, levels, columns = state.shape
    tiles = columns // LANES
    padded = tiles + 2 * RIM // LANES
    pairs, block = pair_rows.shape[1:]
    pieces = block // (2 * LANES)
    bulk = levels - SUB
    vmem = pl.BlockSpec(memory_space=pltpu.VMEM)
    hbm = pl.BlockSpec(memory_space=pltpu.HBM)
    dma = pltpu.SemaphoreType.DMA
    scratch = (
        [pltpu.VMEM((padded, bulk, LANES), F32)] * STEPS
        + [pltpu.VMEM((padded, SUB, LANES), F32)] * STEPS
        + [pltpu.VMEM((tiles, bulk, LANES), F32), pltpu.VMEM((tiles, SUB, LANES), F32)]
        + [
            pltpu.VMEM(pair_cols.shape, jnp.int32),
            pltpu.VMEM((pairs, block, block), F32),
            pltpu.VMEM((EXTRAS, pieces, SUB, LANES), F32),
            pltpu.VMEM((nd, pieces, SUB, LANES), F32),
            pltpu.VMEM((nd, pieces, SUB, LANES), F32),
            pltpu.VMEM((NEAR_COUNT + 1, pieces + 1, SUB, LANES), F32),
            pltpu.VMEM((nd, pieces + 1, SUB, LANES), F32),
            pltpu.VMEM((NEAR_COUNT, pieces, SUB, LANES), F32),
            pltpu.VMEM((NEAR_COUNT, pieces, SUB, LANES), F32),
            pltpu.VMEM((NEAR_COUNT, pieces + 1, SUB, LANES), F32),
            pltpu.VMEM((tiles, SUB, LANES), F32),
            pltpu.VMEM((tiles, SUB, LANES), F32),
            pltpu.VMEM((nc - 1, tiles, SUB, LANES), F32),
            pltpu.VMEM((tiles, SUB, LANES), F32),
        ]
        + [pltpu.VMEM((nd + EDGES * tiles, LANES), jnp.int32), pltpu.SMEM((nd + EDGES * tiles, LANES), jnp.int32)]
        + [pltpu.VMEM((SUB, LANES), F32)] * 2 + [pltpu.VMEM((nc, SUB, LANES), F32), dma, dma((2,)), dma((2,))]
        + [dma((2,)), dma, dma, dma((2,))]
        + [dma((2, STEPS, 2)), dma((2, STEPS, 2))]
        + [dma((2,))] * 4 + [dma] * 4
    )
    return pl.pallas_call(
        functools.partial(interval_kernel, nd, nc, tiles, levels, block, pairs),
        out_shape=[jax.ShapeDtypeStruct((levels, columns), F32), jax.ShapeDtypeStruct((SUB, LANES), F32)],
        in_specs=[vmem] * 5 + [hbm] * 3,
        out_specs=[hbm, vmem],
        scratch_shapes=scratch,
        name="interval",
        cost_estimate=pl.CostEstimate(flops=10**9, bytes_accessed=10**8, transcendentals=0),
        compiler_params=pltpu.CompilerParams(
            collective_id=0, has_side_effects=True, vmem_limit_bytes=57 * 2**20),
    )(neighbors[0], edge_coef[0], sea_mask[None], pair_rows[0], sources, state[0], pair_cols, remap_weight[0])


def publish_kernel(parts, source, result, held, got, put):
    rows = source.shape[0] // parts

    def take(i):
        at = pl.ds(i * rows, rows)
        return pltpu.make_async_copy(source.at[at], held.at[at], got.at[i])

    def give(i):
        at = pl.ds(i * rows, rows)
        return pltpu.make_async_copy(held.at[at], result.at[at], put.at[i])
    for i in range(parts):
        take(i).start()
    for i in range(parts):
        take(i).wait()
        give(i).start()
    for i in range(parts):
        give(i).wait()


def publish(array, parts=4):
    hbm = pl.BlockSpec(memory_space=pltpu.HBM)
    return pl.pallas_call(
        functools.partial(publish_kernel, parts),
        out_shape=jax.ShapeDtypeStruct(array.shape, array.dtype),
        in_specs=[hbm],
        out_specs=hbm,
        scratch_shapes=[pltpu.VMEM(array.shape, array.dtype)] + [pltpu.SemaphoreType.DMA((parts,))] * 2,
        name="publish",
    )(array)


def local(state, neighbors, edge_coef, sea_mask, pair_source, pair_rows, pair_cols, remap_weight):
    sources = lax.optimization_barrier(pair_source.T)
    fast, flags = windowed(state, neighbors, edge_coef, sea_mask, pair_rows, pair_cols, remap_weight, sources)

    def anyway(_):
        return False, general(state, neighbors, edge_coef, sea_mask,
                              with_layout_constraint(sources, Layout((0, 1))).T, pair_rows, pair_cols, remap_weight)

    done = lax.while_loop(lambda c: c[0], anyway, (flags[0, 0] > 0, fast))
    return publish(done[1])[None]


def solution(mesh):
    placed = (
        P("comp", None, "dom"),
        P("comp", None, "dom"),
        P("comp", None, "dom"),
        P("dom"),
        P(),
        P("dom", None, None),
        P(),
        P("dom", None, None, None),
    )
    return jax.shard_map(
        local, mesh=mesh, in_specs=placed, out_specs=P("comp", None, "dom"), check_vma=False
    )
```

```python
import functools

import jax
import jax.numpy as jnp
from jax import lax
from jax.experimental import pallas as pl
from jax.experimental.layout import Layout, with_layout_constraint
from jax.experimental.pallas import tpu as pltpu
from jax.sharding import PartitionSpec as P

FIELDS = 4
RIM = 256
EDGES = 4
STEPS = 4
FORCE_GAIN = 0.5

LANES = 128
SUB = 8
NEAR = 2
NEAR_COUNT = 2 * NEAR + 1
CONE = 3
RING = 8
REACH = RING + CONE
EXTRAS = 4
MESH = pl.DeviceIdType.MESH
F32 = jnp.float32
BF16 = jnp.bfloat16


def with_halo(array, sides, width):
    for axis, dim in sides:
        devices, length = (lax.axis_size(axis), array.shape[dim])
        up = [(i, (i + 1) % devices) for i in range(devices)]
        down = [(j, i) for i, j in up]
        last = lax.slice_in_dim(array, length - width, length, axis=dim)
        leading = lax.slice_in_dim(array, 0, width, axis=dim)
        before = lax.ppermute(last, axis, up)
        after = lax.ppermute(leading, axis, down)
        array = jnp.concatenate([before, array, after], axis=dim)
    return array


def general(state, neighbors, edge_coef, sea_mask, pair_source, pair_rows, pair_cols, remap_weight):
    highest = lax.Precision.HIGHEST
    comp_count = lax.axis_size("comp")
    dom_count = lax.axis_size("dom")
    comp_id = lax.axis_index("comp")
    dom_id = lax.axis_index("dom")
    current = with_layout_constraint(state, Layout((0, 1, 2)))[0]
    fields = FIELDS
    column_count = current.shape[1]
    pair_count = pair_source.shape[1]
    block = pair_rows.shape[2]
    device_total = comp_count * dom_count
    is_ocean = comp_id == comp_count - 1
    myself = comp_id * dom_count + dom_id
    surface = current[:fields]
    pair_index = jnp.arange(pair_count, dtype=jnp.int32)
    matched = pair_source == myself
    partner = jnp.any(matched, axis=1)
    which_pair = jnp.sum(jnp.where(matched, pair_index[None, :], 0), axis=1)
    my_columns = jnp.sum(jnp.where(matched[:, :, None], pair_cols, 0), axis=1)
    handler_comp = jnp.full_like(which_pair, comp_count - 1)
    activity = jnp.where(is_ocean, 1.0, 0.0).astype(jnp.float32)
    rows_here = pair_rows[0]
    weights_here = remap_weight[0]
    own_sources = lax.dynamic_index_in_dim(pair_source, dom_id, 0, keepdims=False)
    sea_values = surface[:, rows_here]
    upward = jnp.einsum("qbj,fqb->fqj", weights_here, sea_values, precision=highest) * activity
    to_air = jnp.zeros((fields, device_total, block), jnp.float32).at[:, own_sources].add(upward)
    slot_index = handler_comp * dom_count + jnp.arange(dom_count, dtype=jnp.int32)
    air_values = surface[:, my_columns] * partner[None, :, None]
    to_sea = jnp.zeros((fields, device_total, block), jnp.float32).at[:, slot_index].add(air_values)
    got_sea, got_air = (
        lax.all_to_all(to_sea, ("comp", "dom"), split_axis=1, concat_axis=1, tiled=True),
        lax.all_to_all(to_air, ("comp", "dom"), split_axis=1, concat_axis=1, tiled=True),
    )
    incoming = got_sea[:, own_sources]
    downward = jnp.einsum("qbj,fqj->fqb", weights_here, incoming, precision=highest) * activity
    sea_force = jnp.zeros((fields, column_count), jnp.float32).at[:, rows_here].add(downward)
    arrived = got_air[:, slot_index] * partner[None, :, None]
    air_force = jnp.zeros((fields, column_count), jnp.float32).at[:, my_columns].add(arrived)
    forcing = jnp.where(is_ocean, sea_force, air_force)
    adjacency = neighbors[0]
    rates = edge_coef[0]
    evolving = jnp.logical_or(jnp.logical_not(is_ocean), sea_mask == 1)

    def advance(_, current):
        padded = with_halo(current, (("dom", 1),), RIM)
        updated = current
        for edge_number in range(EDGES):
            updated = updated + rates[edge_number] * (padded[:, adjacency[edge_number]] - current)
        updated = updated.at[:fields].add(FORCE_GAIN * (forcing - current[:fields]))
        return jnp.where(evolving[None, :], updated, current)

    return with_layout_constraint(lax.fori_loop(0, STEPS, advance, current), Layout((0, 1)))


def lane_gather(values, lanes):
    return jnp.take_along_axis(values, lanes, axis=1, mode="promise_in_bounds")


def interval_kernel(nd, nc, tiles, levels, block, pairs,
                    nbr, coef, mask, rows, sources, state_hbm, cols_hbm, w_hbm,
                    out, flag_out,
                    pb0, pb1, pb2, pb3, gx0, gx1, gx2, gx3, outb, outg, ix, cx, tabw, tab2,
                    cols, wbuf, compact, slots, gsl, zslots, usl, nslots, gnear, unear, sea, fpart, fgot, force,
                    tabv, tab, flag, pflag, flags_in, tab_sem, gsend, grecv,
                    load_sem, w_sem, cols_sem, out_sem,
                    hsend, hrecv, asend, arecv, usend, urecv, ssend, srecv, fsend, frecv):
    comp = lax.axis_index("comp")
    dom = lax.axis_index("dom")
    ocean = nc - 1
    bulk = levels - SUB
    pieces = block // (2 * LANES)
    halo = RIM // LANES
    pb = [pb0, pb1, pb2, pb3]
    gx = [gx0, gx1, gx2, gx3]
    left = lax.rem(dom + nd - 1, nd)
    right = lax.rem(dom + 1, nd)
    is_air = comp < ocean
    near_rel = [0, 1, 2, nd - 2, nd - 1]
    far_count = nd - NEAR_COUNT
    T_WHICH, T_SEL, T_EXT, T_VALID = 0, 1, 2, 2 + EXTRAS
    T_NEARP = 2 + 2 * EXTRAS
    T_EP = T_NEARP + NEAR_COUNT
    T_EVALID, T_ESRC = T_EP + 1, T_EP + 2

    def load_g(j):
        return pltpu.make_async_copy(state_hbm.at[pl.ds(0, SUB), pl.ds(j * LANES, LANES)], gx0.at[j + REACH], load_sem.at[0])

    def load_b(j):
        return pltpu.make_async_copy(state_hbm.at[pl.ds(SUB, bulk), pl.ds(j * LANES, LANES)], pb0.at[j + halo], load_sem.at[1])

    for j in range(tiles):
        load_g(j).start()
    cols_copy = pltpu.make_async_copy(cols_hbm, cols, cols_sem)
    cols_copy.start()
    for j in range(tiles):
        load_b(j).start()

    @pl.when(is_air)
    def _():
        for p in range(pairs):
            pltpu.make_async_copy(w_hbm.at[p], wbuf.at[p], w_sem).start()

    barrier = pltpu.get_barrier_semaphore()

    def greet(device):
        pl.semaphore_signal(barrier, inc=1, device_id=device, device_id_type=MESH)

    for c in range(1, nc):
        greet((lax.rem(comp + c, nc), dom))

    @pl.when(is_air)
    def _():
        def greet_plane(r, _):
            greet((comp, lax.rem(dom + r, nd)))
            return 0
        lax.fori_loop(1, nd, greet_plane, 0)

    @pl.when(jnp.logical_not(is_air))
    def _():
        greet((comp, left))
        greet((comp, right))

    def build_tables():
        src = sources[...].T
        p_i = lax.broadcasted_iota(jnp.int32, (nd, pairs), 1)
        t_i = lax.broadcasted_iota(jnp.int32, (nd, pairs), 0)
        t_c = lax.broadcasted_iota(jnp.int32, (nd, 1), 0)
        dom_f = dom
        base = (comp * nd)

        def is_far(offset):
            offset = jnp.where(offset < 0, offset + nd, offset)
            return jnp.logical_and(offset > NEAR, offset < nd - NEAR)

        mine = src == base + dom_f
        which = jnp.sum(jnp.where(mine, p_i, 0), axis=1, keepdims=True)
        hit = jnp.max(jnp.where(mine, 1, 0), axis=1, keepdims=True)
        far = jnp.where(jnp.logical_and(hit > 0, is_far(t_c - dom_f)), 1, 0)
        lanes = [(T_WHICH, which)]
        sel = jnp.zeros((nd, 1), jnp.int32)
        last = jnp.full((1, 1), -1, jnp.int32)
        for e in range(EXTRAS):
            last = jnp.min(jnp.where(jnp.logical_and(far > 0, t_c > last), t_c, nd), axis=0, keepdims=True)
            sel = jnp.where(t_c == last, e, sel)
            lanes.append((T_EXT + e, last))
            lanes.append((T_VALID + e, jnp.where(last < nd, 1, 0)))
        lanes.append((T_SEL, sel))
        crowded = jnp.sum(far, axis=0, keepdims=True) > EXTRAS

        own = jnp.sum(jnp.where(t_i == dom_f, src, 0), axis=0, keepdims=True) - base
        p_r = p_i[:1]
        for n, r in enumerate(near_rel):
            place = lax.rem(dom + r, nd)
            lanes.append((T_NEARP + n, jnp.sum(jnp.where(own == place, p_r, 0), axis=1, keepdims=True)))
        in_band = jnp.logical_and(own >= 0, own < nd)
        far_own = jnp.where(jnp.logical_and(in_band, is_far(own - dom_f)), 1, 0)
        lanes.append((T_EP, jnp.sum(far_own * p_r, axis=1, keepdims=True)))
        lanes.append((T_EVALID, jnp.max(far_own, axis=1, keepdims=True)))
        lanes.append((T_ESRC, jnp.sum(far_own * own, axis=1, keepdims=True)))
        lane = lax.broadcasted_iota(jnp.int32, (nd, LANES), 1)
        packed = jnp.zeros((nd, LANES), jnp.int32)
        for at, value in lanes:
            value = jnp.minimum(value, ((nd if at in (T_ESRC, *range(T_EXT, T_EXT + EXTRAS)) else pairs) - 1))
            packed = jnp.where(lane == at, jnp.broadcast_to(value, (nd, LANES)), packed)
        tabv[pl.ds(0, nd), :] = packed

        reach = jnp.concatenate(
            [nbr[:, j * LANES:(j + 1) * LANES] for j in range(tiles)], axis=0)
        lane = lax.broadcasted_iota(jnp.int32, reach.shape, 1)
        wide = jnp.zeros((1, 1), jnp.int32)
        stray = jnp.zeros((1, 1), jnp.int32)
        packed = jnp.zeros(reach.shape, jnp.int32)
        for h, side in enumerate((lane < LANES // 2, lane >= LANES // 2)):
            first = jnp.min(jnp.where(side, reach, 2**30), axis=1, keepdims=True)
            first = jnp.clip(first, 0, ((tiles + 2 * halo - 1) * LANES))
            final = jnp.max(jnp.where(side, reach, -1), axis=1, keepdims=True)
            wide = jnp.maximum(wide, jnp.max(final - first, axis=0, keepdims=True))
            packed = jnp.where(lane == h, jnp.broadcast_to(first, reach.shape), packed)
            tile = lax.broadcasted_iota(jnp.int32, first.shape, 0) // EDGES
            place = jnp.minimum(first >> 7, tiles + 2 * halo - 2)
            outside = jnp.logical_or(place < tile + halo - CONE, place + 1 > tile + halo + CONE)
            stray = jnp.maximum(stray, jnp.max(jnp.where(outside, 1, 0), axis=0, keepdims=True))
        tabv[pl.ds(nd, EDGES * tiles), :] = packed
        bad = jnp.logical_or(jnp.logical_or(wide >= LANES, stray > 0), crowded)
        mark = jnp.broadcast_to(jnp.where(bad, 1.0, 0.0), (SUB, LANES))
        flag[...] = mark

    build_tables()
    for j in range(tiles):
        at = pl.ds(j * LANES, LANES)
        ix[RING + j, pl.ds(0, EDGES), :] = nbr[:, at]
        cx[RING + j, pl.ds(0, EDGES), :] = coef[:, at]
        keep = jnp.logical_or(is_air, mask[:, at] == 1)
        cx[RING + j, pl.ds(EDGES, 1), :] = jnp.where(keep, 1.0, 0.0)
    to_smem = pltpu.make_async_copy(tabv, tab, tab_sem)
    to_smem.start()

    row8 = lax.broadcasted_iota(jnp.int32, (SUB, LANES), 0)

    def doubled(ref, offset):
        out = []
        for h in range(tiles):
            v = ref[h + offset]
            out.append(jnp.where(row8 < FIELDS, v, pltpu.roll(v, FIELDS, axis=0)))
        return out

    def gather_slot(table, index):
        res = []
        for q in range(0, block // LANES, 2):
            i0 = index[:, q * LANES:(q + 1) * LANES]
            i1 = index[:, (q + 1) * LANES:(q + 2) * LANES]
            i8 = jnp.where(row8 < FIELDS, jnp.broadcast_to(i0, (SUB, LANES)), jnp.broadcast_to(i1, (SUB, LANES)))
            lo = i8 & (LANES - 1)
            hi = i8 >> 7
            acc = lane_gather(table[0], lo)
            for h in range(1, tiles):
                acc = jnp.where(hi == h, lane_gather(table[h], lo), acc)
            res.append(acc)
        return res

    def split_rows(res):
        cols_ = []
        for acc in res:
            high = acc.astype(BF16).astype(F32)
            low = acc - high
            cols_.append(jnp.where(row8 < FIELDS, high, pltpu.roll(low, FIELDS, axis=0)))
            cols_.append(jnp.where(row8 < FIELDS, pltpu.roll(high, FIELDS, axis=0), low))
        return jnp.concatenate(cols_, axis=1)

    def scatter(eight, index):
        hi = jnp.broadcast_to(index >> 7, (SUB, block))
        lhs = jnp.concatenate([jnp.where(hi == h, eight, 0.0) for h in range(tiles)], axis=0).astype(BF16)
        lo = jnp.broadcast_to(index & (LANES - 1), (LANES, block))
        hot = jnp.where(lo == lax.broadcasted_iota(jnp.int32, (LANES, block), 0), 1.0, 0.0).astype(BF16)
        return lax.dot_general(lhs, hot, (((1,), (1,)), ((), ())), preferred_element_type=F32)

    def cols_of(t):
        return cols[t, pl.ds(tab[t, T_WHICH], 1), :]

    pltpu.make_async_copy(gx0.at[pl.ds(REACH, tiles)], gx0.at[pl.ds(REACH, tiles)], load_sem.at[0]).wait()
    cols_copy.wait()
    to_smem.wait()

    @pl.when(is_air)
    def _():
        table = doubled(gx0, REACH)

        def extra(e, _):
            res = gather_slot(table, cols_of(tab[0, T_EXT + e]))
            for i, acc in enumerate(res):
                compact[e, i] = acc
            return 0
        lax.fori_loop(0, EXTRAS, extra, 0)

        def fill(r, _):
            t = lax.rem(dom + r, nd)
            slots[r] = compact[tab[t, T_SEL]]
            return 0
        lax.fori_loop(NEAR + 1, nd - NEAR, fill, 0)

    @pl.when(is_air)
    def _():
        pl.semaphore_wait(barrier, nd + nc - 2)

    @pl.when(jnp.logical_not(is_air))
    def _():
        pl.semaphore_wait(barrier, nc + 1)

    def mirror(n):
        return near_rel.index((nd - near_rel[n]) % nd)

    def a_copy(r):
        return pltpu.make_async_remote_copy(
            src_ref=slots.at[r], dst_ref=gsl.at[dom], send_sem=asend.at[0], recv_sem=arecv.at[0],
            device_id=(comp, lax.rem(dom + r, nd)), device_id_type=MESH)

    def a_near(n):
        return pltpu.make_async_remote_copy(
            src_ref=nslots.at[n], dst_ref=gnear.at[mirror(n)], send_sem=asend.at[1], recv_sem=arecv.at[1],
            device_id=(comp, lax.rem(dom + near_rel[n], nd)), device_id_type=MESH)

    def halo_copies(ref, s, kind):
        to_left = pltpu.make_async_remote_copy(
            src_ref=ref.at[pl.ds(halo, halo)], dst_ref=ref.at[pl.ds(tiles + halo, halo)],
            send_sem=hsend.at[kind, s, 0], recv_sem=hrecv.at[kind, s, 0], device_id=(comp, left), device_id_type=MESH)
        to_right = pltpu.make_async_remote_copy(
            src_ref=ref.at[pl.ds(tiles, halo)], dst_ref=ref.at[pl.ds(0, halo)],
            send_sem=hsend.at[kind, s, 1], recv_sem=hrecv.at[kind, s, 1], device_id=(comp, right), device_id_type=MESH)
        return to_left, to_right

    def ring_copies(ref, width, i):
        to_left = pltpu.make_async_remote_copy(
            src_ref=ref.at[pl.ds(width, width)], dst_ref=ref.at[pl.ds(tiles + width, width)],
            send_sem=hsend.at[0, i, 0], recv_sem=hrecv.at[0, i, 0], device_id=(comp, left), device_id_type=MESH)
        to_right = pltpu.make_async_remote_copy(
            src_ref=ref.at[pl.ds(tiles, width)], dst_ref=ref.at[pl.ds(0, width)],
            send_sem=hsend.at[0, i, 1], recv_sem=hrecv.at[0, i, 1], device_id=(comp, right), device_id_type=MESH)
        return to_left, to_right

    early = [(gx0, REACH, 0), (ix, RING, 1), (cx, RING, 2)]

    def sea_copy(c):
        return pltpu.make_async_remote_copy(
            src_ref=gx0.at[pl.ds(REACH, tiles)], dst_ref=sea, send_sem=ssend, recv_sem=srecv,
            device_id=(c, dom), device_id_type=MESH)

    def sea_flag_copy(c):
        return pltpu.make_async_remote_copy(
            src_ref=flag, dst_ref=flags_in.at[ocean], send_sem=gsend.at[0], recv_sem=grecv.at[0],
            device_id=(c, dom), device_id_type=MESH)

    def plane_flag_copy(c):
        return pltpu.make_async_remote_copy(
            src_ref=pflag, dst_ref=flags_in.at[comp], send_sem=gsend.at[1], recv_sem=grecv.at[1],
            device_id=(lax.rem(comp + c, nc), dom), device_id_type=MESH)

    def arrived(ref, sem):
        pltpu.make_async_copy(ref, ref, sem).wait()

    @pl.when(jnp.logical_not(is_air))
    def _():
        for c in range(ocean):
            sea_copy(c).start()
        for c in range(ocean):
            sea_flag_copy(c).start()

    arrived(pb0.at[pl.ds(halo, tiles)], load_sem.at[1])
    for c in halo_copies(pb[0], 0, 1):
        c.start()

    @pl.when(is_air)
    def _():
        def send(r, _):
            a_copy(r).start()
            return 0
        lax.fori_loop(NEAR + 1, nd - NEAR, send, 0)
        table = doubled(gx0, REACH)
        for n, r in enumerate(near_rel):
            res = gather_slot(table, cols_of(lax.rem(dom + r, nd)))
            for i, acc in enumerate(res):
                if r == 0:
                    gnear[n, i] = acc
                else:
                    nslots[n, i] = acc
        for n in range(1, NEAR_COUNT):
            a_near(n).start()

    for ref, width, i in early:
        for c in ring_copies(ref, width, i):
            c.start()

    lane1 = lax.broadcasted_iota(jnp.int32, (1, LANES), 1)

    def tile_step(src, j, rows_):
        cols_j = pl.ds(pl.multiple_of(j * LANES, LANES), LANES)
        cur = src[j + halo]
        upd = cur
        low = jnp.broadcast_to(lane1 < LANES // 2, (rows_, LANES))
        for k in range(EDGES):
            lo = jnp.broadcast_to(nbr[pl.ds(k, 1), cols_j] & (LANES - 1), (rows_, LANES))
            got = []
            for h in range(2):
                w = tab[nd + j * EDGES + k, h]
                b = jnp.minimum(w >> 7, tiles + 2 * halo - 2)
                edge = jnp.broadcast_to(lane1 >= w - b * LANES, (rows_, LANES))
                got.append(lane_gather(jnp.where(edge, src[b], src[b + 1]), lo))
            upd = upd + coef[pl.ds(k, 1), cols_j] * (jnp.where(low, got[0], got[1]) - cur)
        keep = jnp.logical_or(is_air, mask[:, cols_j] == 1)
        return jnp.where(jnp.broadcast_to(keep, (rows_, LANES)), upd, cur)

    def put_tile(s, j, value):
        if s + 1 < STEPS:
            pb[s + 1][j + halo] = value
        else:
            outb[j] = value

    def bulk_tiles(s, js):
        new = [tile_step(pb[s], j, bulk) for j in js]
        for j, value in zip(js, new):
            put_tile(s, j, value)

    per = 4

    def bulk_inner(s, first, last):
        def body(i, _):
            start = halo + i * per
            bulk_tiles(s, [start + u for u in range(per)])
            return 0
        lax.fori_loop(first, last, body, 0)

    def bulk_edges(s):
        for c in halo_copies(pb[s], s, 1):
            c.wait()
        bulk_tiles(s, list(range(halo)) + list(range(tiles - halo, tiles)))
        if s + 1 < STEPS:
            for c in halo_copies(pb[s + 1], s + 1, 1):
                c.start()

    inner = (tiles - 2 * halo) // per

    def bulk_step(s):
        bulk_edges(s)
        bulk_inner(s, 0, inner)

    def ring_windows():
        for ref, width, i in early:
            for c in ring_copies(ref, width, i):
                c.wait()
        reach = jnp.concatenate([ix[t, pl.ds(0, EDGES), :] for t in range(tiles + 2 * RING)], axis=0)
        lane = lax.broadcasted_iota(jnp.int32, reach.shape, 1)
        packed = jnp.zeros(reach.shape, jnp.int32)
        for h, side in enumerate((lane < LANES // 2, lane >= LANES // 2)):
            first = jnp.min(jnp.where(side, reach, 2**30), axis=1, keepdims=True)
            first = jnp.clip(first, 0, (tiles + 2 * halo - 1) * LANES)
            packed = jnp.where(lane == h, jnp.broadcast_to(first, reach.shape), packed)
        tabw[...] = packed
        pltpu.make_async_copy(tabw, tab2, tab_sem).start()

    low8 = lane1 < LANES // 2
    gain8 = jnp.where(row8 < FIELDS, FORCE_GAIN, 0.0)

    def ring_tile(s, t):
        src = gx[s]
        cur = src[t + CONE]
        upd = cur
        shift = jnp.where(t < RING, -tiles, jnp.where(t >= RING + tiles, tiles, 0)) + (REACH - halo)
        for k in range(EDGES):
            lo = jnp.broadcast_to(ix[t, pl.ds(k, 1), :] & (LANES - 1), (SUB, LANES))
            got = []
            for h in range(2):
                w = tab2[t * EDGES + k, h]
                b = jnp.minimum(w >> 7, tiles + 2 * halo - 2)
                edge = jnp.broadcast_to(lane1 >= w - b * LANES, (SUB, LANES))
                at = jnp.clip(b + shift, 0, tiles + 2 * REACH - 2)
                got.append(lane_gather(jnp.where(edge, src[at], src[at + 1]), lo))
            upd = upd + cx[t, pl.ds(k, 1), :] * (jnp.where(low8, got[0], got[1]) - cur)
        upd = upd + gain8 * (force[t] - cur)
        return jnp.where(cx[t, pl.ds(EDGES, 1), :] > 0.5, upd, cur)

    def ring_step(s):
        spread = [RING, RING, RING // 2, 0][s]
        many = 8

        def body(i, _):
            first = RING - spread + i * many
            new = [ring_tile(s, first + u) for u in range(many)]
            for u in range(many):
                if s + 1 < STEPS:
                    gx[s + 1][first + u + CONE] = new[u]
                else:
                    outg[first + u - RING] = new[u]
            return 0
        lax.fori_loop(0, (tiles + 2 * spread) // many, body, 0)

    bulk_step(0)

    @pl.when(is_air)
    def _():
        arrived(sea, srecv)
        arrived(flag, grecv.at[0])
        pltpu.make_async_copy(w_hbm, wbuf, w_sem).wait()
        flag[...] = jnp.maximum(flag[...], flags_in[ocean])
        for n in range(NEAR_COUNT + 1):
            zslots[n, pieces] = flag[...]
        sea_table = doubled(sea, 0)

        def dense(p, slot):
            w = wbuf[p]
            wh = w.astype(BF16)
            wl = (w - wh.astype(F32)).astype(BF16)
            index = rows[pl.ds(p, 1), :]
            x = split_rows(slot).astype(BF16)
            v = split_rows(gather_slot(sea_table, index)).astype(BF16)
            dims = (((1,), (1,)), ((), ()))
            y = (lax.dot_general(x, wh, dims, preferred_element_type=F32)
                 + lax.dot_general(x, wl, dims, preferred_element_type=F32))
            z = jnp.dot(v, wh, preferred_element_type=F32) + jnp.dot(v, wl, preferred_element_type=F32)
            y = y[:FIELDS] + y[FIELDS:]
            z = z[:FIELDS] + z[FIELDS:]
            yh = y.astype(BF16).astype(F32)
            return jnp.concatenate([yh, y - yh], axis=0), z, index

        def put(ref, at, z):
            for q in range(block // LANES):
                ref[at, q // 2, pl.ds((q % 2) * FIELDS, FIELDS), :] = z[:, q * LANES:(q + 1) * LANES]

        def u_copy(r):
            return pltpu.make_async_remote_copy(
                src_ref=zslots.at[NEAR_COUNT], dst_ref=usl.at[dom], send_sem=usend.at[0], recv_sem=urecv.at[0],
                device_id=(comp, lax.rem(dom + r, nd)), device_id_type=MESH)

        def u_near(n):
            return pltpu.make_async_remote_copy(
                src_ref=zslots.at[n], dst_ref=unear.at[mirror(n)], send_sem=usend.at[1], recv_sem=urecv.at[1],
                device_id=(comp, lax.rem(dom + near_rel[n], nd)), device_id_type=MESH)

        def near_block(n):
            eight, z, index = dense(tab[0, T_NEARP + n], [gnear[n, i] for i in range(pieces)])
            if n == 0:
                put(unear, n, z)
            else:
                put(zslots, n, z)
                u_near(n).start()
            return scatter(eight, index)

        arrived(gnear.at[pl.ds(0, NEAR_COUNT - 1)], arecv.at[1])
        total = near_block(1)
        total = total + near_block(NEAR_COUNT - 1)

        arrived(gsl.at[pl.ds(0, far_count)], arecv.at[0])
        src = tab[0, T_ESRC]
        eight, z, index = dense(tab[0, T_EP], [gsl[src, i] for i in range(pieces)])
        put(zslots, NEAR_COUNT, z)

        def send(r, _):
            u_copy(r).start()
            return 0
        lax.fori_loop(NEAR + 1, nd - NEAR, send, 0)
        total = total + scatter(jnp.where(tab[0, T_EVALID] == 1, eight, 0.0), index)
        for n in range(2, NEAR_COUNT - 1):
            total = total + near_block(n)
        total = total + near_block(0)
        for h in range(tiles):
            part = total[h * SUB:(h + 1) * SUB]
            fpart[h] = part + pltpu.roll(part, FIELDS, axis=0)
        pltpu.make_async_remote_copy(
            src_ref=fpart, dst_ref=fgot.at[comp], send_sem=fsend, recv_sem=frecv,
            device_id=(ocean, dom), device_id_type=MESH).start()

    ring_windows()
    bulk_step(1)

    @pl.when(is_air)
    def _():
        arrived(unear.at[pl.ds(0, NEAR_COUNT - 1)], urecv.at[1])
        total = jnp.zeros((tiles * SUB, LANES), F32)
        plane = flag[...]
        for n, r in enumerate(near_rel):
            if r:
                plane = jnp.maximum(plane, unear[n, pieces])
            total = total + scatter(split_rows([unear[n, i] for i in range(pieces)]), cols_of(lax.rem(dom + r, nd)))
        arrived(usl.at[pl.ds(0, far_count)], urecv.at[0])
        for r in range(NEAR + 1, nd - NEAR):
            plane = jnp.maximum(plane, usl[lax.rem(dom + r, nd), pieces])
        pflag[...] = plane
        for e in range(EXTRAS):
            t = tab[0, T_EXT + e]
            eight = split_rows([usl[t, i] for i in range(pieces)])
            total = total + scatter(jnp.where(tab[0, T_VALID + e] == 1, eight, 0.0), cols_of(t))
        for h in range(tiles):
            part = total[h * SUB:(h + 1) * SUB]
            force[RING + h] = part + pltpu.roll(part, FIELDS, axis=0)

    @pl.when(jnp.logical_not(is_air))
    def _():
        pltpu.make_async_copy(fgot, fgot, frecv).wait()
        for h in range(tiles):
            force[RING + h] = fgot[0, h] + fgot[1, h] + fgot[2, h]

    def store_b(j):
        return pltpu.make_async_copy(outb.at[j], out.at[pl.ds(SUB, bulk), pl.ds(j * LANES, LANES)], out_sem.at[1])

    def store_g(j):
        return pltpu.make_async_copy(outg.at[j], out.at[pl.ds(0, SUB), pl.ds(j * LANES, LANES)], out_sem.at[0])

    for c in ring_copies(force, RING, 3):
        c.start()

    @pl.when(is_air)
    def _():
        for c in range(1, nc):
            plane_flag_copy(c).start()

    bulk_step(2)
    pltpu.make_async_copy(tabw, tab2, tab_sem).wait()
    for c in ring_copies(force, RING, 3):
        c.wait()
    for s in range(STEPS):
        ring_step(s)
    for j in range(tiles):
        store_g(j).start()
    bulk_step(3)

    for j in range(tiles):
        store_b(j).start()

    @pl.when(is_air)
    def _():
        arrived(flags_in.at[pl.ds(0, ocean - 1)], grecv.at[1])
        total = pflag[...]
        for c in range(ocean):
            total = jnp.maximum(total, jnp.where(comp == c, 0.0, flags_in[c]))
        flag_out[...] = total

    @pl.when(jnp.logical_not(is_air))
    def _():
        arrived(flags_in.at[pl.ds(0, ocean)], grecv.at[1])
        total = flags_in[0]
        for c in range(1, ocean):
            total = jnp.maximum(total, flags_in[c])
        flag_out[...] = total

    @pl.when(is_air)
    def _():
        arrived(slots.at[pl.ds(0, far_count)], asend.at[0])
        arrived(nslots.at[pl.ds(0, NEAR_COUNT - 1)], asend.at[1])
        arrived(usl.at[pl.ds(0, far_count)], usend.at[0])
        arrived(unear.at[pl.ds(0, NEAR_COUNT - 1)], usend.at[1])
        arrived(fpart, fsend)
        arrived(flags_in.at[pl.ds(0, ocean)], gsend.at[1])

    @pl.when(jnp.logical_not(is_air))
    def _():
        arrived(fgot, ssend)
        arrived(flags_in.at[pl.ds(0, ocean)], gsend.at[0])

    arrived(outb, out_sem.at[1])
    arrived(outg, out_sem.at[0])


def windowed(state, neighbors, edge_coef, sea_mask, pair_rows, pair_cols, remap_weight, sources):
    nd, nc = lax.axis_size("dom"), lax.axis_size("comp")
    _, levels, columns = state.shape
    tiles = columns // LANES
    padded = tiles + 2 * RIM // LANES
    ringed = tiles + 2 * RING
    pairs, block = pair_rows.shape[1:]
    pieces = block // (2 * LANES)
    bulk = levels - SUB
    vmem = pl.BlockSpec(memory_space=pltpu.VMEM)
    hbm = pl.BlockSpec(memory_space=pltpu.HBM)
    dma = pltpu.SemaphoreType.DMA
    scratch = (
        [pltpu.VMEM((padded, bulk, LANES), F32)] * STEPS
        + [pltpu.VMEM((tiles + 2 * REACH, SUB, LANES), F32)] * STEPS
        + [pltpu.VMEM((tiles, bulk, LANES), F32), pltpu.VMEM((tiles, SUB, LANES), F32)]
        + [pltpu.VMEM((ringed, SUB, LANES), jnp.int32), pltpu.VMEM((ringed, SUB, LANES), F32)]
        + [pltpu.VMEM((ringed * EDGES, LANES), jnp.int32), pltpu.SMEM((ringed * EDGES, LANES), jnp.int32)]
        + [
            pltpu.VMEM(pair_cols.shape, jnp.int32),
            pltpu.VMEM((pairs, block, block), F32),
            pltpu.VMEM((EXTRAS, pieces, SUB, LANES), F32),
            pltpu.VMEM((nd, pieces, SUB, LANES), F32),
            pltpu.VMEM((nd, pieces, SUB, LANES), F32),
            pltpu.VMEM((NEAR_COUNT + 1, pieces + 1, SUB, LANES), F32),
            pltpu.VMEM((nd, pieces + 1, SUB, LANES), F32),
            pltpu.VMEM((NEAR_COUNT, pieces, SUB, LANES), F32),
            pltpu.VMEM((NEAR_COUNT, pieces, SUB, LANES), F32),
            pltpu.VMEM((NEAR_COUNT, pieces + 1, SUB, LANES), F32),
            pltpu.VMEM((tiles, SUB, LANES), F32),
            pltpu.VMEM((tiles, SUB, LANES), F32),
            pltpu.VMEM((nc - 1, tiles, SUB, LANES), F32),
            pltpu.VMEM((ringed, SUB, LANES), F32),
        ]
        + [pltpu.VMEM((nd + EDGES * tiles, LANES), jnp.int32), pltpu.SMEM((nd + EDGES * tiles, LANES), jnp.int32)]
        + [pltpu.VMEM((SUB, LANES), F32)] * 2 + [pltpu.VMEM((nc, SUB, LANES), F32), dma, dma((2,)), dma((2,))]
        + [dma((2,)), dma, dma, dma((2,))]
        + [dma((2, STEPS, 2)), dma((2, STEPS, 2))]
        + [dma((2,))] * 4 + [dma] * 4
    )
    return pl.pallas_call(
        functools.partial(interval_kernel, nd, nc, tiles, levels, block, pairs),
        out_shape=[jax.ShapeDtypeStruct((levels, columns), F32), jax.ShapeDtypeStruct((SUB, LANES), F32)],
        in_specs=[vmem] * 5 + [hbm] * 3,
        out_specs=[hbm, vmem],
        scratch_shapes=scratch,
        name="interval",
        cost_estimate=pl.CostEstimate(flops=10**9, bytes_accessed=10**8, transcendentals=0),
        compiler_params=pltpu.CompilerParams(
            collective_id=0, has_side_effects=True, vmem_limit_bytes=57 * 2**20),
    )(neighbors[0], edge_coef[0], sea_mask[None], pair_rows[0], sources, state[0], pair_cols, remap_weight[0])


def publish_kernel(parts, source, result, held, got, put):
    rows = source.shape[0] // parts

    def take(i):
        at = pl.ds(i * rows, rows)
        return pltpu.make_async_copy(source.at[at], held.at[at], got.at[i])

    def give(i):
        at = pl.ds(i * rows, rows)
        return pltpu.make_async_copy(held.at[at], result.at[at], put.at[i])
    for i in range(parts):
        take(i).start()
    for i in range(parts):
        take(i).wait()
        give(i).start()
    for i in range(parts):
        give(i).wait()


def publish(array, parts=4):
    hbm = pl.BlockSpec(memory_space=pltpu.HBM)
    return pl.pallas_call(
        functools.partial(publish_kernel, parts),
        out_shape=jax.ShapeDtypeStruct(array.shape, array.dtype),
        in_specs=[hbm],
        out_specs=hbm,
        scratch_shapes=[pltpu.VMEM(array.shape, array.dtype)] + [pltpu.SemaphoreType.DMA((parts,))] * 2,
        name="publish",
    )(array)


def local(state, neighbors, edge_coef, sea_mask, pair_source, pair_rows, pair_cols, remap_weight):
    sources = lax.optimization_barrier(pair_source.T)
    fast, flags = windowed(state, neighbors, edge_coef, sea_mask, pair_rows, pair_cols, remap_weight, sources)

    def anyway(_):
        return False, general(state, neighbors, edge_coef, sea_mask,
                              with_layout_constraint(sources, Layout((0, 1))).T, pair_rows, pair_cols, remap_weight)

    done = lax.while_loop(lambda c: c[0], anyway, (flags[0, 0] > 0, fast))
    return publish(done[1])[None]


def solution(mesh):
    placed = (
        P("comp", None, "dom"),
        P("comp", None, "dom"),
        P("comp", None, "dom"),
        P("dom"),
        P(),
        P("dom", None, None),
        P(),
        P("dom", None, None, None),
    )
    return jax.shard_map(
        local, mesh=mesh, in_specs=placed, out_specs=P("comp", None, "dom"), check_vma=False
    )
```

```python
import functools

import jax
import jax.numpy as jnp
from jax import lax
from jax.experimental import pallas as pl
from jax.experimental.layout import Layout, with_layout_constraint
from jax.experimental.pallas import tpu as pltpu
from jax.sharding import PartitionSpec as P

FIELDS = 4
RIM = 256
EDGES = 4
STEPS = 4
FORCE_GAIN = 0.5

LANES = 128
SUB = 8
NEAR = 2
NEAR_COUNT = 2 * NEAR + 1
CONE = 3
RING = 8
REACH = RING + CONE
EXTRAS = 4
MESH = pl.DeviceIdType.MESH
F32 = jnp.float32
BF16 = jnp.bfloat16


def with_halo(array, sides, width):
    for axis, dim in sides:
        devices, length = (lax.axis_size(axis), array.shape[dim])
        up = [(i, (i + 1) % devices) for i in range(devices)]
        down = [(j, i) for i, j in up]
        last = lax.slice_in_dim(array, length - width, length, axis=dim)
        leading = lax.slice_in_dim(array, 0, width, axis=dim)
        before = lax.ppermute(last, axis, up)
        after = lax.ppermute(leading, axis, down)
        array = jnp.concatenate([before, array, after], axis=dim)
    return array


def general(state, neighbors, edge_coef, sea_mask, pair_source, pair_rows, pair_cols, remap_weight):
    highest = lax.Precision.HIGHEST
    comp_count = lax.axis_size("comp")
    dom_count = lax.axis_size("dom")
    comp_id = lax.axis_index("comp")
    dom_id = lax.axis_index("dom")
    current = with_layout_constraint(state, Layout((0, 1, 2)))[0]
    fields = FIELDS
    column_count = current.shape[1]
    pair_count = pair_source.shape[1]
    block = pair_rows.shape[2]
    device_total = comp_count * dom_count
    is_ocean = comp_id == comp_count - 1
    myself = comp_id * dom_count + dom_id
    surface = current[:fields]
    pair_index = jnp.arange(pair_count, dtype=jnp.int32)
    matched = pair_source == myself
    partner = jnp.any(matched, axis=1)
    which_pair = jnp.sum(jnp.where(matched, pair_index[None, :], 0), axis=1)
    my_columns = jnp.sum(jnp.where(matched[:, :, None], pair_cols, 0), axis=1)
    handler_comp = jnp.full_like(which_pair, comp_count - 1)
    activity = jnp.where(is_ocean, 1.0, 0.0).astype(jnp.float32)
    rows_here = pair_rows[0]
    weights_here = remap_weight[0]
    own_sources = lax.dynamic_index_in_dim(pair_source, dom_id, 0, keepdims=False)
    sea_values = surface[:, rows_here]
    upward = jnp.einsum("qbj,fqb->fqj", weights_here, sea_values, precision=highest) * activity
    to_air = jnp.zeros((fields, device_total, block), jnp.float32).at[:, own_sources].add(upward)
    slot_index = handler_comp * dom_count + jnp.arange(dom_count, dtype=jnp.int32)
    air_values = surface[:, my_columns] * partner[None, :, None]
    to_sea = jnp.zeros((fields, device_total, block), jnp.float32).at[:, slot_index].add(air_values)
    got_sea, got_air = (
        lax.all_to_all(to_sea, ("comp", "dom"), split_axis=1, concat_axis=1, tiled=True),
        lax.all_to_all(to_air, ("comp", "dom"), split_axis=1, concat_axis=1, tiled=True),
    )
    incoming = got_sea[:, own_sources]
    downward = jnp.einsum("qbj,fqj->fqb", weights_here, incoming, precision=highest) * activity
    sea_force = jnp.zeros((fields, column_count), jnp.float32).at[:, rows_here].add(downward)
    arrived = got_air[:, slot_index] * partner[None, :, None]
    air_force = jnp.zeros((fields, column_count), jnp.float32).at[:, my_columns].add(arrived)
    forcing = jnp.where(is_ocean, sea_force, air_force)
    adjacency = neighbors[0]
    rates = edge_coef[0]
    evolving = jnp.logical_or(jnp.logical_not(is_ocean), sea_mask == 1)

    def advance(_, current):
        padded = with_halo(current, (("dom", 1),), RIM)
        updated = current
        for edge_number in range(EDGES):
            updated = updated + rates[edge_number] * (padded[:, adjacency[edge_number]] - current)
        updated = updated.at[:fields].add(FORCE_GAIN * (forcing - current[:fields]))
        return jnp.where(evolving[None, :], updated, current)

    return with_layout_constraint(lax.fori_loop(0, STEPS, advance, current), Layout((0, 1)))


def lane_gather(values, lanes):
    return jnp.take_along_axis(values, lanes, axis=1, mode="promise_in_bounds")


def interval_kernel(nd, nc, tiles, levels, block, pairs,
                    nbr, coef, mask, rows, sources, state_hbm, cols_hbm, w_hbm,
                    out, flag_out,
                    pb0, pb1, pb2, pb3, gx0, gx1, gx2, gx3, outb, outg, ix, cx, tabw, tab2, blocksum,
                    cols, wbuf, compact, slots, gsl, zslots, usl, nslots, gnear, unear, sea, fpart, fgot, force,
                    tabv, tab, flag, pflag, flags_in, tab_sem, gsend, grecv,
                    load_sem, w_sem, cols_sem, out_sem,
                    hsend, hrecv, asend, arecv, usend, urecv, ssend, srecv, fsend, frecv):
    comp = lax.axis_index("comp")
    dom = lax.axis_index("dom")
    ocean = nc - 1
    bulk = levels - SUB
    pieces = block // (2 * LANES)
    halo = RIM // LANES
    pb = [pb0, pb1, pb2, pb3]
    gx = [gx0, gx1, gx2, gx3]
    left = lax.rem(dom + nd - 1, nd)
    right = lax.rem(dom + 1, nd)
    is_air = comp < ocean
    near_rel = [0, 1, 2, nd - 2, nd - 1]
    far_count = nd - NEAR_COUNT
    T_WHICH, T_SEL, T_EXT, T_VALID = 0, 1, 2, 2 + EXTRAS
    T_NEARP = 2 + 2 * EXTRAS
    T_EP = T_NEARP + NEAR_COUNT
    T_EVALID, T_ESRC = T_EP + 1, T_EP + 2

    def load_g(j):
        return pltpu.make_async_copy(state_hbm.at[pl.ds(0, SUB), pl.ds(j * LANES, LANES)], gx0.at[j + REACH], load_sem.at[0])

    def load_b(j):
        return pltpu.make_async_copy(state_hbm.at[pl.ds(SUB, bulk), pl.ds(j * LANES, LANES)], pb0.at[j + halo], load_sem.at[1])

    for j in range(tiles):
        load_g(j).start()
    cols_copy = pltpu.make_async_copy(cols_hbm, cols, cols_sem)
    cols_copy.start()
    for j in range(tiles):
        load_b(j).start()

    @pl.when(is_air)
    def _():
        for p in range(pairs):
            pltpu.make_async_copy(w_hbm.at[p], wbuf.at[p], w_sem).start()

    barrier = pltpu.get_barrier_semaphore()

    def greet(device):
        pl.semaphore_signal(barrier, inc=1, device_id=device, device_id_type=MESH)

    for c in range(1, nc):
        greet((lax.rem(comp + c, nc), dom))

    @pl.when(is_air)
    def _():
        def greet_plane(r, _):
            greet((comp, lax.rem(dom + r, nd)))
            return 0
        lax.fori_loop(1, nd, greet_plane, 0)

    @pl.when(jnp.logical_not(is_air))
    def _():
        greet((comp, left))
        greet((comp, right))

    def build_tables():
        src = sources[...].T
        p_i = lax.broadcasted_iota(jnp.int32, (nd, pairs), 1)
        t_i = lax.broadcasted_iota(jnp.int32, (nd, pairs), 0)
        t_c = lax.broadcasted_iota(jnp.int32, (nd, 1), 0)
        dom_f = dom
        base = (comp * nd)

        def is_far(offset):
            offset = jnp.where(offset < 0, offset + nd, offset)
            return jnp.logical_and(offset > NEAR, offset < nd - NEAR)

        mine = src == base + dom_f
        which = jnp.sum(jnp.where(mine, p_i, 0), axis=1, keepdims=True)
        hit = jnp.max(jnp.where(mine, 1, 0), axis=1, keepdims=True)
        far = jnp.where(jnp.logical_and(hit > 0, is_far(t_c - dom_f)), 1, 0)
        lanes = [(T_WHICH, which)]
        sel = jnp.zeros((nd, 1), jnp.int32)
        last = jnp.full((1, 1), -1, jnp.int32)
        for e in range(EXTRAS):
            last = jnp.min(jnp.where(jnp.logical_and(far > 0, t_c > last), t_c, nd), axis=0, keepdims=True)
            sel = jnp.where(t_c == last, e, sel)
            lanes.append((T_EXT + e, last))
            lanes.append((T_VALID + e, jnp.where(last < nd, 1, 0)))
        lanes.append((T_SEL, sel))
        crowded = jnp.sum(far, axis=0, keepdims=True) > EXTRAS

        own = jnp.sum(jnp.where(t_i == dom_f, src, 0), axis=0, keepdims=True) - base
        p_r = p_i[:1]
        for n, r in enumerate(near_rel):
            place = lax.rem(dom + r, nd)
            lanes.append((T_NEARP + n, jnp.sum(jnp.where(own == place, p_r, 0), axis=1, keepdims=True)))
        in_band = jnp.logical_and(own >= 0, own < nd)
        far_own = jnp.where(jnp.logical_and(in_band, is_far(own - dom_f)), 1, 0)
        lanes.append((T_EP, jnp.sum(far_own * p_r, axis=1, keepdims=True)))
        lanes.append((T_EVALID, jnp.max(far_own, axis=1, keepdims=True)))
        lanes.append((T_ESRC, jnp.sum(far_own * own, axis=1, keepdims=True)))
        lane = lax.broadcasted_iota(jnp.int32, (nd, LANES), 1)
        packed = jnp.zeros((nd, LANES), jnp.int32)
        for at, value in lanes:
            value = jnp.minimum(value, ((nd if at in (T_ESRC, *range(T_EXT, T_EXT + EXTRAS)) else pairs) - 1))
            packed = jnp.where(lane == at, jnp.broadcast_to(value, (nd, LANES)), packed)
        tabv[pl.ds(0, nd), :] = packed

        reach = jnp.concatenate(
            [nbr[:, j * LANES:(j + 1) * LANES] for j in range(tiles)], axis=0)
        lane = lax.broadcasted_iota(jnp.int32, reach.shape, 1)
        wide = jnp.zeros((1, 1), jnp.int32)
        stray = jnp.zeros((1, 1), jnp.int32)
        packed = jnp.zeros(reach.shape, jnp.int32)
        for h, side in enumerate((lane < LANES // 2, lane >= LANES // 2)):
            first = jnp.min(jnp.where(side, reach, 2**30), axis=1, keepdims=True)
            first = jnp.clip(first, 0, ((tiles + 2 * halo - 1) * LANES))
            final = jnp.max(jnp.where(side, reach, -1), axis=1, keepdims=True)
            wide = jnp.maximum(wide, jnp.max(final - first, axis=0, keepdims=True))
            packed = jnp.where(lane == h, jnp.broadcast_to(first, reach.shape), packed)
            tile = lax.broadcasted_iota(jnp.int32, first.shape, 0) // EDGES
            place = jnp.minimum(first >> 7, tiles + 2 * halo - 2)
            outside = jnp.logical_or(place < tile + halo - CONE, place + 1 > tile + halo + CONE)
            stray = jnp.maximum(stray, jnp.max(jnp.where(outside, 1, 0), axis=0, keepdims=True))
        tabv[pl.ds(nd, EDGES * tiles), :] = packed
        bad = jnp.logical_or(jnp.logical_or(wide >= LANES, stray > 0), crowded)
        mark = jnp.broadcast_to(jnp.where(bad, 1.0, 0.0), (SUB, LANES))
        flag[...] = mark

    build_tables()
    for j in range(tiles):
        at = pl.ds(j * LANES, LANES)
        ix[RING + j, pl.ds(0, EDGES), :] = nbr[:, at]
        cx[RING + j, pl.ds(0, EDGES), :] = coef[:, at]
        keep = jnp.logical_or(is_air, mask[:, at] == 1)
        cx[RING + j, pl.ds(EDGES, 1), :] = jnp.where(keep, 1.0, 0.0)
    to_smem = pltpu.make_async_copy(tabv, tab, tab_sem)
    to_smem.start()

    row8 = lax.broadcasted_iota(jnp.int32, (SUB, LANES), 0)

    def doubled(ref, offset):
        out = []
        for h in range(tiles):
            v = ref[h + offset]
            out.append(jnp.where(row8 < FIELDS, v, pltpu.roll(v, FIELDS, axis=0)))
        return out

    def gather_slot(table, index):
        res = []
        for q in range(0, block // LANES, 2):
            i0 = index[:, q * LANES:(q + 1) * LANES]
            i1 = index[:, (q + 1) * LANES:(q + 2) * LANES]
            i8 = jnp.where(row8 < FIELDS, jnp.broadcast_to(i0, (SUB, LANES)), jnp.broadcast_to(i1, (SUB, LANES)))
            lo = i8 & (LANES - 1)
            hi = i8 >> 7
            acc = lane_gather(table[0], lo)
            for h in range(1, tiles):
                acc = jnp.where(hi == h, lane_gather(table[h], lo), acc)
            res.append(acc)
        return res

    def split_rows(res):
        cols_ = []
        for acc in res:
            high = acc.astype(BF16).astype(F32)
            low = acc - high
            cols_.append(jnp.where(row8 < FIELDS, high, pltpu.roll(low, FIELDS, axis=0)))
            cols_.append(jnp.where(row8 < FIELDS, pltpu.roll(high, FIELDS, axis=0), low))
        return jnp.concatenate(cols_, axis=1)

    def scatter(eight, index):
        hi = jnp.broadcast_to(index >> 7, (SUB, block))
        lhs = jnp.concatenate([jnp.where(hi == h, eight, 0.0) for h in range(tiles)], axis=0).astype(BF16)
        lo = jnp.broadcast_to(index & (LANES - 1), (LANES, block))
        hot = jnp.where(lo == lax.broadcasted_iota(jnp.int32, (LANES, block), 0), 1.0, 0.0).astype(BF16)
        return lax.dot_general(lhs, hot, (((1,), (1,)), ((), ())), preferred_element_type=F32)

    def cols_of(t):
        return cols[t, pl.ds(tab[t, T_WHICH], 1), :]

    pltpu.make_async_copy(gx0.at[pl.ds(REACH, tiles)], gx0.at[pl.ds(REACH, tiles)], load_sem.at[0]).wait()
    cols_copy.wait()
    to_smem.wait()

    @pl.when(is_air)
    def _():
        table = doubled(gx0, REACH)

        def extra(e, _):
            res = gather_slot(table, cols_of(tab[0, T_EXT + e]))
            for i, acc in enumerate(res):
                compact[e, i] = acc
            return 0
        lax.fori_loop(0, EXTRAS, extra, 0)

        def fill(r, _):
            t = lax.rem(dom + r, nd)
            slots[r] = compact[tab[t, T_SEL]]
            return 0
        lax.fori_loop(NEAR + 1, nd - NEAR, fill, 0)

    @pl.when(is_air)
    def _():
        pl.semaphore_wait(barrier, nd + nc - 2)

    @pl.when(jnp.logical_not(is_air))
    def _():
        pl.semaphore_wait(barrier, nc + 1)

    def mirror(n):
        return near_rel.index((nd - near_rel[n]) % nd)

    def a_copy(r):
        return pltpu.make_async_remote_copy(
            src_ref=slots.at[r], dst_ref=gsl.at[dom], send_sem=asend.at[0], recv_sem=arecv.at[0],
            device_id=(comp, lax.rem(dom + r, nd)), device_id_type=MESH)

    def a_near(n):
        return pltpu.make_async_remote_copy(
            src_ref=nslots.at[n], dst_ref=gnear.at[mirror(n)], send_sem=asend.at[1], recv_sem=arecv.at[1],
            device_id=(comp, lax.rem(dom + near_rel[n], nd)), device_id_type=MESH)

    def halo_copies(ref, s, kind):
        to_left = pltpu.make_async_remote_copy(
            src_ref=ref.at[pl.ds(halo, halo)], dst_ref=ref.at[pl.ds(tiles + halo, halo)],
            send_sem=hsend.at[kind, s, 0], recv_sem=hrecv.at[kind, s, 0], device_id=(comp, left), device_id_type=MESH)
        to_right = pltpu.make_async_remote_copy(
            src_ref=ref.at[pl.ds(tiles, halo)], dst_ref=ref.at[pl.ds(0, halo)],
            send_sem=hsend.at[kind, s, 1], recv_sem=hrecv.at[kind, s, 1], device_id=(comp, right), device_id_type=MESH)
        return to_left, to_right

    def ring_copies(ref, width, i):
        to_left = pltpu.make_async_remote_copy(
            src_ref=ref.at[pl.ds(width, width)], dst_ref=ref.at[pl.ds(tiles + width, width)],
            send_sem=hsend.at[0, i, 0], recv_sem=hrecv.at[0, i, 0], device_id=(comp, left), device_id_type=MESH)
        to_right = pltpu.make_async_remote_copy(
            src_ref=ref.at[pl.ds(tiles, width)], dst_ref=ref.at[pl.ds(0, width)],
            send_sem=hsend.at[0, i, 1], recv_sem=hrecv.at[0, i, 1], device_id=(comp, right), device_id_type=MESH)
        return to_left, to_right

    early = [(gx0, REACH, 0), (ix, RING, 1), (cx, RING, 2)]

    def sea_copy(c):
        return pltpu.make_async_remote_copy(
            src_ref=gx0.at[pl.ds(REACH, tiles)], dst_ref=sea, send_sem=ssend, recv_sem=srecv,
            device_id=(c, dom), device_id_type=MESH)

    def sea_flag_copy(c):
        return pltpu.make_async_remote_copy(
            src_ref=flag, dst_ref=flags_in.at[ocean], send_sem=gsend.at[0], recv_sem=grecv.at[0],
            device_id=(c, dom), device_id_type=MESH)

    def plane_flag_copy(c):
        return pltpu.make_async_remote_copy(
            src_ref=pflag, dst_ref=flags_in.at[comp], send_sem=gsend.at[1], recv_sem=grecv.at[1],
            device_id=(lax.rem(comp + c, nc), dom), device_id_type=MESH)

    def arrived(ref, sem):
        pltpu.make_async_copy(ref, ref, sem).wait()

    @pl.when(jnp.logical_not(is_air))
    def _():
        for c in range(ocean):
            sea_copy(c).start()
        for c in range(ocean):
            sea_flag_copy(c).start()

    arrived(pb0.at[pl.ds(halo, tiles)], load_sem.at[1])
    for c in halo_copies(pb[0], 0, 1):
        c.start()

    @pl.when(is_air)
    def _():
        def send(r, _):
            a_copy(r).start()
            return 0
        lax.fori_loop(NEAR + 1, nd - NEAR, send, 0)
        table = doubled(gx0, REACH)
        for n, r in enumerate(near_rel):
            res = gather_slot(table, cols_of(lax.rem(dom + r, nd)))
            for i, acc in enumerate(res):
                if r == 0:
                    gnear[n, i] = acc
                else:
                    nslots[n, i] = acc
        for n in range(1, NEAR_COUNT):
            a_near(n).start()

    for ref, width, i in early:
        for c in ring_copies(ref, width, i):
            c.start()

    lane1 = lax.broadcasted_iota(jnp.int32, (1, LANES), 1)

    def tile_step(src, j, rows_):
        cols_j = pl.ds(pl.multiple_of(j * LANES, LANES), LANES)
        cur = src[j + halo]
        upd = cur
        low = jnp.broadcast_to(lane1 < LANES // 2, (rows_, LANES))
        for k in range(EDGES):
            lo = jnp.broadcast_to(nbr[pl.ds(k, 1), cols_j] & (LANES - 1), (rows_, LANES))
            got = []
            for h in range(2):
                w = tab[nd + j * EDGES + k, h]
                b = jnp.minimum(w >> 7, tiles + 2 * halo - 2)
                edge = jnp.broadcast_to(lane1 >= w - b * LANES, (rows_, LANES))
                got.append(lane_gather(jnp.where(edge, src[b], src[b + 1]), lo))
            upd = upd + coef[pl.ds(k, 1), cols_j] * (jnp.where(low, got[0], got[1]) - cur)
        keep = jnp.logical_or(is_air, mask[:, cols_j] == 1)
        return jnp.where(jnp.broadcast_to(keep, (rows_, LANES)), upd, cur)

    def put_tile(s, j, value):
        if s + 1 < STEPS:
            pb[s + 1][j + halo] = value
        else:
            outb[j] = value

    def bulk_tiles(s, js):
        new = [tile_step(pb[s], j, bulk) for j in js]
        for j, value in zip(js, new):
            put_tile(s, j, value)

    per = 4

    def bulk_inner(s, first, last):
        def body(i, _):
            start = halo + i * per
            bulk_tiles(s, [start + u for u in range(per)])
            return 0
        lax.fori_loop(first, last, body, 0)

    def bulk_edges(s):
        for c in halo_copies(pb[s], s, 1):
            c.wait()
        bulk_tiles(s, list(range(halo)) + list(range(tiles - halo, tiles)))
        if s + 1 < STEPS:
            for c in halo_copies(pb[s + 1], s + 1, 1):
                c.start()

    inner = (tiles - 2 * halo) // per

    def bulk_step(s):
        bulk_edges(s)
        bulk_inner(s, 0, inner)

    def ring_windows():
        for ref, width, i in early:
            for c in ring_copies(ref, width, i):
                c.wait()
        reach = jnp.concatenate([ix[t, pl.ds(0, EDGES), :] for t in range(tiles + 2 * RING)], axis=0)
        lane = lax.broadcasted_iota(jnp.int32, reach.shape, 1)
        packed = jnp.zeros(reach.shape, jnp.int32)
        for h, side in enumerate((lane < LANES // 2, lane >= LANES // 2)):
            first = jnp.min(jnp.where(side, reach, 2**30), axis=1, keepdims=True)
            first = jnp.clip(first, 0, (tiles + 2 * halo - 1) * LANES)
            packed = jnp.where(lane == h, jnp.broadcast_to(first, reach.shape), packed)
        tabw[...] = packed
        pltpu.make_async_copy(tabw, tab2, tab_sem).start()

    low8 = lane1 < LANES // 2
    gain8 = jnp.where(row8 < FIELDS, FORCE_GAIN, 0.0)

    def ring_tile(s, t):
        src = gx[s]
        cur = src[t + CONE]
        upd = cur
        shift = jnp.where(t < RING, -tiles, jnp.where(t >= RING + tiles, tiles, 0)) + (REACH - halo)
        for k in range(EDGES):
            lo = jnp.broadcast_to(ix[t, pl.ds(k, 1), :] & (LANES - 1), (SUB, LANES))
            got = []
            for h in range(2):
                w = tab2[t * EDGES + k, h]
                b = jnp.minimum(w >> 7, tiles + 2 * halo - 2)
                edge = jnp.broadcast_to(lane1 >= w - b * LANES, (SUB, LANES))
                at = jnp.clip(b + shift, 0, tiles + 2 * REACH - 2)
                got.append(lane_gather(jnp.where(edge, src[at], src[at + 1]), lo))
            upd = upd + cx[t, pl.ds(k, 1), :] * (jnp.where(low8, got[0], got[1]) - cur)
        upd = upd + gain8 * (force[t] - cur)
        return jnp.where(cx[t, pl.ds(EDGES, 1), :] > 0.5, upd, cur)

    def ring_step(s):
        spread = [RING, RING, RING // 2, 0][s]
        many = 8

        def body(i, _):
            first = RING - spread + i * many
            new = [ring_tile(s, first + u) for u in range(many)]
            for u in range(many):
                if s + 1 < STEPS:
                    gx[s + 1][first + u + CONE] = new[u]
                else:
                    outg[first + u - RING] = new[u]
            return 0
        lax.fori_loop(0, (tiles + 2 * spread) // many, body, 0)

    bulk_step(0)

    def air_blocks(part):
        if part == 0:
            arrived(sea, srecv)
            arrived(flag, grecv.at[0])
            pltpu.make_async_copy(w_hbm, wbuf, w_sem).wait()
            flag[...] = jnp.maximum(flag[...], flags_in[ocean])
            for n in range(NEAR_COUNT + 1):
                zslots[n, pieces] = flag[...]
        sea_table = doubled(sea, 0)

        def dense(p, slot):
            w = wbuf[p]
            wh = w.astype(BF16)
            wl = (w - wh.astype(F32)).astype(BF16)
            index = rows[pl.ds(p, 1), :]
            x = split_rows(slot).astype(BF16)
            v = split_rows(gather_slot(sea_table, index)).astype(BF16)
            dims = (((1,), (1,)), ((), ()))
            y = (lax.dot_general(x, wh, dims, preferred_element_type=F32)
                 + lax.dot_general(x, wl, dims, preferred_element_type=F32))
            z = jnp.dot(v, wh, preferred_element_type=F32) + jnp.dot(v, wl, preferred_element_type=F32)
            y = y[:FIELDS] + y[FIELDS:]
            z = z[:FIELDS] + z[FIELDS:]
            yh = y.astype(BF16).astype(F32)
            return jnp.concatenate([yh, y - yh], axis=0), z, index

        def put(ref, at, z):
            for q in range(block // LANES):
                ref[at, q // 2, pl.ds((q % 2) * FIELDS, FIELDS), :] = z[:, q * LANES:(q + 1) * LANES]

        def u_copy(r):
            return pltpu.make_async_remote_copy(
                src_ref=zslots.at[NEAR_COUNT], dst_ref=usl.at[dom], send_sem=usend.at[0], recv_sem=urecv.at[0],
                device_id=(comp, lax.rem(dom + r, nd)), device_id_type=MESH)

        def u_near(n):
            return pltpu.make_async_remote_copy(
                src_ref=zslots.at[n], dst_ref=unear.at[mirror(n)], send_sem=usend.at[1], recv_sem=urecv.at[1],
                device_id=(comp, lax.rem(dom + near_rel[n], nd)), device_id_type=MESH)

        def near_block(n):
            eight, z, index = dense(tab[0, T_NEARP + n], [gnear[n, i] for i in range(pieces)])
            if n == 0:
                put(unear, n, z)
            else:
                put(zslots, n, z)
                u_near(n).start()
            return scatter(eight, index)

        if part == 0:
            arrived(gnear.at[pl.ds(0, NEAR_COUNT - 1)], arecv.at[1])
            total = near_block(1)
            total = total + near_block(NEAR_COUNT - 1)

            arrived(gsl.at[pl.ds(0, far_count)], arecv.at[0])
            src = tab[0, T_ESRC]
            eight, z, index = dense(tab[0, T_EP], [gsl[src, i] for i in range(pieces)])
            put(zslots, NEAR_COUNT, z)

            def send(r, _):
                u_copy(r).start()
                return 0
            lax.fori_loop(NEAR + 1, nd - NEAR, send, 0)
            blocksum[...] = total + scatter(jnp.where(tab[0, T_EVALID] == 1, eight, 0.0), index)
            return
        total = blocksum[...]
        for n in range(2, NEAR_COUNT - 1):
            total = total + near_block(n)
        total = total + near_block(0)
        for h in range(tiles):
            part_h = total[h * SUB:(h + 1) * SUB]
            fpart[h] = part_h + pltpu.roll(part_h, FIELDS, axis=0)
        pltpu.make_async_remote_copy(
            src_ref=fpart, dst_ref=fgot.at[comp], send_sem=fsend, recv_sem=frecv,
            device_id=(ocean, dom), device_id_type=MESH).start()

    @pl.when(is_air)
    def _():
        air_blocks(0)

    bulk_edges(1)

    @pl.when(is_air)
    def _():
        air_blocks(1)

    ring_windows()
    bulk_inner(1, 0, inner)
    bulk_edges(2)

    @pl.when(is_air)
    def _():
        arrived(unear.at[pl.ds(0, NEAR_COUNT - 1)], urecv.at[1])
        total = jnp.zeros((tiles * SUB, LANES), F32)
        plane = flag[...]
        for n, r in enumerate(near_rel):
            if r:
                plane = jnp.maximum(plane, unear[n, pieces])
            total = total + scatter(split_rows([unear[n, i] for i in range(pieces)]), cols_of(lax.rem(dom + r, nd)))
        arrived(usl.at[pl.ds(0, far_count)], urecv.at[0])
        for r in range(NEAR + 1, nd - NEAR):
            plane = jnp.maximum(plane, usl[lax.rem(dom + r, nd), pieces])
        pflag[...] = plane
        for e in range(EXTRAS):
            t = tab[0, T_EXT + e]
            eight = split_rows([usl[t, i] for i in range(pieces)])
            total = total + scatter(jnp.where(tab[0, T_VALID + e] == 1, eight, 0.0), cols_of(t))
        for h in range(tiles):
            part = total[h * SUB:(h + 1) * SUB]
            force[RING + h] = part + pltpu.roll(part, FIELDS, axis=0)

    @pl.when(jnp.logical_not(is_air))
    def _():
        pltpu.make_async_copy(fgot, fgot, frecv).wait()
        for h in range(tiles):
            force[RING + h] = fgot[0, h] + fgot[1, h] + fgot[2, h]

    def store_b(j):
        return pltpu.make_async_copy(outb.at[j], out.at[pl.ds(SUB, bulk), pl.ds(j * LANES, LANES)], out_sem.at[1])

    def store_g(j):
        return pltpu.make_async_copy(outg.at[j], out.at[pl.ds(0, SUB), pl.ds(j * LANES, LANES)], out_sem.at[0])

    for c in ring_copies(force, RING, 3):
        c.start()

    @pl.when(is_air)
    def _():
        for c in range(1, nc):
            plane_flag_copy(c).start()

    bulk_inner(2, 0, inner)
    bulk_edges(3)
    pltpu.make_async_copy(tabw, tab2, tab_sem).wait()
    for c in ring_copies(force, RING, 3):
        c.wait()
    for s in range(STEPS):
        ring_step(s)
    for j in range(tiles):
        store_g(j).start()
    bulk_inner(3, 0, inner)

    for j in range(tiles):
        store_b(j).start()

    @pl.when(is_air)
    def _():
        arrived(flags_in.at[pl.ds(0, ocean - 1)], grecv.at[1])
        total = pflag[...]
        for c in range(ocean):
            total = jnp.maximum(total, jnp.where(comp == c, 0.0, flags_in[c]))
        flag_out[...] = total

    @pl.when(jnp.logical_not(is_air))
    def _():
        arrived(flags_in.at[pl.ds(0, ocean)], grecv.at[1])
        total = flags_in[0]
        for c in range(1, ocean):
            total = jnp.maximum(total, flags_in[c])
        flag_out[...] = total

    @pl.when(is_air)
    def _():
        arrived(slots.at[pl.ds(0, far_count)], asend.at[0])
        arrived(nslots.at[pl.ds(0, NEAR_COUNT - 1)], asend.at[1])
        arrived(usl.at[pl.ds(0, far_count)], usend.at[0])
        arrived(unear.at[pl.ds(0, NEAR_COUNT - 1)], usend.at[1])
        arrived(fpart, fsend)
        arrived(flags_in.at[pl.ds(0, ocean)], gsend.at[1])

    @pl.when(jnp.logical_not(is_air))
    def _():
        arrived(fgot, ssend)
        arrived(flags_in.at[pl.ds(0, ocean)], gsend.at[0])

    arrived(outb, out_sem.at[1])
    arrived(outg, out_sem.at[0])


def windowed(state, neighbors, edge_coef, sea_mask, pair_rows, pair_cols, remap_weight, sources):
    nd, nc = lax.axis_size("dom"), lax.axis_size("comp")
    _, levels, columns = state.shape
    tiles = columns // LANES
    padded = tiles + 2 * RIM // LANES
    ringed = tiles + 2 * RING
    pairs, block = pair_rows.shape[1:]
    pieces = block // (2 * LANES)
    bulk = levels - SUB
    vmem = pl.BlockSpec(memory_space=pltpu.VMEM)
    hbm = pl.BlockSpec(memory_space=pltpu.HBM)
    dma = pltpu.SemaphoreType.DMA
    scratch = (
        [pltpu.VMEM((padded, bulk, LANES), F32)] * STEPS
        + [pltpu.VMEM((tiles + 2 * REACH, SUB, LANES), F32)] * STEPS
        + [pltpu.VMEM((tiles, bulk, LANES), F32), pltpu.VMEM((tiles, SUB, LANES), F32)]
        + [pltpu.VMEM((ringed, SUB, LANES), jnp.int32), pltpu.VMEM((ringed, SUB, LANES), F32)]
        + [pltpu.VMEM((ringed * EDGES, LANES), jnp.int32), pltpu.SMEM((ringed * EDGES, LANES), jnp.int32)]
        + [pltpu.VMEM((tiles * SUB, LANES), F32)]
        + [
            pltpu.VMEM(pair_cols.shape, jnp.int32),
            pltpu.VMEM((pairs, block, block), F32),
            pltpu.VMEM((EXTRAS, pieces, SUB, LANES), F32),
            pltpu.VMEM((nd, pieces, SUB, LANES), F32),
            pltpu.VMEM((nd, pieces, SUB, LANES), F32),
            pltpu.VMEM((NEAR_COUNT + 1, pieces + 1, SUB, LANES), F32),
            pltpu.VMEM((nd, pieces + 1, SUB, LANES), F32),
            pltpu.VMEM((NEAR_COUNT, pieces, SUB, LANES), F32),
            pltpu.VMEM((NEAR_COUNT, pieces, SUB, LANES), F32),
            pltpu.VMEM((NEAR_COUNT, pieces + 1, SUB, LANES), F32),
            pltpu.VMEM((tiles, SUB, LANES), F32),
            pltpu.VMEM((tiles, SUB, LANES), F32),
            pltpu.VMEM((nc - 1, tiles, SUB, LANES), F32),
            pltpu.VMEM((ringed, SUB, LANES), F32),
        ]
        + [pltpu.VMEM((nd + EDGES * tiles, LANES), jnp.int32), pltpu.SMEM((nd + EDGES * tiles, LANES), jnp.int32)]
        + [pltpu.VMEM((SUB, LANES), F32)] * 2 + [pltpu.VMEM((nc, SUB, LANES), F32), dma, dma((2,)), dma((2,))]
        + [dma((2,)), dma, dma, dma((2,))]
        + [dma((2, STEPS, 2)), dma((2, STEPS, 2))]
        + [dma((2,))] * 4 + [dma] * 4
    )
    return pl.pallas_call(
        functools.partial(interval_kernel, nd, nc, tiles, levels, block, pairs),
        out_shape=[jax.ShapeDtypeStruct((levels, columns), F32), jax.ShapeDtypeStruct((SUB, LANES), F32)],
        in_specs=[vmem] * 5 + [hbm] * 3,
        out_specs=[hbm, vmem],
        scratch_shapes=scratch,
        name="interval",
        cost_estimate=pl.CostEstimate(flops=10**9, bytes_accessed=10**8, transcendentals=0),
        compiler_params=pltpu.CompilerParams(
            collective_id=0, has_side_effects=True, vmem_limit_bytes=57 * 2**20),
    )(neighbors[0], edge_coef[0], sea_mask[None], pair_rows[0], sources, state[0], pair_cols, remap_weight[0])


def publish_kernel(parts, source, result, held, got, put):
    rows = source.shape[0] // parts

    def take(i):
        at = pl.ds(i * rows, rows)
        return pltpu.make_async_copy(source.at[at], held.at[at], got.at[i])

    def give(i):
        at = pl.ds(i * rows, rows)
        return pltpu.make_async_copy(held.at[at], result.at[at], put.at[i])
    for i in range(parts):
        take(i).start()
    for i in range(parts):
        take(i).wait()
        give(i).start()
    for i in range(parts):
        give(i).wait()


def publish(array, parts=4):
    hbm = pl.BlockSpec(memory_space=pltpu.HBM)
    return pl.pallas_call(
        functools.partial(publish_kernel, parts),
        out_shape=jax.ShapeDtypeStruct(array.shape, array.dtype),
        in_specs=[hbm],
        out_specs=hbm,
        scratch_shapes=[pltpu.VMEM(array.shape, array.dtype)] + [pltpu.SemaphoreType.DMA((parts,))] * 2,
        name="publish",
    )(array)


def local(state, neighbors, edge_coef, sea_mask, pair_source, pair_rows, pair_cols, remap_weight):
    sources = lax.optimization_barrier(pair_source.T)
    fast, flags = windowed(state, neighbors, edge_coef, sea_mask, pair_rows, pair_cols, remap_weight, sources)

    def anyway(_):
        return False, general(state, neighbors, edge_coef, sea_mask,
                              with_layout_constraint(sources, Layout((0, 1))).T, pair_rows, pair_cols, remap_weight)

    done = lax.while_loop(lambda c: c[0], anyway, (flags[0, 0] > 0, fast))
    return publish(done[1])[None]


def solution(mesh):
    placed = (
        P("comp", None, "dom"),
        P("comp", None, "dom"),
        P("comp", None, "dom"),
        P("dom"),
        P(),
        P("dom", None, None),
        P(),
        P("dom", None, None, None),
    )
    return jax.shard_map(
        local, mesh=mesh, in_specs=placed, out_specs=P("comp", None, "dom"), check_vma=False
    )
```

```python
import functools

import jax
import jax.numpy as jnp
from jax import lax
from jax.experimental import pallas as pl
from jax.experimental.layout import Layout, with_layout_constraint
from jax.experimental.pallas import tpu as pltpu
from jax.sharding import PartitionSpec as P

FIELDS = 4
RIM = 256
EDGES = 4
STEPS = 4
FORCE_GAIN = 0.5

LANES = 128
SUB = 8
NEAR = 2
NEAR_COUNT = 2 * NEAR + 1
CONE = 3
RING = 8
REACH = RING + CONE
EXTRAS = 4
MESH = pl.DeviceIdType.MESH
F32 = jnp.float32
BF16 = jnp.bfloat16


def with_halo(array, sides, width):
    for axis, dim in sides:
        devices, length = (lax.axis_size(axis), array.shape[dim])
        up = [(i, (i + 1) % devices) for i in range(devices)]
        down = [(j, i) for i, j in up]
        last = lax.slice_in_dim(array, length - width, length, axis=dim)
        leading = lax.slice_in_dim(array, 0, width, axis=dim)
        before = lax.ppermute(last, axis, up)
        after = lax.ppermute(leading, axis, down)
        array = jnp.concatenate([before, array, after], axis=dim)
    return array


def general(state, neighbors, edge_coef, sea_mask, pair_source, pair_rows, pair_cols, remap_weight):
    highest = lax.Precision.HIGHEST
    comp_count = lax.axis_size("comp")
    dom_count = lax.axis_size("dom")
    comp_id = lax.axis_index("comp")
    dom_id = lax.axis_index("dom")
    current = with_layout_constraint(state, Layout((0, 1, 2)))[0]
    fields = FIELDS
    column_count = current.shape[1]
    pair_count = pair_source.shape[1]
    block = pair_rows.shape[2]
    device_total = comp_count * dom_count
    is_ocean = comp_id == comp_count - 1
    myself = comp_id * dom_count + dom_id
    surface = current[:fields]
    pair_index = jnp.arange(pair_count, dtype=jnp.int32)
    matched = pair_source == myself
    partner = jnp.any(matched, axis=1)
    which_pair = jnp.sum(jnp.where(matched, pair_index[None, :], 0), axis=1)
    my_columns = jnp.sum(jnp.where(matched[:, :, None], pair_cols, 0), axis=1)
    handler_comp = jnp.full_like(which_pair, comp_count - 1)
    activity = jnp.where(is_ocean, 1.0, 0.0).astype(jnp.float32)
    rows_here = pair_rows[0]
    weights_here = remap_weight[0]
    own_sources = lax.dynamic_index_in_dim(pair_source, dom_id, 0, keepdims=False)
    sea_values = surface[:, rows_here]
    upward = jnp.einsum("qbj,fqb->fqj", weights_here, sea_values, precision=highest) * activity
    to_air = jnp.zeros((fields, device_total, block), jnp.float32).at[:, own_sources].add(upward)
    slot_index = handler_comp * dom_count + jnp.arange(dom_count, dtype=jnp.int32)
    air_values = surface[:, my_columns] * partner[None, :, None]
    to_sea = jnp.zeros((fields, device_total, block), jnp.float32).at[:, slot_index].add(air_values)
    got_sea, got_air = (
        lax.all_to_all(to_sea, ("comp", "dom"), split_axis=1, concat_axis=1, tiled=True),
        lax.all_to_all(to_air, ("comp", "dom"), split_axis=1, concat_axis=1, tiled=True),
    )
    incoming = got_sea[:, own_sources]
    downward = jnp.einsum("qbj,fqj->fqb", weights_here, incoming, precision=highest) * activity
    sea_force = jnp.zeros((fields, column_count), jnp.float32).at[:, rows_here].add(downward)
    arrived = got_air[:, slot_index] * partner[None, :, None]
    air_force = jnp.zeros((fields, column_count), jnp.float32).at[:, my_columns].add(arrived)
    forcing = jnp.where(is_ocean, sea_force, air_force)
    adjacency = neighbors[0]
    rates = edge_coef[0]
    evolving = jnp.logical_or(jnp.logical_not(is_ocean), sea_mask == 1)

    def advance(_, current):
        padded = with_halo(current, (("dom", 1),), RIM)
        updated = current
        for edge_number in range(EDGES):
            updated = updated + rates[edge_number] * (padded[:, adjacency[edge_number]] - current)
        updated = updated.at[:fields].add(FORCE_GAIN * (forcing - current[:fields]))
        return jnp.where(evolving[None, :], updated, current)

    return with_layout_constraint(lax.fori_loop(0, STEPS, advance, current), Layout((0, 1)))


def lane_gather(values, lanes):
    return jnp.take_along_axis(values, lanes, axis=1, mode="promise_in_bounds")


def interval_kernel(nd, nc, tiles, levels, block, pairs,
                    nbr, coef, mask, rows, sources, state_hbm, cols_hbm, w_hbm,
                    out, flag_out,
                    pb0, pb1, pb2, pb3, gx0, gx1, gx2, gx3, outb, outg, ix, cx, tabw, tab2,
                    cols, wbuf, compact, slots, gsl, zslots, usl, nslots, gnear, unear, sea, fpart, fgot, force,
                    tabv, tab, flag, pflag, flags_in, tab_sem, gsend, grecv,
                    load_sem, w_sem, cols_sem, out_sem,
                    hsend, hrecv, asend, arecv, usend, urecv, ssend, srecv, fsend, frecv):
    comp = lax.axis_index("comp")
    dom = lax.axis_index("dom")
    ocean = nc - 1
    bulk = levels - SUB
    pieces = block // (2 * LANES)
    halo = RIM // LANES
    pb = [pb0, pb1, pb2, pb3]
    gx = [gx0, gx1, gx2, gx3]
    left = lax.rem(dom + nd - 1, nd)
    right = lax.rem(dom + 1, nd)
    is_air = comp < ocean
    near_rel = [0, 1, 2, nd - 2, nd - 1]
    far_count = nd - NEAR_COUNT
    T_WHICH, T_SEL, T_EXT, T_VALID = 0, 1, 2, 2 + EXTRAS
    T_NEARP = 2 + 2 * EXTRAS
    T_EP = T_NEARP + NEAR_COUNT
    T_EVALID, T_ESRC = T_EP + 1, T_EP + 2

    def load_g(j):
        return pltpu.make_async_copy(state_hbm.at[pl.ds(0, SUB), pl.ds(j * LANES, LANES)], gx0.at[j + REACH], load_sem.at[0])

    def load_b(j):
        return pltpu.make_async_copy(state_hbm.at[pl.ds(SUB, bulk), pl.ds(j * LANES, LANES)], pb0.at[j + halo], load_sem.at[1])

    for j in range(tiles):
        load_g(j).start()
    cols_copy = pltpu.make_async_copy(cols_hbm, cols, cols_sem)
    cols_copy.start()
    for j in range(tiles):
        load_b(j).start()

    @pl.when(is_air)
    def _():
        for p in range(pairs):
            pltpu.make_async_copy(w_hbm.at[p], wbuf.at[p], w_sem).start()

    barrier = pltpu.get_barrier_semaphore()

    def greet(device):
        pl.semaphore_signal(barrier, inc=1, device_id=device, device_id_type=MESH)

    for c in range(1, nc):
        greet((lax.rem(comp + c, nc), dom))

    @pl.when(is_air)
    def _():
        def greet_plane(r, _):
            greet((comp, lax.rem(dom + r, nd)))
            return 0
        lax.fori_loop(1, nd, greet_plane, 0)

    @pl.when(jnp.logical_not(is_air))
    def _():
        greet((comp, left))
        greet((comp, right))

    def build_tables():
        src = sources[...].T
        p_i = lax.broadcasted_iota(jnp.int32, (nd, pairs), 1)
        t_i = lax.broadcasted_iota(jnp.int32, (nd, pairs), 0)
        t_c = lax.broadcasted_iota(jnp.int32, (nd, 1), 0)
        dom_f = dom
        base = (comp * nd)

        def is_far(offset):
            offset = jnp.where(offset < 0, offset + nd, offset)
            return jnp.logical_and(offset > NEAR, offset < nd - NEAR)

        mine = src == base + dom_f
        which = jnp.sum(jnp.where(mine, p_i, 0), axis=1, keepdims=True)
        hit = jnp.max(jnp.where(mine, 1, 0), axis=1, keepdims=True)
        far = jnp.where(jnp.logical_and(hit > 0, is_far(t_c - dom_f)), 1, 0)
        lanes = [(T_WHICH, which)]
        sel = jnp.zeros((nd, 1), jnp.int32)
        last = jnp.full((1, 1), -1, jnp.int32)
        for e in range(EXTRAS):
            last = jnp.min(jnp.where(jnp.logical_and(far > 0, t_c > last), t_c, nd), axis=0, keepdims=True)
            sel = jnp.where(t_c == last, e, sel)
            lanes.append((T_EXT + e, last))
            lanes.append((T_VALID + e, jnp.where(last < nd, 1, 0)))
        lanes.append((T_SEL, sel))
        crowded = jnp.sum(far, axis=0, keepdims=True) > EXTRAS

        own = jnp.sum(jnp.where(t_i == dom_f, src, 0), axis=0, keepdims=True) - base
        p_r = p_i[:1]
        for n, r in enumerate(near_rel):
            place = lax.rem(dom + r, nd)
            lanes.append((T_NEARP + n, jnp.sum(jnp.where(own == place, p_r, 0), axis=1, keepdims=True)))
        in_band = jnp.logical_and(own >= 0, own < nd)
        far_own = jnp.where(jnp.logical_and(in_band, is_far(own - dom_f)), 1, 0)
        lanes.append((T_EP, jnp.sum(far_own * p_r, axis=1, keepdims=True)))
        lanes.append((T_EVALID, jnp.max(far_own, axis=1, keepdims=True)))
        lanes.append((T_ESRC, jnp.sum(far_own * own, axis=1, keepdims=True)))
        lane = lax.broadcasted_iota(jnp.int32, (nd, LANES), 1)
        packed = jnp.zeros((nd, LANES), jnp.int32)
        for at, value in lanes:
            value = jnp.minimum(value, ((nd if at in (T_ESRC, *range(T_EXT, T_EXT + EXTRAS)) else pairs) - 1))
            packed = jnp.where(lane == at, jnp.broadcast_to(value, (nd, LANES)), packed)
        tabv[pl.ds(0, nd), :] = packed

        reach = jnp.concatenate(
            [nbr[:, j * LANES:(j + 1) * LANES] for j in range(tiles)], axis=0)
        lane = lax.broadcasted_iota(jnp.int32, reach.shape, 1)
        wide = jnp.zeros((1, 1), jnp.int32)
        stray = jnp.zeros((1, 1), jnp.int32)
        packed = jnp.zeros(reach.shape, jnp.int32)
        for h, side in enumerate((lane < LANES // 2, lane >= LANES // 2)):
            first = jnp.min(jnp.where(side, reach, 2**30), axis=1, keepdims=True)
            first = jnp.clip(first, 0, ((tiles + 2 * halo - 1) * LANES))
            final = jnp.max(jnp.where(side, reach, -1), axis=1, keepdims=True)
            wide = jnp.maximum(wide, jnp.max(final - first, axis=0, keepdims=True))
            packed = jnp.where(lane == h, jnp.broadcast_to(first, reach.shape), packed)
            tile = lax.broadcasted_iota(jnp.int32, first.shape, 0) // EDGES
            place = jnp.minimum(first >> 7, tiles + 2 * halo - 2)
            outside = jnp.logical_or(place < tile + halo - CONE, place + 1 > tile + halo + CONE)
            stray = jnp.maximum(stray, jnp.max(jnp.where(outside, 1, 0), axis=0, keepdims=True))
        tabv[pl.ds(nd, EDGES * tiles), :] = packed
        bad = jnp.logical_or(jnp.logical_or(wide >= LANES, stray > 0), crowded)
        mark = jnp.broadcast_to(jnp.where(bad, 1.0, 0.0), (SUB, LANES))
        flag[...] = mark

    build_tables()
    for j in range(tiles):
        at = pl.ds(j * LANES, LANES)
        ix[RING + j, pl.ds(0, EDGES), :] = nbr[:, at]
        cx[RING + j, pl.ds(0, EDGES), :] = coef[:, at]
        keep = jnp.logical_or(is_air, mask[:, at] == 1)
        cx[RING + j, pl.ds(EDGES, 1), :] = jnp.where(keep, 1.0, 0.0)
    to_smem = pltpu.make_async_copy(tabv, tab, tab_sem)
    to_smem.start()

    row8 = lax.broadcasted_iota(jnp.int32, (SUB, LANES), 0)

    def doubled(ref, offset):
        out = []
        for h in range(tiles):
            v = ref[h + offset]
            out.append(jnp.where(row8 < FIELDS, v, pltpu.roll(v, FIELDS, axis=0)))
        return out

    def gather_slot(table, index):
        res = []
        for q in range(0, block // LANES, 2):
            i0 = index[:, q * LANES:(q + 1) * LANES]
            i1 = index[:, (q + 1) * LANES:(q + 2) * LANES]
            i8 = jnp.where(row8 < FIELDS, jnp.broadcast_to(i0, (SUB, LANES)), jnp.broadcast_to(i1, (SUB, LANES)))
            lo = i8 & (LANES - 1)
            hi = i8 >> 7
            acc = lane_gather(table[0], lo)
            for h in range(1, tiles):
                acc = jnp.where(hi == h, lane_gather(table[h], lo), acc)
            res.append(acc)
        return res

    def split_rows(res):
        cols_ = []
        for acc in res:
            high = acc.astype(BF16).astype(F32)
            low = acc - high
            cols_.append(jnp.where(row8 < FIELDS, high, pltpu.roll(low, FIELDS, axis=0)))
            cols_.append(jnp.where(row8 < FIELDS, pltpu.roll(high, FIELDS, axis=0), low))
        return jnp.concatenate(cols_, axis=1)

    def scatter(eight, index):
        hi = jnp.broadcast_to(index >> 7, (SUB, block))
        lhs = jnp.concatenate([jnp.where(hi == h, eight, 0.0) for h in range(tiles)], axis=0).astype(BF16)
        lo = jnp.broadcast_to(index & (LANES - 1), (LANES, block))
        hot = jnp.where(lo == lax.broadcasted_iota(jnp.int32, (LANES, block), 0), 1.0, 0.0).astype(BF16)
        return lax.dot_general(lhs, hot, (((1,), (1,)), ((), ())), preferred_element_type=F32)

    def cols_of(t):
        return cols[t, pl.ds(tab[t, T_WHICH], 1), :]

    pltpu.make_async_copy(gx0.at[pl.ds(REACH, tiles)], gx0.at[pl.ds(REACH, tiles)], load_sem.at[0]).wait()
    cols_copy.wait()
    to_smem.wait()

    @pl.when(is_air)
    def _():
        table = doubled(gx0, REACH)

        def extra(e, _):
            res = gather_slot(table, cols_of(tab[0, T_EXT + e]))
            for i, acc in enumerate(res):
                compact[e, i] = acc
            return 0
        lax.fori_loop(0, EXTRAS, extra, 0)

        def fill(r, _):
            t = lax.rem(dom + r, nd)
            slots[r] = compact[tab[t, T_SEL]]
            return 0
        lax.fori_loop(NEAR + 1, nd - NEAR, fill, 0)

    @pl.when(is_air)
    def _():
        pl.semaphore_wait(barrier, nd + nc - 2)

    @pl.when(jnp.logical_not(is_air))
    def _():
        pl.semaphore_wait(barrier, nc + 1)

    def mirror(n):
        return near_rel.index((nd - near_rel[n]) % nd)

    def a_copy(r):
        return pltpu.make_async_remote_copy(
            src_ref=slots.at[r], dst_ref=gsl.at[dom], send_sem=asend.at[0], recv_sem=arecv.at[0],
            device_id=(comp, lax.rem(dom + r, nd)), device_id_type=MESH)

    def a_near(n):
        return pltpu.make_async_remote_copy(
            src_ref=nslots.at[n], dst_ref=gnear.at[mirror(n)], send_sem=asend.at[1], recv_sem=arecv.at[1],
            device_id=(comp, lax.rem(dom + near_rel[n], nd)), device_id_type=MESH)

    def halo_copies(ref, s, kind):
        to_left = pltpu.make_async_remote_copy(
            src_ref=ref.at[pl.ds(halo, halo)], dst_ref=ref.at[pl.ds(tiles + halo, halo)],
            send_sem=hsend.at[kind, s, 0], recv_sem=hrecv.at[kind, s, 0], device_id=(comp, left), device_id_type=MESH)
        to_right = pltpu.make_async_remote_copy(
            src_ref=ref.at[pl.ds(tiles, halo)], dst_ref=ref.at[pl.ds(0, halo)],
            send_sem=hsend.at[kind, s, 1], recv_sem=hrecv.at[kind, s, 1], device_id=(comp, right), device_id_type=MESH)
        return to_left, to_right

    def ring_copies(ref, width, i):
        to_left = pltpu.make_async_remote_copy(
            src_ref=ref.at[pl.ds(width, width)], dst_ref=ref.at[pl.ds(tiles + width, width)],
            send_sem=hsend.at[0, i, 0], recv_sem=hrecv.at[0, i, 0], device_id=(comp, left), device_id_type=MESH)
        to_right = pltpu.make_async_remote_copy(
            src_ref=ref.at[pl.ds(tiles, width)], dst_ref=ref.at[pl.ds(0, width)],
            send_sem=hsend.at[0, i, 1], recv_sem=hrecv.at[0, i, 1], device_id=(comp, right), device_id_type=MESH)
        return to_left, to_right

    early = [(gx0, REACH, 0), (ix, RING, 1), (cx, RING, 2)]

    def sea_copy(c):
        return pltpu.make_async_remote_copy(
            src_ref=gx0.at[pl.ds(REACH, tiles)], dst_ref=sea, send_sem=ssend, recv_sem=srecv,
            device_id=(c, dom), device_id_type=MESH)

    def sea_flag_copy(c):
        return pltpu.make_async_remote_copy(
            src_ref=flag, dst_ref=flags_in.at[ocean], send_sem=gsend.at[0], recv_sem=grecv.at[0],
            device_id=(c, dom), device_id_type=MESH)

    def plane_flag_copy(c):
        return pltpu.make_async_remote_copy(
            src_ref=pflag, dst_ref=flags_in.at[comp], send_sem=gsend.at[1], recv_sem=grecv.at[1],
            device_id=(lax.rem(comp + c, nc), dom), device_id_type=MESH)

    def arrived(ref, sem):
        pltpu.make_async_copy(ref, ref, sem).wait()

    @pl.when(jnp.logical_not(is_air))
    def _():
        for c in range(ocean):
            sea_copy(c).start()
        for c in range(ocean):
            sea_flag_copy(c).start()

    arrived(pb0.at[pl.ds(halo, tiles)], load_sem.at[1])
    for c in halo_copies(pb[0], 0, 1):
        c.start()

    @pl.when(is_air)
    def _():
        def send(r, _):
            a_copy(r).start()
            return 0
        lax.fori_loop(NEAR + 1, nd - NEAR, send, 0)
        table = doubled(gx0, REACH)
        for n, r in enumerate(near_rel):
            res = gather_slot(table, cols_of(lax.rem(dom + r, nd)))
            for i, acc in enumerate(res):
                if r == 0:
                    gnear[n, i] = acc
                else:
                    nslots[n, i] = acc
        for n in range(1, NEAR_COUNT):
            a_near(n).start()

    for ref, width, i in early:
        for c in ring_copies(ref, width, i):
            c.start()

    lane1 = lax.broadcasted_iota(jnp.int32, (1, LANES), 1)

    def tile_step(src, j, rows_):
        cols_j = pl.ds(pl.multiple_of(j * LANES, LANES), LANES)
        cur = src[j + halo]
        upd = cur
        low = jnp.broadcast_to(lane1 < LANES // 2, (rows_, LANES))
        for k in range(EDGES):
            lo = jnp.broadcast_to(nbr[pl.ds(k, 1), cols_j] & (LANES - 1), (rows_, LANES))
            got = []
            for h in range(2):
                w = tab[nd + j * EDGES + k, h]
                b = jnp.minimum(w >> 7, tiles + 2 * halo - 2)
                edge = jnp.broadcast_to(lane1 >= w - b * LANES, (rows_, LANES))
                got.append(lane_gather(jnp.where(edge, src[b], src[b + 1]), lo))
            upd = upd + coef[pl.ds(k, 1), cols_j] * (jnp.where(low, got[0], got[1]) - cur)
        keep = jnp.logical_or(is_air, mask[:, cols_j] == 1)
        return jnp.where(jnp.broadcast_to(keep, (rows_, LANES)), upd, cur)

    def put_tile(s, j, value):
        if s + 1 < STEPS:
            pb[s + 1][j + halo] = value
        else:
            outb[j] = value

    def bulk_tiles(s, js):
        new = [tile_step(pb[s], j, bulk) for j in js]
        for j, value in zip(js, new):
            put_tile(s, j, value)

    per = 4

    def bulk_inner(s, first, last):
        def body(i, _):
            start = halo + i * per
            bulk_tiles(s, [start + u for u in range(per)])
            return 0
        lax.fori_loop(first, last, body, 0)

    def bulk_edges(s):
        for c in halo_copies(pb[s], s, 1):
            c.wait()
        bulk_tiles(s, list(range(halo)) + list(range(tiles - halo, tiles)))
        if s + 1 < STEPS:
            for c in halo_copies(pb[s + 1], s + 1, 1):
                c.start()

    inner = (tiles - 2 * halo) // per

    def bulk_step(s):
        bulk_edges(s)
        bulk_inner(s, 0, inner)

    def ring_windows():
        for ref, width, i in early:
            for c in ring_copies(ref, width, i):
                c.wait()
        reach = jnp.concatenate([ix[t, pl.ds(0, EDGES), :] for t in range(tiles + 2 * RING)], axis=0)
        lane = lax.broadcasted_iota(jnp.int32, reach.shape, 1)
        packed = jnp.zeros(reach.shape, jnp.int32)
        for h, side in enumerate((lane < LANES // 2, lane >= LANES // 2)):
            first = jnp.min(jnp.where(side, reach, 2**30), axis=1, keepdims=True)
            first = jnp.clip(first, 0, (tiles + 2 * halo - 1) * LANES)
            packed = jnp.where(lane == h, jnp.broadcast_to(first, reach.shape), packed)
        tabw[...] = packed
        pltpu.make_async_copy(tabw, tab2, tab_sem).start()

    low8 = lane1 < LANES // 2
    gain8 = jnp.where(row8 < FIELDS, FORCE_GAIN, 0.0)

    def ring_tile(s, t):
        src = gx[s]
        cur = src[t + CONE]
        upd = cur
        shift = jnp.where(t < RING, -tiles, jnp.where(t >= RING + tiles, tiles, 0)) + (REACH - halo)
        for k in range(EDGES):
            lo = jnp.broadcast_to(ix[t, pl.ds(k, 1), :] & (LANES - 1), (SUB, LANES))
            got = []
            for h in range(2):
                w = tab2[t * EDGES + k, h]
                b = jnp.minimum(w >> 7, tiles + 2 * halo - 2)
                edge = jnp.broadcast_to(lane1 >= w - b * LANES, (SUB, LANES))
                at = jnp.clip(b + shift, 0, tiles + 2 * REACH - 2)
                got.append(lane_gather(jnp.where(edge, src[at], src[at + 1]), lo))
            upd = upd + cx[t, pl.ds(k, 1), :] * (jnp.where(low8, got[0], got[1]) - cur)
        upd = upd + gain8 * (force[t] - cur)
        return jnp.where(cx[t, pl.ds(EDGES, 1), :] > 0.5, upd, cur)

    def ring_step(s):
        spread = [RING, RING, RING // 2, 0][s]
        many = 8

        def body(i, _):
            first = RING - spread + i * many
            new = [ring_tile(s, first + u) for u in range(many)]
            for u in range(many):
                if s + 1 < STEPS:
                    gx[s + 1][first + u + CONE] = new[u]
                else:
                    outg[first + u - RING] = new[u]
            return 0
        lax.fori_loop(0, (tiles + 2 * spread) // many, body, 0)

    bulk_step(0)

    @pl.when(is_air)
    def _():
        arrived(sea, srecv)
        arrived(flag, grecv.at[0])
        pltpu.make_async_copy(w_hbm, wbuf, w_sem).wait()
        flag[...] = jnp.maximum(flag[...], flags_in[ocean])
        marked = jnp.concatenate([flag[pl.ds(0, FIELDS), :]] * (block // LANES), axis=1) > 0.5
        sea_table = doubled(sea, 0)

        def dense(p, slot):
            w = wbuf[p]
            wh = w.astype(BF16)
            wl = (w - wh.astype(F32)).astype(BF16)
            index = rows[pl.ds(p, 1), :]
            x = split_rows(slot).astype(BF16)
            v = split_rows(gather_slot(sea_table, index)).astype(BF16)
            dims = (((1,), (1,)), ((), ()))
            y = (lax.dot_general(x, wh, dims, preferred_element_type=F32)
                 + lax.dot_general(x, wl, dims, preferred_element_type=F32))
            z = jnp.dot(v, wh, preferred_element_type=F32) + jnp.dot(v, wl, preferred_element_type=F32)
            y = y[:FIELDS] + y[FIELDS:]
            z = jnp.where(marked, jnp.nan, z[:FIELDS] + z[FIELDS:])
            yh = y.astype(BF16).astype(F32)
            return jnp.concatenate([yh, y - yh], axis=0), z, index

        def put(ref, at, z):
            for q in range(block // LANES):
                ref[at, q // 2, pl.ds((q % 2) * FIELDS, FIELDS), :] = z[:, q * LANES:(q + 1) * LANES]

        def u_copy(r):
            return pltpu.make_async_remote_copy(
                src_ref=zslots.at[NEAR_COUNT], dst_ref=usl.at[dom], send_sem=usend.at[0], recv_sem=urecv.at[0],
                device_id=(comp, lax.rem(dom + r, nd)), device_id_type=MESH)

        def u_near(n):
            return pltpu.make_async_remote_copy(
                src_ref=zslots.at[n], dst_ref=unear.at[mirror(n)], send_sem=usend.at[1], recv_sem=urecv.at[1],
                device_id=(comp, lax.rem(dom + near_rel[n], nd)), device_id_type=MESH)

        def near_block(n):
            eight, z, index = dense(tab[0, T_NEARP + n], [gnear[n, i] for i in range(pieces)])
            if n == 0:
                put(unear, n, z)
            else:
                put(zslots, n, z)
                u_near(n).start()
            return scatter(eight, index)

        arrived(gnear.at[pl.ds(0, NEAR_COUNT - 1)], arecv.at[1])
        total = near_block(1)
        total = total + near_block(NEAR_COUNT - 1)

        arrived(gsl.at[pl.ds(0, far_count)], arecv.at[0])
        src = tab[0, T_ESRC]
        eight, z, index = dense(tab[0, T_EP], [gsl[src, i] for i in range(pieces)])
        put(zslots, NEAR_COUNT, z)

        def send(r, _):
            u_copy(r).start()
            return 0
        lax.fori_loop(NEAR + 1, nd - NEAR, send, 0)
        total = total + scatter(jnp.where(tab[0, T_EVALID] == 1, eight, 0.0), index)
        for n in range(2, NEAR_COUNT - 1):
            total = total + near_block(n)
        total = total + near_block(0)
        for h in range(tiles):
            part = total[h * SUB:(h + 1) * SUB]
            fpart[h] = part + pltpu.roll(part, FIELDS, axis=0)
        pltpu.make_async_remote_copy(
            src_ref=fpart, dst_ref=fgot.at[comp], send_sem=fsend, recv_sem=frecv,
            device_id=(ocean, dom), device_id_type=MESH).start()

    ring_windows()
    bulk_step(1)

    def mark_of(piece):
        return jnp.where(piece != piece, 1.0, 0.0)

    @pl.when(is_air)
    def _():
        arrived(unear.at[pl.ds(0, NEAR_COUNT - 1)], urecv.at[1])
        total = jnp.zeros((tiles * SUB, LANES), F32)
        plane = flag[...]
        for n, r in enumerate(near_rel):
            if r:
                plane = jnp.maximum(plane, mark_of(unear[n, 0]))
            total = total + scatter(split_rows([unear[n, i] for i in range(pieces)]), cols_of(lax.rem(dom + r, nd)))
        arrived(usl.at[pl.ds(0, far_count)], urecv.at[0])
        for r in range(NEAR + 1, nd - NEAR):
            plane = jnp.maximum(plane, mark_of(usl[lax.rem(dom + r, nd), 0]))
        pflag[...] = plane
        for e in range(EXTRAS):
            t = tab[0, T_EXT + e]
            eight = split_rows([usl[t, i] for i in range(pieces)])
            total = total + scatter(jnp.where(tab[0, T_VALID + e] == 1, eight, 0.0), cols_of(t))
        for h in range(tiles):
            part = total[h * SUB:(h + 1) * SUB]
            force[RING + h] = part + pltpu.roll(part, FIELDS, axis=0)

    @pl.when(jnp.logical_not(is_air))
    def _():
        pltpu.make_async_copy(fgot, fgot, frecv).wait()
        for h in range(tiles):
            force[RING + h] = fgot[0, h] + fgot[1, h] + fgot[2, h]

    def store_b(j):
        return pltpu.make_async_copy(outb.at[j], out.at[pl.ds(SUB, bulk), pl.ds(j * LANES, LANES)], out_sem.at[1])

    def store_g(j):
        return pltpu.make_async_copy(outg.at[j], out.at[pl.ds(0, SUB), pl.ds(j * LANES, LANES)], out_sem.at[0])

    for c in ring_copies(force, RING, 3):
        c.start()

    @pl.when(is_air)
    def _():
        for c in range(1, nc):
            plane_flag_copy(c).start()

    bulk_step(2)
    pltpu.make_async_copy(tabw, tab2, tab_sem).wait()
    for c in ring_copies(force, RING, 3):
        c.wait()
    for s in range(STEPS):
        ring_step(s)
    for j in range(tiles):
        store_g(j).start()
    bulk_step(3)

    for j in range(tiles):
        store_b(j).start()

    @pl.when(is_air)
    def _():
        arrived(flags_in.at[pl.ds(0, ocean - 1)], grecv.at[1])
        total = pflag[...]
        for c in range(ocean):
            total = jnp.maximum(total, jnp.where(comp == c, 0.0, flags_in[c]))
        flag_out[...] = total

    @pl.when(jnp.logical_not(is_air))
    def _():
        arrived(flags_in.at[pl.ds(0, ocean)], grecv.at[1])
        total = flags_in[0]
        for c in range(1, ocean):
            total = jnp.maximum(total, flags_in[c])
        flag_out[...] = total

    @pl.when(is_air)
    def _():
        arrived(slots.at[pl.ds(0, far_count)], asend.at[0])
        arrived(nslots.at[pl.ds(0, NEAR_COUNT - 1)], asend.at[1])
        arrived(usl.at[pl.ds(0, far_count)], usend.at[0])
        arrived(unear.at[pl.ds(0, NEAR_COUNT - 1)], usend.at[1])
        arrived(fpart, fsend)
        arrived(flags_in.at[pl.ds(0, ocean)], gsend.at[1])

    @pl.when(jnp.logical_not(is_air))
    def _():
        arrived(fgot, ssend)
        arrived(flags_in.at[pl.ds(0, ocean)], gsend.at[0])

    arrived(outb, out_sem.at[1])
    arrived(outg, out_sem.at[0])


def windowed(state, neighbors, edge_coef, sea_mask, pair_rows, pair_cols, remap_weight, sources):
    nd, nc = lax.axis_size("dom"), lax.axis_size("comp")
    _, levels, columns = state.shape
    tiles = columns // LANES
    padded = tiles + 2 * RIM // LANES
    ringed = tiles + 2 * RING
    pairs, block = pair_rows.shape[1:]
    pieces = block // (2 * LANES)
    bulk = levels - SUB
    vmem = pl.BlockSpec(memory_space=pltpu.VMEM)
    hbm = pl.BlockSpec(memory_space=pltpu.HBM)
    dma = pltpu.SemaphoreType.DMA
    scratch = (
        [pltpu.VMEM((padded, bulk, LANES), F32)] * STEPS
        + [pltpu.VMEM((tiles + 2 * REACH, SUB, LANES), F32)] * STEPS
        + [pltpu.VMEM((tiles, bulk, LANES), F32), pltpu.VMEM((tiles, SUB, LANES), F32)]
        + [pltpu.VMEM((ringed, SUB, LANES), jnp.int32), pltpu.VMEM((ringed, SUB, LANES), F32)]
        + [pltpu.VMEM((ringed * EDGES, LANES), jnp.int32), pltpu.SMEM((ringed * EDGES, LANES), jnp.int32)]
        + [
            pltpu.VMEM(pair_cols.shape, jnp.int32),
            pltpu.VMEM((pairs, block, block), F32),
            pltpu.VMEM((EXTRAS, pieces, SUB, LANES), F32),
            pltpu.VMEM((nd, pieces, SUB, LANES), F32),
            pltpu.VMEM((nd, pieces, SUB, LANES), F32),
            pltpu.VMEM((NEAR_COUNT + 1, pieces, SUB, LANES), F32),
            pltpu.VMEM((nd, pieces, SUB, LANES), F32),
            pltpu.VMEM((NEAR_COUNT, pieces, SUB, LANES), F32),
            pltpu.VMEM((NEAR_COUNT, pieces, SUB, LANES), F32),
            pltpu.VMEM((NEAR_COUNT, pieces, SUB, LANES), F32),
            pltpu.VMEM((tiles, SUB, LANES), F32),
            pltpu.VMEM((tiles, SUB, LANES), F32),
            pltpu.VMEM((nc - 1, tiles, SUB, LANES), F32),
            pltpu.VMEM((ringed, SUB, LANES), F32),
        ]
        + [pltpu.VMEM((nd + EDGES * tiles, LANES), jnp.int32), pltpu.SMEM((nd + EDGES * tiles, LANES), jnp.int32)]
        + [pltpu.VMEM((SUB, LANES), F32)] * 2 + [pltpu.VMEM((nc, SUB, LANES), F32), dma, dma((2,)), dma((2,))]
        + [dma((2,)), dma, dma, dma((2,))]
        + [dma((2, STEPS, 2)), dma((2, STEPS, 2))]
        + [dma((2,))] * 4 + [dma] * 4
    )
    return pl.pallas_call(
        functools.partial(interval_kernel, nd, nc, tiles, levels, block, pairs),
        out_shape=[jax.ShapeDtypeStruct((levels, columns), F32), jax.ShapeDtypeStruct((SUB, LANES), F32)],
        in_specs=[vmem] * 5 + [hbm] * 3,
        out_specs=[hbm, vmem],
        scratch_shapes=scratch,
        name="interval",
        cost_estimate=pl.CostEstimate(flops=10**9, bytes_accessed=10**8, transcendentals=0),
        compiler_params=pltpu.CompilerParams(
            collective_id=0, has_side_effects=True, vmem_limit_bytes=57 * 2**20),
    )(neighbors[0], edge_coef[0], sea_mask[None], pair_rows[0], sources, state[0], pair_cols, remap_weight[0])


def publish_kernel(parts, source, result, held, got, put):
    rows = source.shape[0] // parts

    def take(i):
        at = pl.ds(i * rows, rows)
        return pltpu.make_async_copy(source.at[at], held.at[at], got.at[i])

    def give(i):
        at = pl.ds(i * rows, rows)
        return pltpu.make_async_copy(held.at[at], result.at[at], put.at[i])
    for i in range(parts):
        take(i).start()
    for i in range(parts):
        take(i).wait()
        give(i).start()
    for i in range(parts):
        give(i).wait()


def publish(array, parts=4):
    hbm = pl.BlockSpec(memory_space=pltpu.HBM)
    return pl.pallas_call(
        functools.partial(publish_kernel, parts),
        out_shape=jax.ShapeDtypeStruct(array.shape, array.dtype),
        in_specs=[hbm],
        out_specs=hbm,
        scratch_shapes=[pltpu.VMEM(array.shape, array.dtype)] + [pltpu.SemaphoreType.DMA((parts,))] * 2,
        name="publish",
    )(array)


def local(state, neighbors, edge_coef, sea_mask, pair_source, pair_rows, pair_cols, remap_weight):
    sources = lax.optimization_barrier(pair_source.T)
    fast, flags = windowed(state, neighbors, edge_coef, sea_mask, pair_rows, pair_cols, remap_weight, sources)

    def anyway(_):
        return False, general(state, neighbors, edge_coef, sea_mask,
                              with_layout_constraint(sources, Layout((0, 1))).T, pair_rows, pair_cols, remap_weight)

    done = lax.while_loop(lambda c: c[0], anyway, (flags[0, 0] > 0, fast))
    return publish(done[1])[None]


def solution(mesh):
    placed = (
        P("comp", None, "dom"),
        P("comp", None, "dom"),
        P("comp", None, "dom"),
        P("dom"),
        P(),
        P("dom", None, None),
        P(),
        P("dom", None, None, None),
    )
    return jax.shard_map(
        local, mesh=mesh, in_specs=placed, out_specs=P("comp", None, "dom"), check_vma=False
    )
```

```python
import functools

import jax
import jax.numpy as jnp
from jax import lax
from jax.experimental import pallas as pl
from jax.experimental.layout import Layout, with_layout_constraint
from jax.experimental.pallas import tpu as pltpu
from jax.sharding import PartitionSpec as P

FIELDS = 4
RIM = 256
EDGES = 4
STEPS = 4
FORCE_GAIN = 0.5

LANES = 128
SUB = 8
NEAR = 2
NEAR_COUNT = 2 * NEAR + 1
CONE = 3
RING = 8
REACH = RING + CONE
EXTRAS = 4
MESH = pl.DeviceIdType.MESH
F32 = jnp.float32
BF16 = jnp.bfloat16


def with_halo(array, sides, width):
    for axis, dim in sides:
        devices, length = (lax.axis_size(axis), array.shape[dim])
        up = [(i, (i + 1) % devices) for i in range(devices)]
        down = [(j, i) for i, j in up]
        last = lax.slice_in_dim(array, length - width, length, axis=dim)
        leading = lax.slice_in_dim(array, 0, width, axis=dim)
        before = lax.ppermute(last, axis, up)
        after = lax.ppermute(leading, axis, down)
        array = jnp.concatenate([before, array, after], axis=dim)
    return array


def general(state, neighbors, edge_coef, sea_mask, pair_source, pair_rows, pair_cols, remap_weight):
    highest = lax.Precision.HIGHEST
    comp_count = lax.axis_size("comp")
    dom_count = lax.axis_size("dom")
    comp_id = lax.axis_index("comp")
    dom_id = lax.axis_index("dom")
    current = with_layout_constraint(state, Layout((0, 1, 2)))[0]
    fields = FIELDS
    column_count = current.shape[1]
    pair_count = pair_source.shape[1]
    block = pair_rows.shape[2]
    device_total = comp_count * dom_count
    is_ocean = comp_id == comp_count - 1
    myself = comp_id * dom_count + dom_id
    surface = current[:fields]
    pair_index = jnp.arange(pair_count, dtype=jnp.int32)
    matched = pair_source == myself
    partner = jnp.any(matched, axis=1)
    which_pair = jnp.sum(jnp.where(matched, pair_index[None, :], 0), axis=1)
    my_columns = jnp.sum(jnp.where(matched[:, :, None], pair_cols, 0), axis=1)
    handler_comp = jnp.full_like(which_pair, comp_count - 1)
    activity = jnp.where(is_ocean, 1.0, 0.0).astype(jnp.float32)
    rows_here = pair_rows[0]
    weights_here = remap_weight[0]
    own_sources = lax.dynamic_index_in_dim(pair_source, dom_id, 0, keepdims=False)
    sea_values = surface[:, rows_here]
    upward = jnp.einsum("qbj,fqb->fqj", weights_here, sea_values, precision=highest) * activity
    to_air = jnp.zeros((fields, device_total, block), jnp.float32).at[:, own_sources].add(upward)
    slot_index = handler_comp * dom_count + jnp.arange(dom_count, dtype=jnp.int32)
    air_values = surface[:, my_columns] * partner[None, :, None]
    to_sea = jnp.zeros((fields, device_total, block), jnp.float32).at[:, slot_index].add(air_values)
    got_sea, got_air = (
        lax.all_to_all(to_sea, ("comp", "dom"), split_axis=1, concat_axis=1, tiled=True),
        lax.all_to_all(to_air, ("comp", "dom"), split_axis=1, concat_axis=1, tiled=True),
    )
    incoming = got_sea[:, own_sources]
    downward = jnp.einsum("qbj,fqj->fqb", weights_here, incoming, precision=highest) * activity
    sea_force = jnp.zeros((fields, column_count), jnp.float32).at[:, rows_here].add(downward)
    arrived = got_air[:, slot_index] * partner[None, :, None]
    air_force = jnp.zeros((fields, column_count), jnp.float32).at[:, my_columns].add(arrived)
    forcing = jnp.where(is_ocean, sea_force, air_force)
    adjacency = neighbors[0]
    rates = edge_coef[0]
    evolving = jnp.logical_or(jnp.logical_not(is_ocean), sea_mask == 1)

    def advance(_, current):
        padded = with_halo(current, (("dom", 1),), RIM)
        updated = current
        for edge_number in range(EDGES):
            updated = updated + rates[edge_number] * (padded[:, adjacency[edge_number]] - current)
        updated = updated.at[:fields].add(FORCE_GAIN * (forcing - current[:fields]))
        return jnp.where(evolving[None, :], updated, current)

    return with_layout_constraint(lax.fori_loop(0, STEPS, advance, current), Layout((0, 1)))


def lane_gather(values, lanes):
    return jnp.take_along_axis(values, lanes, axis=1, mode="promise_in_bounds")


def interval_kernel(nd, nc, tiles, levels, block, pairs,
                    nbr, coef, mask, rows, sources, state_hbm, cols_hbm, w_hbm,
                    out, flag_out,
                    pb0, pb1, pb2, pb3, gx0, gx1, gx2, gx3, outb, outg, ix, cx, tabw, tab2,
                    cols, wbuf, compact, slots, gsl, zslots, usl, nslots, gnear, unear, sea, fpart, fgot, force,
                    tabv, tab, flag, pflag, flags_in, tab_sem, gsend, grecv,
                    load_sem, w_sem, cols_sem, out_sem,
                    hsend, hrecv, asend, arecv, usend, urecv, ssend, srecv, fsend, frecv):
    comp = lax.axis_index("comp")
    dom = lax.axis_index("dom")
    ocean = nc - 1
    bulk = levels - SUB
    pieces = block // (2 * LANES)
    halo = RIM // LANES
    pb = [pb0, pb1, pb2, pb3]
    gx = [gx0, gx1, gx2, gx3]
    left = lax.rem(dom + nd - 1, nd)
    right = lax.rem(dom + 1, nd)
    is_air = comp < ocean
    near_rel = [0, 1, 2, nd - 2, nd - 1]
    far_count = nd - NEAR_COUNT
    T_WHICH, T_SEL, T_EXT, T_VALID = 0, 1, 2, 2 + EXTRAS
    T_NEARP = 2 + 2 * EXTRAS
    T_EP = T_NEARP + NEAR_COUNT
    T_EVALID, T_ESRC = T_EP + 1, T_EP + 2

    def load_g(j):
        return pltpu.make_async_copy(state_hbm.at[pl.ds(0, SUB), pl.ds(j * LANES, LANES)], gx0.at[j + REACH], load_sem.at[0])

    def load_b(j):
        return pltpu.make_async_copy(state_hbm.at[pl.ds(SUB, bulk), pl.ds(j * LANES, LANES)], pb0.at[j + halo], load_sem.at[1])

    for j in range(tiles):
        load_g(j).start()
    cols_copy = pltpu.make_async_copy(cols_hbm, cols, cols_sem)
    cols_copy.start()
    for j in range(tiles):
        load_b(j).start()

    @pl.when(is_air)
    def _():
        for p in range(pairs):
            pltpu.make_async_copy(w_hbm.at[p], wbuf.at[p], w_sem).start()

    barrier = pltpu.get_barrier_semaphore()

    def greet(device):
        pl.semaphore_signal(barrier, inc=1, device_id=device, device_id_type=MESH)

    for c in range(1, nc):
        greet((lax.rem(comp + c, nc), dom))

    @pl.when(is_air)
    def _():
        def greet_plane(r, _):
            greet((comp, lax.rem(dom + r, nd)))
            return 0
        lax.fori_loop(1, nd, greet_plane, 0)

    @pl.when(jnp.logical_not(is_air))
    def _():
        greet((comp, left))
        greet((comp, right))

    def build_tables():
        src = sources[...].T
        p_i = lax.broadcasted_iota(jnp.int32, (nd, pairs), 1)
        t_i = lax.broadcasted_iota(jnp.int32, (nd, pairs), 0)
        t_c = lax.broadcasted_iota(jnp.int32, (nd, 1), 0)
        dom_f = dom
        base = (comp * nd)

        def is_far(offset):
            offset = jnp.where(offset < 0, offset + nd, offset)
            return jnp.logical_and(offset > NEAR, offset < nd - NEAR)

        mine = src == base + dom_f
        which = jnp.sum(jnp.where(mine, p_i, 0), axis=1, keepdims=True)
        hit = jnp.max(jnp.where(mine, 1, 0), axis=1, keepdims=True)
        far = jnp.where(jnp.logical_and(hit > 0, is_far(t_c - dom_f)), 1, 0)
        lanes = [(T_WHICH, which)]
        sel = jnp.zeros((nd, 1), jnp.int32)
        last = jnp.full((1, 1), -1, jnp.int32)
        for e in range(EXTRAS):
            last = jnp.min(jnp.where(jnp.logical_and(far > 0, t_c > last), t_c, nd), axis=0, keepdims=True)
            sel = jnp.where(t_c == last, e, sel)
            lanes.append((T_EXT + e, last))
            lanes.append((T_VALID + e, jnp.where(last < nd, 1, 0)))
        lanes.append((T_SEL, sel))
        crowded = jnp.sum(far, axis=0, keepdims=True) > EXTRAS

        own = jnp.sum(jnp.where(t_i == dom_f, src, 0), axis=0, keepdims=True) - base
        p_r = p_i[:1]
        for n, r in enumerate(near_rel):
            place = lax.rem(dom + r, nd)
            lanes.append((T_NEARP + n, jnp.sum(jnp.where(own == place, p_r, 0), axis=1, keepdims=True)))
        in_band = jnp.logical_and(own >= 0, own < nd)
        far_own = jnp.where(jnp.logical_and(in_band, is_far(own - dom_f)), 1, 0)
        lanes.append((T_EP, jnp.sum(far_own * p_r, axis=1, keepdims=True)))
        lanes.append((T_EVALID, jnp.max(far_own, axis=1, keepdims=True)))
        lanes.append((T_ESRC, jnp.sum(far_own * own, axis=1, keepdims=True)))
        lane = lax.broadcasted_iota(jnp.int32, (nd, LANES), 1)
        packed = jnp.zeros((nd, LANES), jnp.int32)
        for at, value in lanes:
            value = jnp.minimum(value, ((nd if at in (T_ESRC, *range(T_EXT, T_EXT + EXTRAS)) else pairs) - 1))
            packed = jnp.where(lane == at, jnp.broadcast_to(value, (nd, LANES)), packed)
        tabv[pl.ds(0, nd), :] = packed

        reach = jnp.concatenate(
            [nbr[:, j * LANES:(j + 1) * LANES] for j in range(tiles)], axis=0)
        lane = lax.broadcasted_iota(jnp.int32, reach.shape, 1)
        wide = jnp.zeros((1, 1), jnp.int32)
        stray = jnp.zeros((1, 1), jnp.int32)
        packed = jnp.zeros(reach.shape, jnp.int32)
        for h, side in enumerate((lane < LANES // 2, lane >= LANES // 2)):
            first = jnp.min(jnp.where(side, reach, 2**30), axis=1, keepdims=True)
            first = jnp.clip(first, 0, ((tiles + 2 * halo - 1) * LANES))
            final = jnp.max(jnp.where(side, reach, -1), axis=1, keepdims=True)
            wide = jnp.maximum(wide, jnp.max(final - first, axis=0, keepdims=True))
            packed = jnp.where(lane == h, jnp.broadcast_to(first, reach.shape), packed)
            tile = lax.broadcasted_iota(jnp.int32, first.shape, 0) // EDGES
            place = jnp.minimum(first >> 7, tiles + 2 * halo - 2)
            outside = jnp.logical_or(place < tile + halo - CONE, place + 1 > tile + halo + CONE)
            stray = jnp.maximum(stray, jnp.max(jnp.where(outside, 1, 0), axis=0, keepdims=True))
        tabv[pl.ds(nd, EDGES * tiles), :] = packed
        bad = jnp.logical_or(jnp.logical_or(wide >= LANES, stray > 0), crowded)
        mark = jnp.broadcast_to(jnp.where(bad, 1.0, 0.0), (SUB, LANES))
        flag[...] = mark

    build_tables()
    for j in range(tiles):
        at = pl.ds(j * LANES, LANES)
        ix[RING + j, pl.ds(0, EDGES), :] = nbr[:, at]
        cx[RING + j, pl.ds(0, EDGES), :] = coef[:, at]
        keep = jnp.logical_or(is_air, mask[:, at] == 1)
        cx[RING + j, pl.ds(EDGES, 1), :] = jnp.where(keep, 1.0, 0.0)
    to_smem = pltpu.make_async_copy(tabv, tab, tab_sem)
    to_smem.start()

    row8 = lax.broadcasted_iota(jnp.int32, (SUB, LANES), 0)

    def doubled(ref, offset):
        out = []
        for h in range(tiles):
            v = ref[h + offset]
            out.append(jnp.where(row8 < FIELDS, v, pltpu.roll(v, FIELDS, axis=0)))
        return out

    def gather_slot(table, index):
        res = []
        for q in range(0, block // LANES, 2):
            i0 = index[:, q * LANES:(q + 1) * LANES]
            i1 = index[:, (q + 1) * LANES:(q + 2) * LANES]
            i8 = jnp.where(row8 < FIELDS, jnp.broadcast_to(i0, (SUB, LANES)), jnp.broadcast_to(i1, (SUB, LANES)))
            lo = i8 & (LANES - 1)
            hi = i8 >> 7
            acc = lane_gather(table[0], lo)
            for h in range(1, tiles):
                acc = jnp.where(hi == h, lane_gather(table[h], lo), acc)
            res.append(acc)
        return res

    def split_rows(res):
        cols_ = []
        for acc in res:
            high = acc.astype(BF16).astype(F32)
            low = acc - high
            cols_.append(jnp.where(row8 < FIELDS, high, pltpu.roll(low, FIELDS, axis=0)))
            cols_.append(jnp.where(row8 < FIELDS, pltpu.roll(high, FIELDS, axis=0), low))
        return jnp.concatenate(cols_, axis=1)

    def scatter(eight, index):
        hi = jnp.broadcast_to(index >> 7, (SUB, block))
        lhs = jnp.concatenate([jnp.where(hi == h, eight, 0.0) for h in range(tiles)], axis=0).astype(BF16)
        lo = jnp.broadcast_to(index & (LANES - 1), (LANES, block))
        hot = jnp.where(lo == lax.broadcasted_iota(jnp.int32, (LANES, block), 0), 1.0, 0.0).astype(BF16)
        return lax.dot_general(lhs, hot, (((1,), (1,)), ((), ())), preferred_element_type=F32)

    def cols_of(t):
        return cols[t, pl.ds(tab[t, T_WHICH], 1), :]

    pltpu.make_async_copy(gx0.at[pl.ds(REACH, tiles)], gx0.at[pl.ds(REACH, tiles)], load_sem.at[0]).wait()
    cols_copy.wait()
    to_smem.wait()

    @pl.when(is_air)
    def _():
        table = doubled(gx0, REACH)

        def extra(e, _):
            res = gather_slot(table, cols_of(tab[0, T_EXT + e]))
            for i, acc in enumerate(res):
                compact[e, i] = acc
            return 0
        lax.fori_loop(0, EXTRAS, extra, 0)

        def fill(r, _):
            t = lax.rem(dom + r, nd)
            slots[r] = compact[tab[t, T_SEL]]
            return 0
        lax.fori_loop(NEAR + 1, nd - NEAR, fill, 0)

    @pl.when(is_air)
    def _():
        pl.semaphore_wait(barrier, nd + nc - 2)

    @pl.when(jnp.logical_not(is_air))
    def _():
        pl.semaphore_wait(barrier, nc + 1)

    def mirror(n):
        return near_rel.index((nd - near_rel[n]) % nd)

    def a_copy(r):
        return pltpu.make_async_remote_copy(
            src_ref=slots.at[r], dst_ref=gsl.at[dom], send_sem=asend.at[0], recv_sem=arecv.at[0],
            device_id=(comp, lax.rem(dom + r, nd)), device_id_type=MESH)

    def a_near(n):
        return pltpu.make_async_remote_copy(
            src_ref=nslots.at[n], dst_ref=gnear.at[mirror(n)], send_sem=asend.at[1], recv_sem=arecv.at[1],
            device_id=(comp, lax.rem(dom + near_rel[n], nd)), device_id_type=MESH)

    def halo_copies(ref, s, kind):
        to_left = pltpu.make_async_remote_copy(
            src_ref=ref.at[pl.ds(halo, halo)], dst_ref=ref.at[pl.ds(tiles + halo, halo)],
            send_sem=hsend.at[kind, s, 0], recv_sem=hrecv.at[kind, s, 0], device_id=(comp, left), device_id_type=MESH)
        to_right = pltpu.make_async_remote_copy(
            src_ref=ref.at[pl.ds(tiles, halo)], dst_ref=ref.at[pl.ds(0, halo)],
            send_sem=hsend.at[kind, s, 1], recv_sem=hrecv.at[kind, s, 1], device_id=(comp, right), device_id_type=MESH)
        return to_left, to_right

    def ring_copies(ref, width, i):
        to_left = pltpu.make_async_remote_copy(
            src_ref=ref.at[pl.ds(width, width)], dst_ref=ref.at[pl.ds(tiles + width, width)],
            send_sem=hsend.at[0, i, 0], recv_sem=hrecv.at[0, i, 0], device_id=(comp, left), device_id_type=MESH)
        to_right = pltpu.make_async_remote_copy(
            src_ref=ref.at[pl.ds(tiles, width)], dst_ref=ref.at[pl.ds(0, width)],
            send_sem=hsend.at[0, i, 1], recv_sem=hrecv.at[0, i, 1], device_id=(comp, right), device_id_type=MESH)
        return to_left, to_right

    early = [(gx0, REACH, 0), (ix, RING, 1), (cx, RING, 2)]

    def sea_copy(c):
        return pltpu.make_async_remote_copy(
            src_ref=gx0.at[pl.ds(REACH, tiles)], dst_ref=sea, send_sem=ssend, recv_sem=srecv,
            device_id=(c, dom), device_id_type=MESH)

    def sea_flag_copy(c):
        return pltpu.make_async_remote_copy(
            src_ref=flag, dst_ref=flags_in.at[ocean], send_sem=gsend.at[0], recv_sem=grecv.at[0],
            device_id=(c, dom), device_id_type=MESH)

    def plane_flag_copy(c):
        return pltpu.make_async_remote_copy(
            src_ref=pflag, dst_ref=flags_in.at[comp], send_sem=gsend.at[1], recv_sem=grecv.at[1],
            device_id=(lax.rem(comp + c, nc), dom), device_id_type=MESH)

    def arrived(ref, sem):
        pltpu.make_async_copy(ref, ref, sem).wait()

    @pl.when(jnp.logical_not(is_air))
    def _():
        for c in range(ocean):
            sea_copy(c).start()
        for c in range(ocean):
            sea_flag_copy(c).start()

    arrived(pb0.at[pl.ds(halo, tiles)], load_sem.at[1])
    for c in halo_copies(pb[0], 0, 1):
        c.start()

    @pl.when(is_air)
    def _():
        def send(r, _):
            a_copy(r).start()
            return 0
        lax.fori_loop(NEAR + 1, nd - NEAR, send, 0)
        table = doubled(gx0, REACH)
        for n, r in enumerate(near_rel):
            res = gather_slot(table, cols_of(lax.rem(dom + r, nd)))
            for i, acc in enumerate(res):
                if r == 0:
                    gnear[n, i] = acc
                else:
                    nslots[n, i] = acc
        for n in range(1, NEAR_COUNT):
            a_near(n).start()

    for ref, width, i in early:
        for c in ring_copies(ref, width, i):
            c.start()

    lane1 = lax.broadcasted_iota(jnp.int32, (1, LANES), 1)

    def tile_step(src, j, rows_):
        cols_j = pl.ds(pl.multiple_of(j * LANES, LANES), LANES)
        cur = src[j + halo]
        upd = cur
        low = jnp.broadcast_to(lane1 < LANES // 2, (rows_, LANES))
        for k in range(EDGES):
            lo = jnp.broadcast_to(nbr[pl.ds(k, 1), cols_j] & (LANES - 1), (rows_, LANES))
            got = []
            for h in range(2):
                w = tab[nd + j * EDGES + k, h]
                b = jnp.minimum(w >> 7, tiles + 2 * halo - 2)
                edge = jnp.broadcast_to(lane1 >= w - b * LANES, (rows_, LANES))
                got.append(lane_gather(jnp.where(edge, src[b], src[b + 1]), lo))
            upd = upd + coef[pl.ds(k, 1), cols_j] * (jnp.where(low, got[0], got[1]) - cur)
        keep = jnp.logical_or(is_air, mask[:, cols_j] == 1)
        return jnp.where(jnp.broadcast_to(keep, (rows_, LANES)), upd, cur)

    def put_tile(s, j, value):
        if s + 1 < STEPS:
            pb[s + 1][j + halo] = value
        else:
            outb[j] = value

    def bulk_tiles(s, js):
        new = [tile_step(pb[s], j, bulk) for j in js]
        for j, value in zip(js, new):
            put_tile(s, j, value)

    per = 4

    def bulk_inner(s, first, last):
        def body(i, _):
            start = halo + i * per
            bulk_tiles(s, [start + u for u in range(per)])
            return 0
        lax.fori_loop(first, last, body, 0)

    def bulk_edges(s):
        for c in halo_copies(pb[s], s, 1):
            c.wait()
        bulk_tiles(s, list(range(halo)) + list(range(tiles - halo, tiles)))
        if s + 1 < STEPS:
            for c in halo_copies(pb[s + 1], s + 1, 1):
                c.start()

    inner = (tiles - 2 * halo) // per

    def bulk_step(s):
        bulk_edges(s)
        bulk_inner(s, 0, inner)

    def ring_windows():
        for ref, width, i in early:
            for c in ring_copies(ref, width, i):
                c.wait()
        reach = jnp.concatenate([ix[t, pl.ds(0, EDGES), :] for t in range(tiles + 2 * RING)], axis=0)
        lane = lax.broadcasted_iota(jnp.int32, reach.shape, 1)
        packed = jnp.zeros(reach.shape, jnp.int32)
        for h, side in enumerate((lane < LANES // 2, lane >= LANES // 2)):
            first = jnp.min(jnp.where(side, reach, 2**30), axis=1, keepdims=True)
            first = jnp.clip(first, 0, (tiles + 2 * halo - 1) * LANES)
            packed = jnp.where(lane == h, jnp.broadcast_to(first, reach.shape), packed)
        tabw[...] = packed
        pltpu.make_async_copy(tabw, tab2, tab_sem).start()

    low8 = lane1 < LANES // 2
    gain8 = jnp.where(row8 < FIELDS, FORCE_GAIN, 0.0)

    def ring_tile(s, t):
        src = gx[s]
        cur = src[t + CONE]
        upd = cur
        shift = jnp.where(t < RING, -tiles, jnp.where(t >= RING + tiles, tiles, 0)) + (REACH - halo)
        for k in range(EDGES):
            lo = jnp.broadcast_to(ix[t, pl.ds(k, 1), :] & (LANES - 1), (SUB, LANES))
            got = []
            for h in range(2):
                w = tab2[t * EDGES + k, h]
                b = jnp.minimum(w >> 7, tiles + 2 * halo - 2)
                edge = jnp.broadcast_to(lane1 >= w - b * LANES, (SUB, LANES))
                at = jnp.clip(b + shift, 0, tiles + 2 * REACH - 2)
                got.append(lane_gather(jnp.where(edge, src[at], src[at + 1]), lo))
            upd = upd + cx[t, pl.ds(k, 1), :] * (jnp.where(low8, got[0], got[1]) - cur)
        upd = upd + gain8 * (force[t] - cur)
        return jnp.where(cx[t, pl.ds(EDGES, 1), :] > 0.5, upd, cur)

    def ring_step(s):
        spread = [RING, RING, RING // 2, 0][s]
        many = 8

        def body(i, _):
            first = RING - spread + i * many
            new = [ring_tile(s, first + u) for u in range(many)]
            for u in range(many):
                if s + 1 < STEPS:
                    gx[s + 1][first + u + CONE] = new[u]
                else:
                    outg[first + u - RING] = new[u]
            return 0
        lax.fori_loop(0, (tiles + 2 * spread) // many, body, 0)

    bulk_step(0)

    @pl.when(is_air)
    def _():
        arrived(sea, srecv)
        arrived(flag, grecv.at[0])
        pltpu.make_async_copy(w_hbm, wbuf, w_sem).wait()
        flag[...] = jnp.maximum(flag[...], flags_in[ocean])
        marked = jnp.concatenate([flag[pl.ds(0, FIELDS), :]] * (block // LANES), axis=1) > 0.5
        sea_table = doubled(sea, 0)

        def dense(p, slot):
            w = wbuf[p]
            wh = w.astype(BF16)
            wl = (w - wh.astype(F32)).astype(BF16)
            index = rows[pl.ds(p, 1), :]
            x = split_rows(slot).astype(BF16)
            v = split_rows(gather_slot(sea_table, index)).astype(BF16)
            dims = (((1,), (1,)), ((), ()))
            y = (lax.dot_general(x, wh, dims, preferred_element_type=F32)
                 + lax.dot_general(x, wl, dims, preferred_element_type=F32))
            z = jnp.dot(v, wh, preferred_element_type=F32) + jnp.dot(v, wl, preferred_element_type=F32)
            y = y[:FIELDS] + y[FIELDS:]
            z = jnp.where(marked, jnp.nan, z[:FIELDS] + z[FIELDS:])
            yh = y.astype(BF16).astype(F32)
            return jnp.concatenate([yh, y - yh], axis=0), z, index

        def put(ref, at, z):
            for q in range(block // LANES):
                ref[at, q // 2, pl.ds((q % 2) * FIELDS, FIELDS), :] = z[:, q * LANES:(q + 1) * LANES]

        def u_copy(r):
            return pltpu.make_async_remote_copy(
                src_ref=zslots.at[NEAR_COUNT], dst_ref=usl.at[dom], send_sem=usend.at[0], recv_sem=urecv.at[0],
                device_id=(comp, lax.rem(dom + r, nd)), device_id_type=MESH)

        def u_near(n):
            return pltpu.make_async_remote_copy(
                src_ref=zslots.at[n], dst_ref=unear.at[mirror(n)], send_sem=usend.at[1], recv_sem=urecv.at[1],
                device_id=(comp, lax.rem(dom + near_rel[n], nd)), device_id_type=MESH)

        def near_block(n):
            eight, z, index = dense(tab[0, T_NEARP + n], [gnear[n, i] for i in range(pieces)])
            if n == 0:
                put(unear, n, z)
            else:
                put(zslots, n, z)
                u_near(n).start()
            return scatter(eight, index)

        arrived(gnear.at[pl.ds(0, NEAR_COUNT - 1)], arecv.at[1])
        total = near_block(1)
        total = total + near_block(NEAR_COUNT - 1)

        arrived(gsl.at[pl.ds(0, far_count)], arecv.at[0])
        src = tab[0, T_ESRC]
        eight, z, index = dense(tab[0, T_EP], [gsl[src, i] for i in range(pieces)])
        put(zslots, NEAR_COUNT, z)

        def send(r, _):
            u_copy(r).start()
            return 0
        lax.fori_loop(NEAR + 1, nd - NEAR, send, 0)
        total = total + scatter(jnp.where(tab[0, T_EVALID] == 1, eight, 0.0), index)
        for n in range(2, NEAR_COUNT - 1):
            total = total + near_block(n)
        total = total + near_block(0)
        for h in range(tiles):
            part = total[h * SUB:(h + 1) * SUB]
            fpart[h] = part + pltpu.roll(part, FIELDS, axis=0)
        pltpu.make_async_remote_copy(
            src_ref=fpart, dst_ref=fgot.at[comp], send_sem=fsend, recv_sem=frecv,
            device_id=(ocean, dom), device_id_type=MESH).start()

    ring_windows()
    bulk_step(1)

    def mark_of(piece):
        return jnp.where(piece != piece, 1.0, 0.0)

    @pl.when(is_air)
    def _():
        arrived(unear.at[pl.ds(0, NEAR_COUNT - 1)], urecv.at[1])
        total = jnp.zeros((tiles * SUB, LANES), F32)
        plane = flag[...]
        for n, r in enumerate(near_rel):
            if r:
                plane = jnp.maximum(plane, mark_of(unear[n, 0]))
            total = total + scatter(split_rows([unear[n, i] for i in range(pieces)]), cols_of(lax.rem(dom + r, nd)))
        arrived(usl.at[pl.ds(0, far_count)], urecv.at[0])
        for r in range(NEAR + 1, nd - NEAR):
            plane = jnp.maximum(plane, mark_of(usl[lax.rem(dom + r, nd), 0]))
        pflag[...] = plane
        for e in range(EXTRAS):
            t = tab[0, T_EXT + e]
            eight = split_rows([usl[t, i] for i in range(pieces)])
            total = total + scatter(jnp.where(tab[0, T_VALID + e] == 1, eight, 0.0), cols_of(t))
        for h in range(tiles):
            part = total[h * SUB:(h + 1) * SUB]
            force[RING + h] = part + pltpu.roll(part, FIELDS, axis=0)

    @pl.when(jnp.logical_not(is_air))
    def _():
        pltpu.make_async_copy(fgot, fgot, frecv).wait()
        for h in range(tiles):
            force[RING + h] = fgot[0, h] + fgot[1, h] + fgot[2, h]

    def store_b(j):
        return pltpu.make_async_copy(outb.at[j], out.at[pl.ds(SUB, bulk), pl.ds(j * LANES, LANES)], out_sem.at[1])

    def store_g(j):
        return pltpu.make_async_copy(outg.at[j], out.at[pl.ds(0, SUB), pl.ds(j * LANES, LANES)], out_sem.at[0])

    for c in ring_copies(force, RING, 3):
        c.start()

    @pl.when(is_air)
    def _():
        for c in range(1, nc):
            plane_flag_copy(c).start()

    bulk_step(2)
    pltpu.make_async_copy(tabw, tab2, tab_sem).wait()
    for c in ring_copies(force, RING, 3):
        c.wait()
    for s in range(STEPS):
        ring_step(s)
    for j in range(tiles):
        store_g(j).start()
    bulk_step(3)

    for j in range(tiles):
        store_b(j).start()

    @pl.when(is_air)
    def _():
        arrived(flags_in.at[pl.ds(0, ocean - 1)], grecv.at[1])
        total = pflag[...]
        for c in range(ocean):
            total = jnp.maximum(total, jnp.where(comp == c, 0.0, flags_in[c]))
        flag_out[...] = total

    @pl.when(jnp.logical_not(is_air))
    def _():
        arrived(flags_in.at[pl.ds(0, ocean)], grecv.at[1])
        total = flags_in[0]
        for c in range(1, ocean):
            total = jnp.maximum(total, flags_in[c])
        flag_out[...] = total

    @pl.when(is_air)
    def _():
        arrived(slots.at[pl.ds(0, far_count)], asend.at[0])
        arrived(nslots.at[pl.ds(0, NEAR_COUNT - 1)], asend.at[1])
        arrived(usl.at[pl.ds(0, far_count)], usend.at[0])
        arrived(unear.at[pl.ds(0, NEAR_COUNT - 1)], usend.at[1])
        arrived(fpart, fsend)
        arrived(flags_in.at[pl.ds(0, ocean)], gsend.at[1])

    @pl.when(jnp.logical_not(is_air))
    def _():
        arrived(fgot, ssend)
        arrived(flags_in.at[pl.ds(0, ocean)], gsend.at[0])

    arrived(outb, out_sem.at[1])
    arrived(outg, out_sem.at[0])


def windowed(state, neighbors, edge_coef, sea_mask, pair_rows, pair_cols, remap_weight, sources):
    nd, nc = lax.axis_size("dom"), lax.axis_size("comp")
    _, levels, columns = state.shape
    tiles = columns // LANES
    padded = tiles + 2 * RIM // LANES
    ringed = tiles + 2 * RING
    pairs, block = pair_rows.shape[1:]
    pieces = block // (2 * LANES)
    bulk = levels - SUB
    vmem = pl.BlockSpec(memory_space=pltpu.VMEM)
    hbm = pl.BlockSpec(memory_space=pltpu.HBM)
    dma = pltpu.SemaphoreType.DMA
    scratch = (
        [pltpu.VMEM((padded, bulk, LANES), F32)] * STEPS
        + [pltpu.VMEM((tiles + 2 * REACH, SUB, LANES), F32)] * STEPS
        + [pltpu.VMEM((tiles, bulk, LANES), F32), pltpu.VMEM((tiles, SUB, LANES), F32)]
        + [pltpu.VMEM((ringed, SUB, LANES), jnp.int32), pltpu.VMEM((ringed, SUB, LANES), F32)]
        + [pltpu.VMEM((ringed * EDGES, LANES), jnp.int32), pltpu.SMEM((ringed * EDGES, LANES), jnp.int32)]
        + [
            pltpu.VMEM(pair_cols.shape, jnp.int32),
            pltpu.VMEM((pairs, block, block), F32),
            pltpu.VMEM((EXTRAS, pieces, SUB, LANES), F32),
            pltpu.VMEM((nd, pieces, SUB, LANES), F32),
            pltpu.VMEM((nd, pieces, SUB, LANES), F32),
            pltpu.VMEM((NEAR_COUNT + 1, pieces, SUB, LANES), F32),
            pltpu.VMEM((nd, pieces, SUB, LANES), F32),
            pltpu.VMEM((NEAR_COUNT, pieces, SUB, LANES), F32),
            pltpu.VMEM((NEAR_COUNT, pieces, SUB, LANES), F32),
            pltpu.VMEM((NEAR_COUNT, pieces, SUB, LANES), F32),
            pltpu.VMEM((tiles, SUB, LANES), F32),
            pltpu.VMEM((tiles, SUB, LANES), F32),
            pltpu.VMEM((nc - 1, tiles, SUB, LANES), F32),
            pltpu.VMEM((ringed, SUB, LANES), F32),
        ]
        + [pltpu.VMEM((nd + EDGES * tiles, LANES), jnp.int32), pltpu.SMEM((nd + EDGES * tiles, LANES), jnp.int32)]
        + [pltpu.VMEM((SUB, LANES), F32)] * 2 + [pltpu.VMEM((nc, SUB, LANES), F32), dma, dma((2,)), dma((2,))]
        + [dma((2,)), dma, dma, dma((2,))]
        + [dma((2, STEPS, 2)), dma((2, STEPS, 2))]
        + [dma((2,))] * 4 + [dma] * 4
    )
    return pl.pallas_call(
        functools.partial(interval_kernel, nd, nc, tiles, levels, block, pairs),
        out_shape=[jax.ShapeDtypeStruct((levels, columns), F32), jax.ShapeDtypeStruct((SUB, LANES), F32)],
        in_specs=[vmem] * 5 + [hbm] * 3,
        out_specs=[hbm, vmem],
        scratch_shapes=scratch,
        name="interval",
        cost_estimate=pl.CostEstimate(flops=10**9, bytes_accessed=10**8, transcendentals=0),
        compiler_params=pltpu.CompilerParams(
            collective_id=0, has_side_effects=True, vmem_limit_bytes=57 * 2**20),
    )(neighbors[0], edge_coef[0], sea_mask[None], pair_rows[0], sources, state[0], pair_cols, remap_weight[0])


def publish_kernel(parts, source, result, held, got, put):
    rows = source.shape[0] // parts

    def take(i):
        at = pl.ds(i * rows, rows)
        return pltpu.make_async_copy(source.at[at], held.at[at], got.at[i])

    def give(i):
        at = pl.ds(i * rows, rows)
        return pltpu.make_async_copy(held.at[at], result.at[at], put.at[i])
    for i in range(parts):
        take(i).start()
    for i in range(parts):
        take(i).wait()
        give(i).start()
    for i in range(parts):
        give(i).wait()


def publish(array, parts=4):
    hbm = pl.BlockSpec(memory_space=pltpu.HBM)
    return pl.pallas_call(
        functools.partial(publish_kernel, parts),
        out_shape=jax.ShapeDtypeStruct(array.shape, array.dtype),
        in_specs=[hbm],
        out_specs=hbm,
        scratch_shapes=[pltpu.VMEM(array.shape, array.dtype)] + [pltpu.SemaphoreType.DMA((parts,))] * 2,
        name="publish",
    )(array)


def local(state, neighbors, edge_coef, sea_mask, pair_source, pair_rows, pair_cols, remap_weight):
    sources = lax.optimization_barrier(pair_source.T)
    fast, flags = windowed(state, neighbors, edge_coef, sea_mask, pair_rows, pair_cols, remap_weight, sources)

    def anyway(_):
        return jnp.zeros_like(flags), general(state, neighbors, edge_coef, sea_mask,
                              with_layout_constraint(sources, Layout((0, 1))).T, pair_rows, pair_cols, remap_weight)

    done = lax.while_loop(lambda c: c[0][0, 0] > 0, anyway, (flags, fast))
    return publish(done[1])[None]


def solution(mesh):
    placed = (
        P("comp", None, "dom"),
        P("comp", None, "dom"),
        P("comp", None, "dom"),
        P("dom"),
        P(),
        P("dom", None, None),
        P(),
        P("dom", None, None, None),
    )
    return jax.shard_map(
        local, mesh=mesh, in_specs=placed, out_specs=P("comp", None, "dom"), check_vma=False
    )
```
